32 devices in a mesh: groups: 2 (over y), tile: 16 (over z, x, core).
Axes of the slice: x: 2, y: 2, z: 4, core: 2. Of those that a mesh axis runs over, the one named last changes fastest.
Arguments:
- fine: bfloat16 [64, 256, 256], P(('groups', 'tile')), parts along dimension 0, may hold values from -12 to 12
- conv_weight: bfloat16 [3, 3, 256, 256], replicated, may hold values from -0.125 to 0.125
- qk_weight: bfloat16 [2, 256, 128], replicated, may hold values from -2 to 2
- v_weight: bfloat16 [256, 128], replicated, may hold values from -0.375 to 0.375
- o_weight: bfloat16 [128, 256], replicated, may hold values from -0.5 to 0.5
- upstream: bfloat16 [4096, 256], P(('groups', 'tile')), parts along dimension 0, may hold values from -6 to 6
Outputs:
- block_out: bfloat16 [4096, 256], P(('groups', 'tile')), parts along dimension 0
- grad_conv: float32 [6, 3, 256, 256], P('groups'), parts along dimension 0
- grad_fine: bfloat16 [64, 256, 256], P(('groups', 'tile')), parts along dimension 0
The draws below stay inside these ranges and needn't reach their ends.
There are 2 independent parts, one for each index of `groups`. The reference program is written for one: setup_inputs(seed, part) draws one part's arguments, and reference() takes and returns one part's arrays. A program takes and returns all parts, laid end to end along the dimension named above; an argument that names none is the same for every part. Nothing has to cross between parts.
All inputs are finite; a program needn't handle non-finite values.
Results may differ from the reference program's by a relative error of at most 0.035.
The reference program's roundings to bfloat16 on the way count: a program that leaves them out, or rounds other values in their place, can miss the bound.
Values may be sent and summed in bfloat16 or wider, within the bound.
A program may use at most 64 MiB of HBM per device.

```python
import math
import jax
import jax.numpy as jnp
from jax import lax

C = 256
HEADS = 2
HDIM = 64
WC = 128
HD = 128
ROWS = 16
FROWS = 32
FCOLS = 256
TOKENS = 2048


def draw_fine(key, part):
    base = jnp.clip(jax.random.normal(key, (FROWS, FCOLS, C), jnp.float32), -4.0, 4.0)
    return base.astype(jnp.bfloat16)


def draw_qk_weight(key, part):
    first = jax.random.normal(jax.random.fold_in(key, 1), (C, HD), jnp.float32)
    second = jax.random.normal(jax.random.fold_in(key, 2), (C, HD), jnp.float32)
    stacked = jnp.clip(jnp.stack([first, second]), -5.0, 5.0) * (1.7 / math.sqrt(C))
    return stacked.astype(jnp.bfloat16)


def level_of(own_key, dims, shards, smallest, largest):
    level = 1.0
    for axis_at, parts in shards:
        heights = jax.random.uniform(jax.random.fold_in(jax.random.fold_in(own_key, 6), axis_at), (parts,), jnp.float32, smallest / len(shards), largest / len(shards))
        level = level * jnp.repeat(jnp.exp(heights), dims[axis_at] // parts).reshape((-1,) + (1,) * (len(dims) - 1 - axis_at))
    return level


def noise(key, extent, width, reach, cuts=(), kind=jnp.bfloat16):
    entries = jax.random.normal(key, extent, jnp.float32) * width
    if len(cuts) > 0:
        entries = level_of(key, extent, cuts, -0.22, 0.18) * entries
    return jnp.clip(entries, min=-reach, max=reach).astype(kind)


def setup_inputs(seed: int = 0, part: int = 0) -> dict:
    streams_of = jax.random.split(jax.random.key(seed), 7)
    part_keys = jax.random.split(jax.random.fold_in(streams_of[6], part), 7)
    return {
        "fine": draw_fine(jax.random.fold_in(jax.random.fold_in(streams_of[6], part), 71), part),
        "conv_weight": noise(streams_of[1], (3, 3, C, C), (9 * C) ** -0.5, 0.125),
        "qk_weight": draw_qk_weight(jax.random.fold_in(streams_of[6], 71), part),
        "v_weight": noise(streams_of[3], (C, HD), C ** -0.5, 0.375),
        "o_weight": noise(streams_of[4], (HD, C), HD ** -0.5, 0.5),
        "upstream": noise(part_keys[5], (TOKENS, C), 1.0, 6.0, ((0, 16),)),
    }


def conv_taps(fine):
    padded = jnp.pad(fine, ((1, 0), (1, 0), (0, 0)))
    taps = []
    for a in range(3):
        for b in range(3):
            taps.append(padded[a:a + 2 * ROWS:2, b:b + 2 * WC:2].reshape(ROWS * WC, C))
    return taps

def split_heads(mat):
    return mat.reshape(mat.shape[0], HEADS, HDIM).transpose(1, 0, 2).astype(jnp.float32)

def join_heads(mat):
    return mat.transpose(1, 0, 2).reshape(mat.shape[1], HD)

def reference(fine, conv_weight, qk_weight, v_weight, o_weight, upstream):
    taps = conv_taps(fine)
    total = jnp.zeros((TOKENS, C), jnp.float32)
    for a in range(3):
        for b in range(3):
            total = total + jnp.dot(taps[3 * a + b], conv_weight[a, b], preferred_element_type=jnp.float32)
    hidden = total.astype(jnp.bfloat16)
    query = jnp.dot(hidden, qk_weight[0], preferred_element_type=jnp.float32).astype(jnp.bfloat16)
    keys = jnp.dot(hidden, qk_weight[1], preferred_element_type=jnp.float32).astype(jnp.bfloat16)
    values = jnp.dot(hidden, v_weight, preferred_element_type=jnp.float32).astype(jnp.bfloat16)
    q_heads = split_heads(query)
    k_heads = split_heads(keys)
    v_heads = split_heads(values)
    scale = HDIM ** (-0.5)
    block = math.gcd(TOKENS, 1024)
    count = TOKENS // block

    def forward_block(index):
        q_part = lax.dynamic_slice_in_dim(q_heads, index * block, block, 1)
        scores = jnp.einsum('hqd,hkd->hqk', q_part, k_heads) * scale
        top = lax.optimization_barrier(jnp.max(scores, axis=2, keepdims=True))
        lse = top + jnp.log(lax.optimization_barrier(jnp.sum(jnp.exp(scores - top), axis=2, keepdims=True)))
        prob = jnp.exp(scores - lse).astype(jnp.bfloat16).astype(jnp.float32)
        return (jnp.einsum('hqk,hkd->hqd', prob, v_heads), lse[:, :, 0])
    out_blocks, lse_blocks = lax.map(forward_block, jnp.arange(count, dtype=jnp.int32))
    attended = join_heads(out_blocks.transpose(1, 0, 2, 3).reshape(HEADS, TOKENS, HDIM)).astype(jnp.bfloat16)
    lse = lse_blocks.transpose(1, 0, 2).reshape(HEADS, TOKENS)
    block_out = (hidden.astype(jnp.float32) + jnp.dot(attended, o_weight, preferred_element_type=jnp.float32)).astype(jnp.bfloat16)
    dattended = jnp.dot(upstream, o_weight.T, preferred_element_type=jnp.float32).astype(jnp.bfloat16)
    d_heads = split_heads(dattended)
    a_heads = split_heads(attended)
    delta = lax.optimization_barrier(jnp.sum(d_heads * a_heads, axis=2))

    def query_block(index):
        q_part = lax.dynamic_slice_in_dim(q_heads, index * block, block, 1)
        d_part = lax.dynamic_slice_in_dim(d_heads, index * block, block, 1)
        l_part = lax.dynamic_slice_in_dim(lse, index * block, block, 1)
        e_part = lax.dynamic_slice_in_dim(delta, index * block, block, 1)
        scores = jnp.einsum('hqd,hkd->hqk', q_part, k_heads) * scale
        prob = jnp.exp(scores - l_part[:, :, None])
        dprob = jnp.einsum('hqd,hkd->hqk', d_part, v_heads)
        dscore = (prob * (dprob - e_part[:, :, None]) * scale).astype(jnp.bfloat16).astype(jnp.float32)
        return jnp.einsum('hqk,hkd->hqd', dscore, k_heads)

    def key_block(index):
        k_part = lax.dynamic_slice_in_dim(k_heads, index * block, block, 1)
        v_part = lax.dynamic_slice_in_dim(v_heads, index * block, block, 1)
        scores = jnp.einsum('hqd,hkd->hqk', q_heads, k_part) * scale
        prob = jnp.exp(scores - lse[:, :, None])
        prob_low = prob.astype(jnp.bfloat16).astype(jnp.float32)
        dvals = jnp.einsum('hqk,hqd->hkd', prob_low, d_heads)
        dprob = jnp.einsum('hqd,hkd->hqk', d_heads, v_part)
        dscore = (prob * (dprob - delta[:, :, None]) * scale).astype(jnp.bfloat16).astype(jnp.float32)
        dkeys = jnp.einsum('hqk,hqd->hkd', dscore, q_heads)
        return (dkeys, dvals)
    dq_blocks = lax.map(query_block, jnp.arange(count, dtype=jnp.int32))
    dk_blocks, dv_blocks = lax.map(key_block, jnp.arange(count, dtype=jnp.int32))

    def gather_blocks(blocks):
        return join_heads(blocks.transpose(1, 0, 2, 3).reshape(HEADS, TOKENS, HDIM)).astype(jnp.bfloat16)
    dquery = gather_blocks(dq_blocks)
    dkeys = gather_blocks(dk_blocks)
    dvalues = gather_blocks(dv_blocks)
    dhidden = upstream.astype(jnp.float32)
    dhidden = dhidden + jnp.dot(dquery, qk_weight[0].T, preferred_element_type=jnp.float32)
    dhidden = dhidden + jnp.dot(dkeys, qk_weight[1].T, preferred_element_type=jnp.float32)
    dhidden = dhidden + jnp.dot(dvalues, v_weight.T, preferred_element_type=jnp.float32)
    dhidden = dhidden.astype(jnp.bfloat16)
    kernel_rows = []
    dpadded = jnp.zeros((2 * ROWS + 1, 2 * WC + 1, C), jnp.float32)
    for a in range(3):
        row_list = []
        for b in range(3):
            row_list.append(jnp.dot(taps[3 * a + b].T, dhidden, preferred_element_type=jnp.float32))
            back = jnp.dot(dhidden, conv_weight[a, b].T, preferred_element_type=jnp.float32)
            dpadded = dpadded.at[a:a + 2 * ROWS:2, b:b + 2 * WC:2].add(back.reshape(ROWS, WC, C))
        kernel_rows.append(jnp.stack(row_list))
    grad_conv = jnp.stack(kernel_rows) * (1.0 / math.sqrt(TOKENS))
    grad_fine = dpadded[1:, 1:].astype(jnp.bfloat16)
    return (block_out, grad_conv, grad_fine)
```

```python
import functools
import math

import jax
import jax.numpy as jnp
from jax import lax
from jax.experimental import pallas as pl
from jax.experimental.pallas import tpu as pltpu
from jax.sharding import PartitionSpec as P

HEADS = 2
HDIM = 64
HD = 128


def shifted(x, axis, by):
    peers = lax.axis_size(axis)
    pairs = [(i, i + by) for i in range(peers) if 0 <= i + by < peers]
    return lax.ppermute(x, axis, pairs)


def head_view(mat):
    return mat.reshape(mat.shape[0], HEADS, HDIM)


def score_block(queries, keys):
    product = jnp.einsum(
        "qhd,khd->hqk", head_view(queries), head_view(keys), preferred_element_type=jnp.float32
    )
    return product * HDIM ** (-0.5)


def dot_back(left, right):
    return lax.dot_general(
        left, right, (((1,), (1,)), ((), ())), preferred_element_type=jnp.float32
    )


def dot_over(left, right):
    return lax.dot_general(
        left, right, (((0,), (0,)), ((), ())), preferred_element_type=jnp.float32
    )


def body(fine, conv_weight, qk_weight, v_weight, o_weight, upstream):
    rows = fine.shape[0] // 2
    cols = fine.shape[1] // 2
    chans = fine.shape[2]
    local = rows * cols
    scale = HDIM ** (-0.5)
    above = shifted(fine[-1:], "tile", 1)
    padded = jnp.pad(jnp.concatenate([above, fine], axis=0), ((0, 0), (1, 0), (0, 0)))
    taps = []
    total = jnp.zeros((local, chans), jnp.float32)
    for a in range(3):
        for b in range(3):
            tap = padded[a : a + 2 * rows : 2, b : b + 2 * cols : 2].reshape(local, chans)
            taps.append(tap)
            total = total + jnp.dot(tap, conv_weight[a, b], preferred_element_type=jnp.float32)
    hidden = total.astype(jnp.bfloat16)
    query = jnp.dot(hidden, qk_weight[0], preferred_element_type=jnp.float32).astype(jnp.bfloat16)
    key_loc = jnp.dot(hidden, qk_weight[1], preferred_element_type=jnp.float32).astype(jnp.bfloat16)
    value_loc = jnp.dot(hidden, v_weight, preferred_element_type=jnp.float32).astype(jnp.bfloat16)
    keys_all, values_all = (
        lax.all_gather(key_loc, "tile", axis=0, tiled=True),
        lax.all_gather(value_loc, "tile", axis=0, tiled=True),
    )
    everyone = keys_all.shape[0]
    block = math.gcd(everyone, 2048)
    steps_total = everyone // block

    def stats_step(index, carry):
        top, summed = carry
        scores = score_block(query, lax.dynamic_slice_in_dim(keys_all, index * block, block, 0))
        new_top = jnp.maximum(top, jnp.max(scores, axis=2))
        summed = summed * jnp.exp(top - new_top) + jnp.sum(
            jnp.exp(scores - new_top[:, :, None]), axis=2
        )
        return (new_top, summed)

    start_top = jnp.full((HEADS, local), -jnp.inf, jnp.float32)
    top, summed = lax.fori_loop(
        0, steps_total, stats_step, (start_top, jnp.zeros((HEADS, local), jnp.float32))
    )
    lse = top + jnp.log(summed)

    def value_step(index, acc):
        scores = score_block(query, lax.dynamic_slice_in_dim(keys_all, index * block, block, 0))
        weights = jnp.exp(scores - lse[:, :, None]).astype(jnp.bfloat16)
        v_part = head_view(lax.dynamic_slice_in_dim(values_all, index * block, block, 0))
        return acc + jnp.einsum("hqk,khd->qhd", weights, v_part, preferred_element_type=jnp.float32)

    mixed = lax.fori_loop(0, steps_total, value_step, jnp.zeros((local, HEADS, HDIM), jnp.float32))
    attended = mixed.reshape(local, HD).astype(jnp.bfloat16)
    block_out = (
        hidden.astype(jnp.float32) + jnp.dot(attended, o_weight, preferred_element_type=jnp.float32)
    ).astype(jnp.bfloat16)
    dattended = dot_back(upstream, o_weight).astype(jnp.bfloat16)
    product = dattended.astype(jnp.float32) * attended.astype(jnp.float32)
    delta = jnp.sum(product.reshape(local, HEADS, HDIM), axis=2).T

    def query_step(index, acc):
        k_part = lax.dynamic_slice_in_dim(keys_all, index * block, block, 0)
        v_part = lax.dynamic_slice_in_dim(values_all, index * block, block, 0)
        prob = jnp.exp(score_block(query, k_part) - lse[:, :, None])
        dprob = jnp.einsum(
            "qhd,khd->hqk",
            head_view(dattended),
            head_view(v_part),
            preferred_element_type=jnp.float32,
        )
        dscore = (prob * (dprob - delta[:, :, None]) * scale).astype(jnp.bfloat16)
        return acc + jnp.einsum(
            "hqk,khd->qhd", dscore, head_view(k_part), preferred_element_type=jnp.float32
        )

    dq_acc = lax.fori_loop(0, steps_total, query_step, jnp.zeros((local, HEADS, HDIM), jnp.float32))
    dquery = dq_acc.reshape(local, HD).astype(jnp.bfloat16)
    lse_all, delta_all = (
        lax.all_gather(lse.T, "tile", axis=0, tiled=True),
        lax.all_gather(delta.T, "tile", axis=0, tiled=True),
    )
    empty = jnp.zeros((local, HEADS, HDIM), jnp.float32)
    q_in = lax.all_gather(query, "tile", axis=0, tiled=True)
    d_in = lax.all_gather(dattended, "tile", axis=0, tiled=True)
    incoming = q_in.shape[0]
    sub = math.gcd(incoming, 2048)

    def inner(index, acc):
        dk_acc, dv_acc = acc
        at = index * sub
        q_part = lax.dynamic_slice_in_dim(q_in, at, sub, 0)
        d_part = lax.dynamic_slice_in_dim(d_in, at, sub, 0)
        l_part = lax.dynamic_slice_in_dim(lse_all, at, sub, 0).T
        e_part = lax.dynamic_slice_in_dim(delta_all, at, sub, 0).T
        prob = jnp.exp(score_block(q_part, key_loc) - l_part[:, :, None])
        dv_acc = dv_acc + jnp.einsum(
            "hqk,qhd->khd",
            prob.astype(jnp.bfloat16),
            head_view(d_part),
            preferred_element_type=jnp.float32,
        )
        dprob = jnp.einsum(
            "qhd,khd->hqk",
            head_view(d_part),
            head_view(value_loc),
            preferred_element_type=jnp.float32,
        )
        dscore = (prob * (dprob - e_part[:, :, None]) * scale).astype(jnp.bfloat16)
        dk_acc = dk_acc + jnp.einsum(
            "hqk,qhd->khd", dscore, head_view(q_part), preferred_element_type=jnp.float32
        )
        return (dk_acc, dv_acc)

    dk_acc, dv_acc = lax.fori_loop(0, incoming // sub, inner, (empty, empty))
    dkeys = dk_acc.reshape(local, HD).astype(jnp.bfloat16)
    dvalues = dv_acc.reshape(local, HD).astype(jnp.bfloat16)
    dhidden = upstream.astype(jnp.float32)
    dhidden = dhidden + dot_back(dquery, qk_weight[0])
    dhidden = dhidden + dot_back(dkeys, qk_weight[1])
    dhidden = dhidden + dot_back(dvalues, v_weight)
    dhidden = dhidden.astype(jnp.bfloat16)
    kernel_rows = []
    dpadded = jnp.zeros((2 * rows + 1, 2 * cols + 1, chans), jnp.float32)
    for a in range(3):
        row_list = []
        for b in range(3):
            row_list.append(dot_over(taps[3 * a + b], dhidden))
            back = dot_back(dhidden, conv_weight[a, b])
            dpadded = dpadded.at[a : a + 2 * rows : 2, b : b + 2 * cols : 2].add(
                back.reshape(rows, cols, chans)
            )
        kernel_rows.append(jnp.stack(row_list))
    kernel_local = jnp.stack(kernel_rows)
    grad_conv = lax.psum(kernel_local, "tile") * (1.0 / math.sqrt(everyone))
    below = shifted(dpadded[0:1, 1:].astype(jnp.bfloat16), "tile", -1).astype(jnp.float32)
    grad_fine = dpadded[1:, 1:]
    grad_fine = grad_fine.at[-1:].add(below)
    return (block_out, grad_conv, grad_fine.astype(jnp.bfloat16))


NT = (((1,), (1,)), ((), ()))
NN = (((1,), (0,)), ((), ()))


def mm(left, right, dims=NN):
    return lax.dot_general(left, right, dims, preferred_element_type=jnp.float32)


def two_heads(mat):
    lane = lax.broadcasted_iota(jnp.int32, mat.shape, 1)
    zero = jnp.zeros_like(mat)
    return jnp.concatenate(
        [jnp.where(lane < HDIM, mat, zero), jnp.where(lane < HDIM, zero, mat)], axis=0
    )


def pick_heads(mat):
    half = mat.shape[0] // 2
    lane = lax.broadcasted_iota(jnp.int32, (half, mat.shape[1]), 1)
    return jnp.where(lane < HDIM, mat[:half], mat[half:])


class Gather:
    def __init__(self, view, place, send, recv, slot):
        self.view, self.place, self.send, self.recv, self.slot = view, place, send, recv, slot
        self.copies = []

    def copy(self, index, block, target):
        return pltpu.make_async_remote_copy(
            src_ref=self.view(block),
            dst_ref=self.view(block),
            send_sem=self.send.at[self.slot, index],
            recv_sem=self.recv.at[self.slot, index],
            device_id={"tile": target},
            device_id_type=pl.DeviceIdType.MESH,
        )

    def go(self, index, block, target):
        made = self.copy(index, block, target)
        made.start()
        self.copies.append(made)

    def landed(self, index, block):
        self.copy(index, block, self.place(0, 0, 1)).wait_recv()

    def own(self):
        block = self.place(0, 0, 0)
        for k in (1, 2, 3):
            self.go(k, block, self.place(k, 0, 0))
        self.go(4, block, self.place(0, 1, 0))
        self.go(8, block, self.place(0, 0, 1))

    def across(self, *which):
        for k in which or (1, 2, 3):
            block = self.place(k, 0, 0)
            self.landed(k, block)
            self.go(4 + k, block, self.place(0, 1, 0))
            self.go(8 + k, block, self.place(0, 0, 1))

    def over(self, *which):
        for k in which or (0, 1, 2, 3):
            block = self.place(k, 1, 0)
            self.landed(4 + k, block)
            self.go(12 + k, block, self.place(0, 0, 1))

    def finish_column(self, *which):
        for k in which or (0, 1, 2, 3):
            self.landed(8 + k, self.place(k, 0, 1))

    def finish_other(self, *which):
        for k in which or (0, 1, 2, 3):
            self.landed(12 + k, self.place(k, 1, 1))

    def drain(self):
        for made in self.copies:
            made.wait_send()


def fused_kernel(
    peers,
    fine_hbm,
    conv_hbm,
    qk_hbm,
    vw_hbm,
    ow_hbm,
    up_hbm,
    block_res,
    grad_conv_res,
    grad_fine_res,
    fine,
    conv,
    qk,
    vw,
    ow,
    up,
    block_out,
    grad_conv,
    grad_fine,
    in_sem,
    out_sem,
    above,
    hid_all,
    kv_all,
    q_all,
    d_all,
    dh_all,
    mid_t,
    low_t,
    stats,
    exp_buf,
    st_buf,
    dpt_buf,
    kv_w,
    acc,
    send,
    recv,
    stat_send,
    stat_recv,
    halo_send,
    halo_recv,
):
    me = lax.axis_index("tile")
    n = up.shape[0]
    chans = up.shape[1]
    full = n * peers
    pair = 2 * n
    lower = lax.rem(me + 1, peers)
    core = lax.rem(me, 2)
    col = lax.rem(lax.div(me, 2), 2)
    level = lax.div(me, 4)
    levels = (level, level + 1 - 2 * lax.rem(level, 2), lax.rem(level + 2, 4), 3 - level)

    def place(k, flip_x, flip_core):
        x = 1 - col if flip_x else col
        c = 1 - core if flip_core else core
        return levels[k] * 4 + x * 2 + c

    def chip(k, flip_x):
        return levels[k] * 4 + (1 - col if flip_x else col) * 2

    barrier = pltpu.get_barrier_semaphore()
    for step in range(1, peers):
        pl.semaphore_signal(
            barrier,
            inc=1,
            device_id={"tile": lax.rem(me + step, peers)},
            device_id_type=pl.DeviceIdType.MESH,
        )
    moves = (
        (up_hbm, up), (ow_hbm, ow), (fine_hbm, fine), (conv_hbm, conv), (qk_hbm, qk), (vw_hbm, vw)
    )
    loads = [pltpu.make_async_copy(a, b, in_sem.at[i]) for i, (a, b) in enumerate(moves)]
    for load in loads:
        load.start()
    stores = []

    def store(source, target):
        made = pltpu.make_async_copy(source, target, out_sem.at[len(stores)])
        made.start()
        stores.append(made)

    def rows(ref):
        return lambda t: ref.at[pl.ds(pl.multiple_of(t * n, n), n), :]

    def cols(ref, part, shift):
        lines = pl.ds(part * chans, chans)
        return lambda t: ref.at[t + shift, lines, :]

    def both(t):
        return pl.ds(pl.multiple_of(t * n, pair), pair)

    mine = pl.ds(pl.multiple_of(me * n, n), n)
    halo = pltpu.make_async_remote_copy(
        src_ref=fine_hbm.at[1],
        dst_ref=above,
        send_sem=halo_send,
        recv_sem=halo_recv,
        device_id={"tile": lower},
        device_id_type=pl.DeviceIdType.MESH,
    )
    pl.semaphore_wait(barrier, peers - 1)
    halo.start()
    views = (cols(mid_t, 0, 0), cols(mid_t, 1, 0), cols(low_t, 1, 1), cols(low_t, 0, 1))
    parts = [Gather(view, place, send, recv, i) for i, view in enumerate(views)]
    hid_gather = Gather(rows(hid_all), place, send, recv, 4)
    d_gather = Gather(rows(d_all), place, send, recv, 5)
    dh_gather = Gather(rows(dh_all), place, send, recv, 6)

    loads[0].wait()
    loads[1].wait()
    dattended = mm(up[...], ow[...], NT).astype(jnp.bfloat16)
    d_all[mine, :] = dattended
    d_gather.own()

    line = lax.broadcasted_iota(jnp.int32, (2 * n, 2 * n), 0)
    cell = lax.broadcasted_iota(jnp.int32, (2 * n, 2 * n), 1)
    wanted = jnp.where(line < n, 2 * line, 2 * (line - n) + 1)
    order = jnp.where(cell == wanted, 1.0, 0.0).astype(jnp.bfloat16)

    def apart(row):
        sorted_row = mm(order, row).astype(jnp.bfloat16)
        return sorted_row[:n], sorted_row[n:]

    loads[2].wait()
    mid_even, mid_odd = apart(fine[0])
    low_even, low_odd = apart(fine[1])
    mid_t[me, :chans, :] = mid_even.T
    parts[0].own()
    for load in loads[3:]:
        load.wait()
    mid_t[me, chans:, :] = mid_odd.T
    low_t[me + 1, :chans, :] = low_even.T
    low_t[me + 1, chans:, :] = low_odd.T
    low_t[0] = jnp.zeros_like(low_t[0])
    kv_w[:, :HD] = qk[1]
    kv_w[:, HD:] = vw[...]

    def conv_row(a, even, odd):
        return mm(even, conv[a, 1]) + mm(odd, conv[a, 2]), mm(odd, conv[a, 0])

    mid, mid_late = conv_row(1, mid_even, mid_odd)
    low, low_late = conv_row(2, low_even, low_odd)
    halo.wait_recv()
    top_even, top_odd = apart(jnp.where(me == 0, jnp.zeros_like(above[...]), above[...]))
    top, top_late = conv_row(0, top_even, top_odd)
    late = top_late + mid_late + low_late
    row_at = lax.broadcasted_iota(jnp.int32, (n, chans), 0)
    late = jnp.where(row_at == 0, 0.0, pltpu.roll(late, 1, 0))
    hidden = (top + mid + low + late).astype(jnp.bfloat16)
    hid_all[mine, :] = hidden
    hid_gather.own()

    def scaled_query(mat):
        full_query = mm(mat, qk[0]).astype(jnp.bfloat16)
        return (full_query.astype(jnp.float32) * HDIM**-0.5).astype(jnp.bfloat16)

    key_value = mm(hidden, kv_w[...]).astype(jnp.bfloat16)
    q2 = two_heads(scaled_query(hidden))
    d2 = two_heads(dattended)

    def project(k, flip_x):
        span = both(chip(k, flip_x))
        kv_all[span, :] = mm(hid_all[span, :], kv_w[...]).astype(jnp.bfloat16)

    def attend(flip_x):
        tops = []
        for k in range(4):
            j = 4 * flip_x + k
            scores = mm(q2, kv_all[both(chip(k, flip_x)), :HD], NT)
            st_buf[:, j * pair : (j + 1) * pair] = scores
            tops.append(scores)
        block = st_buf[:, 4 * flip_x * pair : 4 * (flip_x + 1) * pair]
        high = jnp.max(block, axis=1, keepdims=True)
        expd = jnp.exp(block - high)
        exp_buf[:, 4 * flip_x * pair : 4 * (flip_x + 1) * pair] = expd
        total = jnp.sum(expd, axis=1, keepdims=True)
        mixed = jnp.zeros((pair, HD), jnp.float32)
        for k in range(4):
            weights = expd[:, k * pair : (k + 1) * pair].astype(jnp.bfloat16)
            mixed = mixed + mm(weights, kv_all[both(chip(k, flip_x)), HD:])
        return high, total, mixed

    parts[0].across()
    d_gather.across()
    hid_gather.across()
    parts[1].own()
    d_gather.over()
    parts[0].over()
    hid_gather.over(0)
    hid_gather.finish_column()
    for k in range(4):
        project(k, 0)
    high_a, total_a, mixed_a = attend(0)
    hid_gather.over(1, 2, 3)
    hid_gather.finish_other()
    for k in range(4):
        project(k, 1)
    high_b, total_b, mixed_b = attend(1)
    high = jnp.maximum(high_a, high_b)
    part_a = jnp.exp(high_a - high)
    part_b = jnp.exp(high_b - high)
    total = total_a * part_a + total_b * part_b
    lse = high + jnp.log(total)
    inverse = 1.0 / total
    part_a = part_a * inverse
    part_b = part_b * inverse
    attended = pick_heads(mixed_a * part_a + mixed_b * part_b).astype(jnp.bfloat16)
    product = dattended.astype(jnp.float32) * attended.astype(jnp.float32)
    delta = jnp.sum(two_heads(product), axis=1, keepdims=True)
    lane = lax.broadcasted_iota(jnp.int32, (2 * n, 128), 1)
    packed = jnp.where(lane == 0, lse, jnp.where(lane == 1, delta, 0.0)).T
    stats[me] = packed[:2]
    stat_copies = []
    for step in range(1, peers):
        made = pltpu.make_async_remote_copy(
            src_ref=stats.at[me],
            dst_ref=stats.at[me],
            send_sem=stat_send.at[step],
            recv_sem=stat_recv.at[step],
            device_id={"tile": lax.rem(me + step, peers)},
            device_id_type=pl.DeviceIdType.MESH,
        )
        made.start()
        stat_copies.append(made)
    parts[1].across()
    parts[2].own()
    block_out[...] = (hidden.astype(jnp.float32) + mm(attended, ow[...])).astype(jnp.bfloat16)
    store(block_out, block_res)
    q_all[...] = scaled_query(hid_all[...])
    dquery = jnp.zeros((pair, HD), jnp.float32)
    for flip_x in (0, 1):
        part = part_b if flip_x else part_a
        for k in range(4):
            j = 4 * flip_x + k
            span = both(chip(k, flip_x))
            prob = exp_buf[:, j * pair : (j + 1) * pair] * part
            dprob = mm(d2, kv_all[span, HD:], NT)
            dscore = (prob * (dprob - delta)).astype(jnp.bfloat16)
            dquery = dquery + mm(dscore, kv_all[span, :HD])
    dquery = (pick_heads(dquery) * HDIM**-0.5).astype(jnp.bfloat16)
    grad_h = up[...].astype(jnp.float32) + mm(dquery, qk[0], NT)
    d_gather.finish_column()
    d_gather.finish_other()

    k2 = two_heads(key_value[:, :HD])
    v2 = two_heads(key_value[:, HD:])
    st_buf[...] = mm(k2, q_all[...], NT)
    dpt_buf[...] = mm(v2, d_all[...], NT)
    for step in range(1, peers):
        block = lax.rem(me - step + peers, peers)
        pltpu.make_async_remote_copy(
            src_ref=stats.at[block],
            dst_ref=stats.at[block],
            send_sem=stat_send.at[step],
            recv_sem=stat_recv.at[step],
            device_id={"tile": lower},
            device_id_type=pl.DeviceIdType.MESH,
        ).wait_recv()
    dk = jnp.zeros((2 * n, HD), jnp.float32)
    dv = jnp.zeros((2 * n, HD), jnp.float32)
    group = 4
    for at in range(0, peers, group):
        span = slice(at * n, (at + group) * n)

        def stat_rows(kind):
            heads = []
            for h in range(HEADS):
                lines = [stats[t, kind : kind + 1, h * n : (h + 1) * n] for t in range(at, at + group)]
                heads.append(jnp.broadcast_to(jnp.concatenate(lines, axis=1), (n, group * n)))
            return jnp.concatenate(heads, axis=0)

        prob_t = jnp.exp(st_buf[:, span] - stat_rows(0))
        dscore_t = (prob_t * (dpt_buf[:, span] - stat_rows(1))).astype(jnp.bfloat16)
        dv = dv + mm(prob_t.astype(jnp.bfloat16), d_all[span, :])
        dk = dk + mm(dscore_t, q_all[span, :])
    dkeys = pick_heads(dk).astype(jnp.bfloat16)
    dvalues = pick_heads(dv).astype(jnp.bfloat16)
    grad_h = grad_h + mm(dkeys, qk[1], NT) + mm(dvalues, vw[...], NT)
    dhidden = grad_h.astype(jnp.bfloat16)
    dh_all[mine, :] = dhidden
    dh_gather.own()
    parts[1].over()
    parts[2].across()
    parts[3].own()

    def back_row(a, grads):
        even = mm(grads, conv[a, 1], NT)
        later = mm(grads, conv[a, 0], NT)
        later = jnp.where(row_at == n - 1, 0.0, pltpu.roll(later, n - 1, 0))
        return even, mm(grads, conv[a, 2], NT) + later

    even_mid, odd_mid = back_row(1, dhidden)
    grad_fine[0, :, :chans] = even_mid.astype(jnp.bfloat16)
    grad_fine[0, :, chans:] = odd_mid.astype(jnp.bfloat16)
    even_low, odd_low = back_row(2, dhidden)
    norm = 1.0 / math.sqrt(full)
    pair_at = lax.broadcasted_iota(jnp.int32, (pair, chans), 0)
    edge = jnp.logical_or(pair_at == n - 1, pair_at == pair - 1)

    def kernel_grads(flip_x, which, last, first):
        straight = []
        moved = []
        for k in which:
            block = dh_all[both(chip(k, flip_x)), :]
            rolled = pltpu.roll(block.astype(jnp.float32), pair - 1, 0)
            straight.append(block)
            moved.append(jnp.where(edge, 0.0, rolled).astype(jnp.bfloat16))
        straight = jnp.concatenate(straight, axis=0)
        moved = jnp.concatenate(moved, axis=0)

        def features(ref, part, shift):
            picks = []
            for k in which:
                at = chip(k, flip_x) + shift
                picks.append(ref[at, part * chans : (part + 1) * chans, :])
                picks.append(ref[at + 1, part * chans : (part + 1) * chans, :])
            return jnp.concatenate(picks, axis=1)

        for a, ref, shift in ((1, mid_t, 0), (2, low_t, 1), (0, low_t, 0)):
            for b in (1, 2, 0):
                part = mm(features(ref, 0 if b == 1 else 1, shift), straight if b else moved)
                tap = 3 * a + b
                if not first:
                    part = part + acc[tap]
                if last:
                    grad_conv[tap] = part * norm
                    store(grad_conv.at[tap], grad_conv_res.at[tap])
                else:
                    acc[tap] = part

    dh_gather.across()
    parts[3].across()
    parts[2].over()
    dh_gather.over(0)
    parts[3].over()
    for part in parts:
        part.finish_column()
        part.finish_other()
    dh_gather.finish_column()
    kernel_grads(0, (0, 1, 2, 3), False, True)
    dh_gather.over(1, 2, 3)
    dh_gather.finish_other(0, 1)
    kernel_grads(1, (0, 1), False, False)
    dh_gather.finish_other(2, 3)

    below = dh_all[pl.ds(pl.multiple_of(lower * n, n), n), :]
    below = jnp.where(me == peers - 1, jnp.zeros_like(below), below)
    even_top, odd_top = back_row(0, below)
    grad_fine[1, :, :chans] = (even_low + even_top).astype(jnp.bfloat16)
    grad_fine[1, :, chans:] = (odd_low + odd_top).astype(jnp.bfloat16)
    store(grad_fine, grad_fine_res)

    kernel_grads(1, (2, 3), True, False)
    halo.wait_send()
    for gather in (*parts, hid_gather, d_gather, dh_gather):
        gather.drain()
    for made in stat_copies:
        made.wait_send()
    for made in stores:
        made.wait()


def emit_kernel(count, *refs):
    sources, targets, sem = refs[:count], refs[count : 2 * count], refs[2 * count]
    moves = []
    for source, target in zip(sources, targets):
        pieces = source.shape[0] if len(source.shape) > 2 else 1
        for i in range(pieces):
            a, b = (source.at[i], target.at[i]) if pieces > 1 else (source, target)
            moves.append(pltpu.make_async_copy(a, b, sem.at[len(moves)]))
    for move in moves:
        move.start()
    for move in moves:
        move.wait()


def emit(*arrays):
    where = pl.BlockSpec(memory_space=pl.ANY)
    return pl.pallas_call(
        functools.partial(emit_kernel, len(arrays)),
        out_shape=tuple(jax.ShapeDtypeStruct(v.shape, v.dtype) for v in arrays),
        in_specs=[where] * len(arrays),
        out_specs=(where,) * len(arrays),
        scratch_shapes=[pltpu.SemaphoreType.DMA((16,))],
        compiler_params=pltpu.CompilerParams(vmem_limit_bytes=2**20),
    )(*arrays)


def fused_body(fine, conv_weight, qk_weight, v_weight, o_weight, upstream):
    peers = lax.axis_size("tile")
    n, chans = upstream.shape
    full = n * peers
    hbm = pl.BlockSpec(memory_space=pltpu.HBM)
    free = pl.BlockSpec(memory_space=pl.ANY)
    dma = pltpu.SemaphoreType.DMA
    low = jnp.bfloat16
    sources = (fine, conv_weight, qk_weight, v_weight, o_weight, upstream)
    block_out, grad_conv, grad_fine = pl.pallas_call(
        functools.partial(fused_kernel, peers),
        out_shape=(
            jax.ShapeDtypeStruct((n, chans), low),
            jax.ShapeDtypeStruct((9, chans, chans), jnp.float32),
            jax.ShapeDtypeStruct((2, n, 2 * chans), low),
        ),
        in_specs=[hbm] * 6,
        out_specs=(free, free, free),
        scratch_shapes=[
            pltpu.VMEM(fine.shape, low),
            pltpu.VMEM(conv_weight.shape, low),
            pltpu.VMEM(qk_weight.shape, low),
            pltpu.VMEM(v_weight.shape, low),
            pltpu.VMEM(o_weight.shape, low),
            pltpu.VMEM(upstream.shape, low),
            pltpu.VMEM((n, chans), low),
            pltpu.VMEM((9, chans, chans), jnp.float32),
            pltpu.VMEM((2, n, 2 * chans), low),
            dma((6,)),
            dma((11,)),
            pltpu.VMEM((2 * n, chans), low),
            pltpu.VMEM((full, chans), low),
            pltpu.VMEM((full, 2 * HD), low),
            pltpu.VMEM((full, HD), low),
            pltpu.VMEM((full, HD), low),
            pltpu.VMEM((full, chans), low),
            pltpu.VMEM((peers, 2 * chans, n), low),
            pltpu.VMEM((peers + 1, 2 * chans, n), low),
            pltpu.VMEM((peers, 2, 2 * n), jnp.float32),
            pltpu.VMEM((2 * n, full), jnp.float32),
            pltpu.VMEM((2 * n, full), jnp.float32),
            pltpu.VMEM((2 * n, full), jnp.float32),
            pltpu.VMEM((chans, 2 * HD), low),
            pltpu.VMEM((9, chans, chans), jnp.float32),
            dma((7, 16)),
            dma((7, 16)),
            dma((peers,)),
            dma((peers,)),
            dma,
            dma,
        ],
        compiler_params=pltpu.CompilerParams(
            collective_id=0, has_side_effects=True, vmem_limit_bytes=36 * 2**20
        ),
    )(*[pltpu.with_memory_space_constraint(v, pltpu.HBM) for v in sources])
    block_out, grad_conv, grad_fine = emit(block_out, grad_conv, grad_fine.reshape(fine.shape))
    return block_out, grad_conv.reshape(3, 3, chans, chans), grad_fine


def solution(mesh):
    def whole(fine, *rest):
        devices = mesh.shape["groups"] * mesh.shape["tile"]
        one_row = fine.shape[0] == 2 * devices and fine.shape[1] == 256 and fine.shape[2] == 256
        fits = mesh.shape["tile"] == 16
        return jax.shard_map(
            fused_body if one_row and fits else body,
            mesh=mesh,
            in_specs=(
                P(("groups", "tile"), None, None),
                P(),
                P(),
                P(),
                P(),
                P(("groups", "tile"), None),
            ),
            out_specs=(
                P(("groups", "tile"), None),
                P("groups", None, None, None),
                P(("groups", "tile"), None, None),
            ),
            check_vma=False,
        )(fine, *rest)

    return whole
```

```python
import functools
import math

import jax
import jax.numpy as jnp
from jax import lax
from jax.experimental import pallas as pl
from jax.experimental.pallas import tpu as pltpu
from jax.sharding import PartitionSpec as P

HEADS = 2
HDIM = 64
HD = 128


def shifted(x, axis, by):
    peers = lax.axis_size(axis)
    pairs = [(i, i + by) for i in range(peers) if 0 <= i + by < peers]
    return lax.ppermute(x, axis, pairs)


def head_view(mat):
    return mat.reshape(mat.shape[0], HEADS, HDIM)


def score_block(queries, keys):
    product = jnp.einsum(
        "qhd,khd->hqk", head_view(queries), head_view(keys), preferred_element_type=jnp.float32
    )
    return product * HDIM ** (-0.5)


def dot_back(left, right):
    return lax.dot_general(
        left, right, (((1,), (1,)), ((), ())), preferred_element_type=jnp.float32
    )


def dot_over(left, right):
    return lax.dot_general(
        left, right, (((0,), (0,)), ((), ())), preferred_element_type=jnp.float32
    )


def body(fine, conv_weight, qk_weight, v_weight, o_weight, upstream):
    rows = fine.shape[0] // 2
    cols = fine.shape[1] // 2
    chans = fine.shape[2]
    local = rows * cols
    scale = HDIM ** (-0.5)
    above = shifted(fine[-1:], "tile", 1)
    padded = jnp.pad(jnp.concatenate([above, fine], axis=0), ((0, 0), (1, 0), (0, 0)))
    taps = []
    total = jnp.zeros((local, chans), jnp.float32)
    for a in range(3):
        for b in range(3):
            tap = padded[a : a + 2 * rows : 2, b : b + 2 * cols : 2].reshape(local, chans)
            taps.append(tap)
            total = total + jnp.dot(tap, conv_weight[a, b], preferred_element_type=jnp.float32)
    hidden = total.astype(jnp.bfloat16)
    query = jnp.dot(hidden, qk_weight[0], preferred_element_type=jnp.float32).astype(jnp.bfloat16)
    key_loc = jnp.dot(hidden, qk_weight[1], preferred_element_type=jnp.float32).astype(jnp.bfloat16)
    value_loc = jnp.dot(hidden, v_weight, preferred_element_type=jnp.float32).astype(jnp.bfloat16)
    keys_all, values_all = (
        lax.all_gather(key_loc, "tile", axis=0, tiled=True),
        lax.all_gather(value_loc, "tile", axis=0, tiled=True),
    )
    everyone = keys_all.shape[0]
    block = math.gcd(everyone, 2048)
    steps_total = everyone // block

    def stats_step(index, carry):
        top, summed = carry
        scores = score_block(query, lax.dynamic_slice_in_dim(keys_all, index * block, block, 0))
        new_top = jnp.maximum(top, jnp.max(scores, axis=2))
        summed = summed * jnp.exp(top - new_top) + jnp.sum(
            jnp.exp(scores - new_top[:, :, None]), axis=2
        )
        return (new_top, summed)

    start_top = jnp.full((HEADS, local), -jnp.inf, jnp.float32)
    top, summed = lax.fori_loop(
        0, steps_total, stats_step, (start_top, jnp.zeros((HEADS, local), jnp.float32))
    )
    lse = top + jnp.log(summed)

    def value_step(index, acc):
        scores = score_block(query, lax.dynamic_slice_in_dim(keys_all, index * block, block, 0))
        weights = jnp.exp(scores - lse[:, :, None]).astype(jnp.bfloat16)
        v_part = head_view(lax.dynamic_slice_in_dim(values_all, index * block, block, 0))
        return acc + jnp.einsum("hqk,khd->qhd", weights, v_part, preferred_element_type=jnp.float32)

    mixed = lax.fori_loop(0, steps_total, value_step, jnp.zeros((local, HEADS, HDIM), jnp.float32))
    attended = mixed.reshape(local, HD).astype(jnp.bfloat16)
    block_out = (
        hidden.astype(jnp.float32) + jnp.dot(attended, o_weight, preferred_element_type=jnp.float32)
    ).astype(jnp.bfloat16)
    dattended = dot_back(upstream, o_weight).astype(jnp.bfloat16)
    product = dattended.astype(jnp.float32) * attended.astype(jnp.float32)
    delta = jnp.sum(product.reshape(local, HEADS, HDIM), axis=2).T

    def query_step(index, acc):
        k_part = lax.dynamic_slice_in_dim(keys_all, index * block, block, 0)
        v_part = lax.dynamic_slice_in_dim(values_all, index * block, block, 0)
        prob = jnp.exp(score_block(query, k_part) - lse[:, :, None])
        dprob = jnp.einsum(
            "qhd,khd->hqk",
            head_view(dattended),
            head_view(v_part),
            preferred_element_type=jnp.float32,
        )
        dscore = (prob * (dprob - delta[:, :, None]) * scale).astype(jnp.bfloat16)
        return acc + jnp.einsum(
            "hqk,khd->qhd", dscore, head_view(k_part), preferred_element_type=jnp.float32
        )

    dq_acc = lax.fori_loop(0, steps_total, query_step, jnp.zeros((local, HEADS, HDIM), jnp.float32))
    dquery = dq_acc.reshape(local, HD).astype(jnp.bfloat16)
    lse_all, delta_all = (
        lax.all_gather(lse.T, "tile", axis=0, tiled=True),
        lax.all_gather(delta.T, "tile", axis=0, tiled=True),
    )
    empty = jnp.zeros((local, HEADS, HDIM), jnp.float32)
    q_in = lax.all_gather(query, "tile", axis=0, tiled=True)
    d_in = lax.all_gather(dattended, "tile", axis=0, tiled=True)
    incoming = q_in.shape[0]
    sub = math.gcd(incoming, 2048)

    def inner(index, acc):
        dk_acc, dv_acc = acc
        at = index * sub
        q_part = lax.dynamic_slice_in_dim(q_in, at, sub, 0)
        d_part = lax.dynamic_slice_in_dim(d_in, at, sub, 0)
        l_part = lax.dynamic_slice_in_dim(lse_all, at, sub, 0).T
        e_part = lax.dynamic_slice_in_dim(delta_all, at, sub, 0).T
        prob = jnp.exp(score_block(q_part, key_loc) - l_part[:, :, None])
        dv_acc = dv_acc + jnp.einsum(
            "hqk,qhd->khd",
            prob.astype(jnp.bfloat16),
            head_view(d_part),
            preferred_element_type=jnp.float32,
        )
        dprob = jnp.einsum(
            "qhd,khd->hqk",
            head_view(d_part),
            head_view(value_loc),
            preferred_element_type=jnp.float32,
        )
        dscore = (prob * (dprob - e_part[:, :, None]) * scale).astype(jnp.bfloat16)
        dk_acc = dk_acc + jnp.einsum(
            "hqk,qhd->khd", dscore, head_view(q_part), preferred_element_type=jnp.float32
        )
        return (dk_acc, dv_acc)

    dk_acc, dv_acc = lax.fori_loop(0, incoming // sub, inner, (empty, empty))
    dkeys = dk_acc.reshape(local, HD).astype(jnp.bfloat16)
    dvalues = dv_acc.reshape(local, HD).astype(jnp.bfloat16)
    dhidden = upstream.astype(jnp.float32)
    dhidden = dhidden + dot_back(dquery, qk_weight[0])
    dhidden = dhidden + dot_back(dkeys, qk_weight[1])
    dhidden = dhidden + dot_back(dvalues, v_weight)
    dhidden = dhidden.astype(jnp.bfloat16)
    kernel_rows = []
    dpadded = jnp.zeros((2 * rows + 1, 2 * cols + 1, chans), jnp.float32)
    for a in range(3):
        row_list = []
        for b in range(3):
            row_list.append(dot_over(taps[3 * a + b], dhidden))
            back = dot_back(dhidden, conv_weight[a, b])
            dpadded = dpadded.at[a : a + 2 * rows : 2, b : b + 2 * cols : 2].add(
                back.reshape(rows, cols, chans)
            )
        kernel_rows.append(jnp.stack(row_list))
    kernel_local = jnp.stack(kernel_rows)
    grad_conv = lax.psum(kernel_local, "tile") * (1.0 / math.sqrt(everyone))
    below = shifted(dpadded[0:1, 1:].astype(jnp.bfloat16), "tile", -1).astype(jnp.float32)
    grad_fine = dpadded[1:, 1:]
    grad_fine = grad_fine.at[-1:].add(below)
    return (block_out, grad_conv, grad_fine.astype(jnp.bfloat16))


NT = (((1,), (1,)), ((), ()))
NN = (((1,), (0,)), ((), ()))


def mm(left, right, dims=NN):
    return lax.dot_general(left, right, dims, preferred_element_type=jnp.float32)


def two_heads(mat):
    lane = lax.broadcasted_iota(jnp.int32, mat.shape, 1)
    zero = jnp.zeros_like(mat)
    return jnp.concatenate(
        [jnp.where(lane < HDIM, mat, zero), jnp.where(lane < HDIM, zero, mat)], axis=0
    )


def pick_heads(mat):
    half = mat.shape[0] // 2
    lane = lax.broadcasted_iota(jnp.int32, (half, mat.shape[1]), 1)
    return jnp.where(lane < HDIM, mat[:half], mat[half:])


class Gather:
    def __init__(self, view, place, middle, send, recv, slot, relayed=False):
        self.view, self.place, self.send, self.recv, self.slot = view, place, send, recv, slot
        self.middle, self.relayed = middle, relayed
        self.copies = []
        self.middle_copies = []

    def copy(self, index, block, target):
        return pltpu.make_async_remote_copy(
            src_ref=self.view(block),
            dst_ref=self.view(block),
            send_sem=self.send.at[self.slot, index],
            recv_sem=self.recv.at[self.slot, index],
            device_id={"tile": target},
            device_id_type=pl.DeviceIdType.MESH,
        )

    def go(self, index, block, target):
        made = self.copy(index, block, target)
        made.start()
        self.copies.append(made)

    def go_middle(self, index, out, block, target):
        made = pltpu.make_async_remote_copy(
            src_ref=self.view(block),
            dst_ref=self.view(block),
            send_sem=self.send.at[self.slot, out],
            recv_sem=self.recv.at[self.slot, index],
            device_id={"tile": target},
            device_id_type=pl.DeviceIdType.MESH,
        )

        @pl.when(self.middle)
        def _():
            made.start()

        self.middle_copies.append(made)

    def landed(self, index, block):
        self.copy(index, block, self.place(0, 0, 1)).wait_recv()

    def own_z(self, *which):
        block = self.place(0, 0, 0)
        for k in which or (1, 2, 3):
            if k == 3 and self.relayed:
                self.go_middle(3, 3, block, self.place(3, 0, 0))
            else:
                self.go(k, block, self.place(k, 0, 0))

    def own_core(self):
        self.go(8, self.place(0, 0, 0), self.place(0, 0, 1))

    def own_x(self):
        self.go(4, self.place(0, 0, 0), self.place(0, 1, 0))
        self.own_core()

    def own(self):
        self.own_z()
        self.own_x()

    def across(self, *which, wide=True):
        for k in which or ((2, 1, 3) if self.relayed else (1, 2, 3)):
            block = self.place(k, 0, 0)
            self.landed(k, block)
            if k == 2 and self.relayed:
                self.go_middle(3, 0, block, self.place(1, 0, 0))
            if wide:
                self.go(4 + k, block, self.place(0, 1, 0))
            self.go(8 + k, block, self.place(0, 0, 1))

    def over(self, *which):
        for k in which or (0, 1, 2, 3):
            block = self.place(k, 1, 0)
            self.landed(4 + k, block)
            self.go(12 + k, block, self.place(0, 0, 1))

    def finish_column(self, *which):
        for k in which or (0, 1, 2, 3):
            self.landed(8 + k, self.place(k, 0, 1))

    def finish_other(self, *which):
        for k in which or (0, 1, 2, 3):
            self.landed(12 + k, self.place(k, 1, 1))

    def drain(self):
        for made in self.copies:
            made.wait_send()
        for made in self.middle_copies:

            @pl.when(self.middle)
            def _(made=made):
                made.wait_send()


def fused_kernel(
    peers,
    fine_hbm,
    conv_hbm,
    qk_hbm,
    vw_hbm,
    ow_hbm,
    up_hbm,
    block_res,
    grad_conv_res,
    grad_fine_res,
    fine,
    conv,
    qk,
    vw,
    ow,
    up,
    block_out,
    grad_conv,
    grad_fine,
    in_sem,
    out_sem,
    above,
    hid_all,
    kv_all,
    q_all,
    d_all,
    dh_all,
    mid_t,
    low_t,
    stats,
    exp_buf,
    st_buf,
    dpt_buf,
    kv_w,
    acc,
    send,
    recv,
    stat_send,
    stat_recv,
    halo_send,
    halo_recv,
    strip_sum,
    strip_out,
    strip_in,
    fin_all,
):
    me = lax.axis_index("tile")
    n = up.shape[0]
    chans = up.shape[1]
    full = n * peers
    pair = 2 * n
    lower = lax.rem(me + 1, peers)
    core = lax.rem(me, 2)
    col = lax.rem(lax.div(me, 2), 2)
    level = lax.div(me, 4)
    middle = lax.rem(level + 1, 4) >= 2
    levels = (level, level + 1 - 2 * lax.rem(level, 2), lax.rem(level + 2, 4), 3 - level)

    def place(k, flip_x, flip_core):
        x = 1 - col if flip_x else col
        c = 1 - core if flip_core else core
        return levels[k] * 4 + x * 2 + c

    def chip(k, flip_x):
        return levels[k] * 4 + (1 - col if flip_x else col) * 2

    barrier = pltpu.get_barrier_semaphore()
    for step in range(1, peers):
        pl.semaphore_signal(
            barrier,
            inc=1,
            device_id={"tile": lax.rem(me + step, peers)},
            device_id_type=pl.DeviceIdType.MESH,
        )
    moves = (
        (up_hbm, up), (ow_hbm, ow), (fine_hbm, fine), (conv_hbm, conv), (qk_hbm, qk), (vw_hbm, vw)
    )
    loads = [pltpu.make_async_copy(a, b, in_sem.at[i]) for i, (a, b) in enumerate(moves)]
    for load in loads:
        load.start()
    stores = []

    def store(source, target):
        made = pltpu.make_async_copy(source, target, out_sem.at[len(stores)])
        made.start()
        stores.append(made)

    def rows(ref):
        return lambda t: ref.at[pl.ds(pl.multiple_of(t * n, n), n), :]

    def cols(ref, part, shift):
        lines = pl.ds(part * chans, chans)
        return lambda t: ref.at[t + shift, lines, :]

    def both(t):
        return pl.ds(pl.multiple_of(t * n, pair), pair)

    mine = pl.ds(pl.multiple_of(me * n, n), n)
    halo = pltpu.make_async_remote_copy(
        src_ref=fine_hbm.at[1],
        dst_ref=above,
        send_sem=halo_send,
        recv_sem=halo_recv,
        device_id={"tile": lower},
        device_id_type=pl.DeviceIdType.MESH,
    )
    pl.semaphore_wait(barrier, peers - 1)
    halo.start()
    views = (cols(low_t, 1, 1), cols(low_t, 0, 1))
    parts = [Gather(view, place, middle, send, recv, i, True) for i, view in enumerate(views)]
    mid_gather = Gather(lambda t: mid_t.at[t], place, middle, send, recv, 2)
    fin_gather = Gather(lambda t: fin_all.at[t], place, middle, send, recv, 3)
    hid_gather = Gather(rows(hid_all), place, middle, send, recv, 4)
    d_gather = Gather(rows(d_all), place, middle, send, recv, 5)
    dh_gather = Gather(rows(dh_all), place, middle, send, recv, 6)

    loads[0].wait()
    loads[1].wait()
    dattended = mm(up[...], ow[...], NT).astype(jnp.bfloat16)
    d_all[mine, :] = dattended
    d_gather.own()

    line = lax.broadcasted_iota(jnp.int32, (2 * n, 2 * n), 0)
    cell = lax.broadcasted_iota(jnp.int32, (2 * n, 2 * n), 1)
    wanted = jnp.where(line < n, 2 * line, 2 * (line - n) + 1)
    order = jnp.where(cell == wanted, 1.0, 0.0).astype(jnp.bfloat16)

    def apart(row):
        sorted_row = mm(order, row).astype(jnp.bfloat16)
        return sorted_row[:n], sorted_row[n:]

    loads[2].wait()
    mid_even, mid_odd = apart(fine[0])
    low_even, low_odd = apart(fine[1])
    mid_t[me, :chans, :] = mid_even.T

    for load in loads[3:]:
        load.wait()
    mid_t[me, chans:, :] = mid_odd.T
    low_t[me + 1, :chans, :] = low_even.T
    low_t[me + 1, chans:, :] = low_odd.T
    mid_gather.own_x()
    for part in parts:
        part.own_x()
    low_t[0] = jnp.zeros_like(low_t[0])
    kv_w[:, :HD] = qk[1]
    kv_w[:, HD:] = vw[...]

    def conv_row(a, even, odd):
        return mm(even, conv[a, 1]) + mm(odd, conv[a, 2]), mm(odd, conv[a, 0])

    mid, mid_late = conv_row(1, mid_even, mid_odd)
    low, low_late = conv_row(2, low_even, low_odd)
    halo.wait_recv()
    top_even, top_odd = apart(jnp.where(me == 0, jnp.zeros_like(above[...]), above[...]))
    top, top_late = conv_row(0, top_even, top_odd)
    late = top_late + mid_late + low_late
    row_at = lax.broadcasted_iota(jnp.int32, (n, chans), 0)
    late = jnp.where(row_at == 0, 0.0, pltpu.roll(late, 1, 0))
    hidden = (top + mid + low + late).astype(jnp.bfloat16)
    hid_all[mine, :] = hidden
    hid_gather.own()

    def scaled_query(mat):
        full_query = mm(mat, qk[0]).astype(jnp.bfloat16)
        return (full_query.astype(jnp.float32) * HDIM**-0.5).astype(jnp.bfloat16)

    key_value = mm(hidden, kv_w[...]).astype(jnp.bfloat16)
    q2 = two_heads(scaled_query(hidden))
    d2 = two_heads(dattended)

    def project(k, flip_x):
        span = both(chip(k, flip_x))
        kv_all[span, :] = mm(hid_all[span, :], kv_w[...]).astype(jnp.bfloat16)

    def attend(flip_x):
        tops = []
        for k in range(4):
            j = 4 * flip_x + k
            scores = mm(q2, kv_all[both(chip(k, flip_x)), :HD], NT)
            st_buf[:, j * pair : (j + 1) * pair] = scores
            tops.append(scores)
        block = st_buf[:, 4 * flip_x * pair : 4 * (flip_x + 1) * pair]
        high = jnp.max(block, axis=1, keepdims=True)
        expd = jnp.exp(block - high)
        exp_buf[:, 4 * flip_x * pair : 4 * (flip_x + 1) * pair] = expd
        total = jnp.sum(expd, axis=1, keepdims=True)
        mixed = jnp.zeros((pair, HD), jnp.float32)
        for k in range(4):
            weights = expd[:, k * pair : (k + 1) * pair].astype(jnp.bfloat16)
            mixed = mixed + mm(weights, kv_all[both(chip(k, flip_x)), HD:])
        return high, total, mixed

    d_gather.across()
    hid_gather.across()
    parts[0].own_z()
    mid_gather.over(0)
    d_gather.over()
    hid_gather.over(0)
    hid_gather.finish_column()
    for k in range(4):
        project(k, 0)
    high_a, total_a, mixed_a = attend(0)
    parts[1].own_z()
    hid_gather.over(1, 2, 3)
    hid_gather.finish_other()
    for k in range(4):
        project(k, 1)

    high_b, total_b, mixed_b = attend(1)
    high = jnp.maximum(high_a, high_b)
    part_a = jnp.exp(high_a - high)
    part_b = jnp.exp(high_b - high)
    total = total_a * part_a + total_b * part_b
    lse = high + jnp.log(total)
    inverse = 1.0 / total
    part_a = part_a * inverse
    part_b = part_b * inverse
    attended = pick_heads(mixed_a * part_a + mixed_b * part_b).astype(jnp.bfloat16)
    product = dattended.astype(jnp.float32) * attended.astype(jnp.float32)
    delta = jnp.sum(two_heads(product), axis=1, keepdims=True)
    lane = lax.broadcasted_iota(jnp.int32, (2 * n, 128), 1)
    packed = jnp.where(lane == 0, lse, jnp.where(lane == 1, delta, 0.0)).T
    stats[me] = packed[:2]
    stat_copies = []
    for step in range(1, peers):
        made = pltpu.make_async_remote_copy(
            src_ref=stats.at[me],
            dst_ref=stats.at[me],
            send_sem=stat_send.at[step],
            recv_sem=stat_recv.at[step],
            device_id={"tile": lax.rem(me + step, peers)},
            device_id_type=pl.DeviceIdType.MESH,
        )
        made.start()
        stat_copies.append(made)
    parts[0].across()
    block_out[...] = (hidden.astype(jnp.float32) + mm(attended, ow[...])).astype(jnp.bfloat16)
    store(block_out, block_res)
    q_all[...] = scaled_query(hid_all[...])
    dquery = jnp.zeros((pair, HD), jnp.float32)
    for flip_x in (0, 1):
        part = part_b if flip_x else part_a
        for k in range(4):
            j = 4 * flip_x + k
            span = both(chip(k, flip_x))
            prob = exp_buf[:, j * pair : (j + 1) * pair] * part
            dprob = mm(d2, kv_all[span, HD:], NT)
            dscore = (prob * (dprob - delta)).astype(jnp.bfloat16)
            dquery = dquery + mm(dscore, kv_all[span, :HD])
    dquery = (pick_heads(dquery) * HDIM**-0.5).astype(jnp.bfloat16)
    grad_h = up[...].astype(jnp.float32) + mm(dquery, qk[0], NT)
    d_gather.finish_column()
    d_gather.finish_other()
    parts[1].across()

    k2 = two_heads(key_value[:, :HD])
    v2 = two_heads(key_value[:, HD:])
    st_buf[...] = mm(k2, q_all[...], NT)
    dpt_buf[...] = mm(v2, d_all[...], NT)
    for step in range(1, peers):
        block = lax.rem(me - step + peers, peers)
        pltpu.make_async_remote_copy(
            src_ref=stats.at[block],
            dst_ref=stats.at[block],
            send_sem=stat_send.at[step],
            recv_sem=stat_recv.at[step],
            device_id={"tile": lower},
            device_id_type=pl.DeviceIdType.MESH,
        ).wait_recv()
    dk = jnp.zeros((2 * n, HD), jnp.float32)
    dv = jnp.zeros((2 * n, HD), jnp.float32)
    group = 4
    for at in range(0, peers, group):
        span = slice(at * n, (at + group) * n)

        def stat_rows(kind):
            heads = []
            for h in range(HEADS):
                lines = [stats[t, kind : kind + 1, h * n : (h + 1) * n] for t in range(at, at + group)]
                heads.append(jnp.broadcast_to(jnp.concatenate(lines, axis=1), (n, group * n)))
            return jnp.concatenate(heads, axis=0)

        prob_t = jnp.exp(st_buf[:, span] - stat_rows(0))
        dscore_t = (prob_t * (dpt_buf[:, span] - stat_rows(1))).astype(jnp.bfloat16)
        dv = dv + mm(prob_t.astype(jnp.bfloat16), d_all[span, :])
        dk = dk + mm(dscore_t, q_all[span, :])
    dkeys = pick_heads(dk).astype(jnp.bfloat16)
    dvalues = pick_heads(dv).astype(jnp.bfloat16)
    grad_h = grad_h + mm(dkeys, qk[1], NT) + mm(dvalues, vw[...], NT)
    dhidden = grad_h.astype(jnp.bfloat16)
    dh_all[mine, :] = dhidden
    dh_gather.own()


    def back_row(a, grads):
        even = mm(grads, conv[a, 1], NT)
        later = mm(grads, conv[a, 0], NT)
        later = jnp.where(row_at == n - 1, 0.0, pltpu.roll(later, n - 1, 0))
        return even, mm(grads, conv[a, 2], NT) + later

    even_mid, odd_mid = back_row(1, dhidden)
    grad_fine[0, :, :chans] = even_mid.astype(jnp.bfloat16)
    grad_fine[0, :, chans:] = odd_mid.astype(jnp.bfloat16)
    even_low, odd_low = back_row(2, dhidden)
    norm = 1.0 / math.sqrt(full)
    pair_at = lax.broadcasted_iota(jnp.int32, (pair, chans), 0)
    edge = jnp.logical_or(pair_at == n - 1, pair_at == pair - 1)

    def kernel_grads(flip_x, which, last, first):
        straight = []
        moved = []
        for k in which:
            block = dh_all[both(chip(k, flip_x)), :]
            rolled = pltpu.roll(block.astype(jnp.float32), pair - 1, 0)
            straight.append(block)
            moved.append(jnp.where(edge, 0.0, rolled).astype(jnp.bfloat16))
        straight = jnp.concatenate(straight, axis=0)
        moved = jnp.concatenate(moved, axis=0)

        def features(part, shift):
            picks = []
            for k in which:
                at = chip(k, flip_x) + shift
                picks.append(low_t[at, part * chans : (part + 1) * chans, :])
                picks.append(low_t[at + 1, part * chans : (part + 1) * chans, :])
            return jnp.concatenate(picks, axis=1)

        for a, shift in ((2, 1), (0, 0)):
            for b in (1, 2, 0):
                part = mm(features(0 if b == 1 else 1, shift), straight if b else moved)
                tap = 3 * a + b
                if not first:
                    part = part + acc[tap]
                if last:
                    grad_conv[tap] = part * norm
                    store(grad_conv.at[tap], grad_conv_res.at[tap])
                else:
                    acc[tap] = part

    strip = chans // 4
    slim = strip // 4
    strip_at = pl.multiple_of((col * 2 + core) * strip, strip)
    strip_copies = []

    def strip_copy(k, target_level):
        return pltpu.make_async_remote_copy(
            src_ref=strip_out.at[target_level],
            dst_ref=strip_in.at[level],
            send_sem=stat_send.at[peers + k],
            recv_sem=stat_recv.at[peers + k],
            device_id={"tile": place(k, 0, 0)},
            device_id_type=pl.DeviceIdType.MESH,
        )

    def strips():
        at = level * 4
        block = dh_all[pl.ds(pl.multiple_of(at * n, 4 * n), 4 * n), :]
        block_row = lax.broadcasted_iota(jnp.int32, block.shape, 0)
        rolled = pltpu.roll(block.astype(jnp.float32), 4 * n - 1, 0)
        rolled = jnp.where(lax.rem(block_row, n) == n - 1, 0.0, rolled).astype(jnp.bfloat16)
        for b, part, grads in ((0, 1, rolled), (1, 0, block), (2, 1, block)):
            lines = pl.ds(pl.multiple_of(part * chans + strip_at, strip), strip)
            picks = jnp.concatenate([mid_t[at + i, lines, :] for i in range(4)], axis=1)
            sums = mm(picks, grads)
            for i in range(4):
                piece = sums[i * slim : (i + 1) * slim]
                strip_sum[i, b * slim : (b + 1) * slim, :] = piece
                strip_out[i, b * slim : (b + 1) * slim, :] = piece.astype(jnp.bfloat16)
        for k in (2, 3, 1):
            made = strip_copy(k, levels[k])
            made.start()
            strip_copies.append(made)

    def strips_sum():
        total = strip_sum[level]
        for k in (1, 2, 3):
            strip_copy(k, levels[k]).wait_recv()
        for k in (1, 2, 3):
            total = total + strip_in[levels[k]].astype(jnp.float32)
        fin_all[me] = (total * norm).astype(jnp.bfloat16)

    def strips_end():
        for b in range(3):
            for i in range(4):
                for r in range(4):
                    rows_at = r * strip + i * slim
                    piece = fin_all[i * 4 + r, b * slim : (b + 1) * slim, :]
                    grad_conv[3 + b, rows_at : rows_at + slim, :] = piece.astype(jnp.float32)
            store(grad_conv.at[3 + b], grad_conv_res.at[3 + b])

    dh_gather.over(0)
    dh_gather.across(1)
    dh_gather.finish_column(0)
    dh_gather.finish_other(0)
    mid_gather.finish_column(0)
    mid_gather.finish_other(0)
    strips()
    dh_gather.across(2, 3)

    for part in parts:
        part.over()
    dh_gather.over(1)
    dh_gather.finish_column(1, 2, 3)
    for part in parts:
        part.finish_column()
        part.finish_other()
    kernel_grads(0, (0, 1, 2, 3), False, True)
    dh_gather.over(2)

    strips_sum()
    fin_gather.own()
    dh_gather.over(3)
    dh_gather.finish_other(1, 2, 3)
    kernel_grads(1, (0, 1, 2, 3), True, False)
    fin_gather.across()

    below = dh_all[pl.ds(pl.multiple_of(lower * n, n), n), :]
    below = jnp.where(me == peers - 1, jnp.zeros_like(below), below)
    even_top, odd_top = back_row(0, below)
    grad_fine[1, :, :chans] = (even_low + even_top).astype(jnp.bfloat16)
    grad_fine[1, :, chans:] = (odd_low + odd_top).astype(jnp.bfloat16)
    store(grad_fine, grad_fine_res)

    fin_gather.over()
    fin_gather.finish_column()
    fin_gather.finish_other()
    strips_end()
    for made in strip_copies:
        made.wait_send()
    halo.wait_send()
    for gather in (*parts, mid_gather, fin_gather, hid_gather, d_gather, dh_gather):
        gather.drain()
    for made in stat_copies:
        made.wait_send()
    for made in stores:
        made.wait()


def emit_kernel(count, *refs):
    sources, targets, sem = refs[:count], refs[count : 2 * count], refs[2 * count]
    moves = []
    for source, target in zip(sources, targets):
        pieces = source.shape[0] if len(source.shape) > 2 else 1
        for i in range(pieces):
            a, b = (source.at[i], target.at[i]) if pieces > 1 else (source, target)
            moves.append(pltpu.make_async_copy(a, b, sem.at[len(moves)]))
    for move in moves:
        move.start()
    for move in moves:
        move.wait()


def emit(*arrays):
    where = pl.BlockSpec(memory_space=pl.ANY)
    return pl.pallas_call(
        functools.partial(emit_kernel, len(arrays)),
        out_shape=tuple(jax.ShapeDtypeStruct(v.shape, v.dtype) for v in arrays),
        in_specs=[where] * len(arrays),
        out_specs=(where,) * len(arrays),
        scratch_shapes=[pltpu.SemaphoreType.DMA((16,))],
        compiler_params=pltpu.CompilerParams(vmem_limit_bytes=2**20),
    )(*arrays)


def fused_body(fine, conv_weight, qk_weight, v_weight, o_weight, upstream):
    peers = lax.axis_size("tile")
    n, chans = upstream.shape
    full = n * peers
    hbm = pl.BlockSpec(memory_space=pltpu.HBM)
    free = pl.BlockSpec(memory_space=pl.ANY)
    dma = pltpu.SemaphoreType.DMA
    low = jnp.bfloat16
    sources = (fine, conv_weight, qk_weight, v_weight, o_weight, upstream)
    block_out, grad_conv, grad_fine = pl.pallas_call(
        functools.partial(fused_kernel, peers),
        out_shape=(
            jax.ShapeDtypeStruct((n, chans), low),
            jax.ShapeDtypeStruct((9, chans, chans), jnp.float32),
            jax.ShapeDtypeStruct((2, n, 2 * chans), low),
        ),
        in_specs=[hbm] * 6,
        out_specs=(free, free, free),
        scratch_shapes=[
            pltpu.VMEM(fine.shape, low),
            pltpu.VMEM(conv_weight.shape, low),
            pltpu.VMEM(qk_weight.shape, low),
            pltpu.VMEM(v_weight.shape, low),
            pltpu.VMEM(o_weight.shape, low),
            pltpu.VMEM(upstream.shape, low),
            pltpu.VMEM((n, chans), low),
            pltpu.VMEM((9, chans, chans), jnp.float32),
            pltpu.VMEM((2, n, 2 * chans), low),
            dma((6,)),
            dma((11,)),
            pltpu.VMEM((2 * n, chans), low),
            pltpu.VMEM((full, chans), low),
            pltpu.VMEM((full, 2 * HD), low),
            pltpu.VMEM((full, HD), low),
            pltpu.VMEM((full, HD), low),
            pltpu.VMEM((full, chans), low),
            pltpu.VMEM((peers, 2 * chans, n), low),
            pltpu.VMEM((peers + 1, 2 * chans, n), low),
            pltpu.VMEM((peers, 2, 2 * n), jnp.float32),
            pltpu.VMEM((2 * n, full), jnp.float32),
            pltpu.VMEM((2 * n, full), jnp.float32),
            pltpu.VMEM((2 * n, full), jnp.float32),
            pltpu.VMEM((chans, 2 * HD), low),
            pltpu.VMEM((9, chans, chans), jnp.float32),
            dma((7, 16)),
            dma((7, 16)),
            dma((peers + 4,)),
            dma((peers + 4,)),
            dma,
            dma,
            pltpu.VMEM((4, 3 * chans // 16, chans), jnp.float32),
            pltpu.VMEM((4, 3 * chans // 16, chans), low),
            pltpu.VMEM((4, 3 * chans // 16, chans), low),
            pltpu.VMEM((peers, 3 * chans // 16, chans), low),
        ],
        compiler_params=pltpu.CompilerParams(
            collective_id=0, has_side_effects=True, vmem_limit_bytes=36 * 2**20
        ),
    )(*[pltpu.with_memory_space_constraint(v, pltpu.HBM) for v in sources])
    block_out, grad_conv, grad_fine = emit(block_out, grad_conv, grad_fine.reshape(fine.shape))
    return block_out, grad_conv.reshape(3, 3, chans, chans), grad_fine


def solution(mesh):
    def whole(fine, *rest):
        devices = mesh.shape["groups"] * mesh.shape["tile"]
        one_row = fine.shape[0] == 2 * devices and fine.shape[1] == 256 and fine.shape[2] == 256
        fits = mesh.shape["tile"] == 16
        return jax.shard_map(
            fused_body if one_row and fits else body,
            mesh=mesh,
            in_specs=(
                P(("groups", "tile"), None, None),
                P(),
                P(),
                P(),
                P(),
                P(("groups", "tile"), None),
            ),
            out_specs=(
                P(("groups", "tile"), None),
                P("groups", None, None, None),
                P(("groups", "tile"), None, None),
            ),
            check_vma=False,
        )(fine, *rest)

    return whole
```

```python
import functools
import math

import jax
import jax.numpy as jnp
from jax import lax
from jax.experimental import pallas as pl
from jax.experimental.pallas import tpu as pltpu
from jax.sharding import PartitionSpec as P

HEADS = 2
HDIM = 64
HD = 128


def shifted(x, axis, by):
    peers = lax.axis_size(axis)
    pairs = [(i, i + by) for i in range(peers) if 0 <= i + by < peers]
    return lax.ppermute(x, axis, pairs)


def head_view(mat):
    return mat.reshape(mat.shape[0], HEADS, HDIM)


def score_block(queries, keys):
    product = jnp.einsum(
        "qhd,khd->hqk", head_view(queries), head_view(keys), preferred_element_type=jnp.float32
    )
    return product * HDIM ** (-0.5)


def dot_back(left, right):
    return lax.dot_general(
        left, right, (((1,), (1,)), ((), ())), preferred_element_type=jnp.float32
    )


def dot_over(left, right):
    return lax.dot_general(
        left, right, (((0,), (0,)), ((), ())), preferred_element_type=jnp.float32
    )


def body(fine, conv_weight, qk_weight, v_weight, o_weight, upstream):
    rows = fine.shape[0] // 2
    cols = fine.shape[1] // 2
    chans = fine.shape[2]
    local = rows * cols
    scale = HDIM ** (-0.5)
    above = shifted(fine[-1:], "tile", 1)
    padded = jnp.pad(jnp.concatenate([above, fine], axis=0), ((0, 0), (1, 0), (0, 0)))
    taps = []
    total = jnp.zeros((local, chans), jnp.float32)
    for a in range(3):
        for b in range(3):
            tap = padded[a : a + 2 * rows : 2, b : b + 2 * cols : 2].reshape(local, chans)
            taps.append(tap)
            total = total + jnp.dot(tap, conv_weight[a, b], preferred_element_type=jnp.float32)
    hidden = total.astype(jnp.bfloat16)
    query = jnp.dot(hidden, qk_weight[0], preferred_element_type=jnp.float32).astype(jnp.bfloat16)
    key_loc = jnp.dot(hidden, qk_weight[1], preferred_element_type=jnp.float32).astype(jnp.bfloat16)
    value_loc = jnp.dot(hidden, v_weight, preferred_element_type=jnp.float32).astype(jnp.bfloat16)
    keys_all, values_all = (
        lax.all_gather(key_loc, "tile", axis=0, tiled=True),
        lax.all_gather(value_loc, "tile", axis=0, tiled=True),
    )
    everyone = keys_all.shape[0]
    block = math.gcd(everyone, 2048)
    steps_total = everyone // block

    def stats_step(index, carry):
        top, summed = carry
        scores = score_block(query, lax.dynamic_slice_in_dim(keys_all, index * block, block, 0))
        new_top = jnp.maximum(top, jnp.max(scores, axis=2))
        summed = summed * jnp.exp(top - new_top) + jnp.sum(
            jnp.exp(scores - new_top[:, :, None]), axis=2
        )
        return (new_top, summed)

    start_top = jnp.full((HEADS, local), -jnp.inf, jnp.float32)
    top, summed = lax.fori_loop(
        0, steps_total, stats_step, (start_top, jnp.zeros((HEADS, local), jnp.float32))
    )
    lse = top + jnp.log(summed)

    def value_step(index, acc):
        scores = score_block(query, lax.dynamic_slice_in_dim(keys_all, index * block, block, 0))
        weights = jnp.exp(scores - lse[:, :, None]).astype(jnp.bfloat16)
        v_part = head_view(lax.dynamic_slice_in_dim(values_all, index * block, block, 0))
        return acc + jnp.einsum("hqk,khd->qhd", weights, v_part, preferred_element_type=jnp.float32)

    mixed = lax.fori_loop(0, steps_total, value_step, jnp.zeros((local, HEADS, HDIM), jnp.float32))
    attended = mixed.reshape(local, HD).astype(jnp.bfloat16)
    block_out = (
        hidden.astype(jnp.float32) + jnp.dot(attended, o_weight, preferred_element_type=jnp.float32)
    ).astype(jnp.bfloat16)
    dattended = dot_back(upstream, o_weight).astype(jnp.bfloat16)
    product = dattended.astype(jnp.float32) * attended.astype(jnp.float32)
    delta = jnp.sum(product.reshape(local, HEADS, HDIM), axis=2).T

    def query_step(index, acc):
        k_part = lax.dynamic_slice_in_dim(keys_all, index * block, block, 0)
        v_part = lax.dynamic_slice_in_dim(values_all, index * block, block, 0)
        prob = jnp.exp(score_block(query, k_part) - lse[:, :, None])
        dprob = jnp.einsum(
            "qhd,khd->hqk",
            head_view(dattended),
            head_view(v_part),
            preferred_element_type=jnp.float32,
        )
        dscore = (prob * (dprob - delta[:, :, None]) * scale).astype(jnp.bfloat16)
        return acc + jnp.einsum(
            "hqk,khd->qhd", dscore, head_view(k_part), preferred_element_type=jnp.float32
        )

    dq_acc = lax.fori_loop(0, steps_total, query_step, jnp.zeros((local, HEADS, HDIM), jnp.float32))
    dquery = dq_acc.reshape(local, HD).astype(jnp.bfloat16)
    lse_all, delta_all = (
        lax.all_gather(lse.T, "tile", axis=0, tiled=True),
        lax.all_gather(delta.T, "tile", axis=0, tiled=True),
    )
    empty = jnp.zeros((local, HEADS, HDIM), jnp.float32)
    q_in = lax.all_gather(query, "tile", axis=0, tiled=True)
    d_in = lax.all_gather(dattended, "tile", axis=0, tiled=True)
    incoming = q_in.shape[0]
    sub = math.gcd(incoming, 2048)

    def inner(index, acc):
        dk_acc, dv_acc = acc
        at = index * sub
        q_part = lax.dynamic_slice_in_dim(q_in, at, sub, 0)
        d_part = lax.dynamic_slice_in_dim(d_in, at, sub, 0)
        l_part = lax.dynamic_slice_in_dim(lse_all, at, sub, 0).T
        e_part = lax.dynamic_slice_in_dim(delta_all, at, sub, 0).T
        prob = jnp.exp(score_block(q_part, key_loc) - l_part[:, :, None])
        dv_acc = dv_acc + jnp.einsum(
            "hqk,qhd->khd",
            prob.astype(jnp.bfloat16),
            head_view(d_part),
            preferred_element_type=jnp.float32,
        )
        dprob = jnp.einsum(
            "qhd,khd->hqk",
            head_view(d_part),
            head_view(value_loc),
            preferred_element_type=jnp.float32,
        )
        dscore = (prob * (dprob - e_part[:, :, None]) * scale).astype(jnp.bfloat16)
        dk_acc = dk_acc + jnp.einsum(
            "hqk,qhd->khd", dscore, head_view(q_part), preferred_element_type=jnp.float32
        )
        return (dk_acc, dv_acc)

    dk_acc, dv_acc = lax.fori_loop(0, incoming // sub, inner, (empty, empty))
    dkeys = dk_acc.reshape(local, HD).astype(jnp.bfloat16)
    dvalues = dv_acc.reshape(local, HD).astype(jnp.bfloat16)
    dhidden = upstream.astype(jnp.float32)
    dhidden = dhidden + dot_back(dquery, qk_weight[0])
    dhidden = dhidden + dot_back(dkeys, qk_weight[1])
    dhidden = dhidden + dot_back(dvalues, v_weight)
    dhidden = dhidden.astype(jnp.bfloat16)
    kernel_rows = []
    dpadded = jnp.zeros((2 * rows + 1, 2 * cols + 1, chans), jnp.float32)
    for a in range(3):
        row_list = []
        for b in range(3):
            row_list.append(dot_over(taps[3 * a + b], dhidden))
            back = dot_back(dhidden, conv_weight[a, b])
            dpadded = dpadded.at[a : a + 2 * rows : 2, b : b + 2 * cols : 2].add(
                back.reshape(rows, cols, chans)
            )
        kernel_rows.append(jnp.stack(row_list))
    kernel_local = jnp.stack(kernel_rows)
    grad_conv = lax.psum(kernel_local, "tile") * (1.0 / math.sqrt(everyone))
    below = shifted(dpadded[0:1, 1:].astype(jnp.bfloat16), "tile", -1).astype(jnp.float32)
    grad_fine = dpadded[1:, 1:]
    grad_fine = grad_fine.at[-1:].add(below)
    return (block_out, grad_conv, grad_fine.astype(jnp.bfloat16))


NT = (((1,), (1,)), ((), ()))
NN = (((1,), (0,)), ((), ()))


def mm(left, right, dims=NN):
    return lax.dot_general(left, right, dims, preferred_element_type=jnp.float32)


def two_heads(mat):
    lane = lax.broadcasted_iota(jnp.int32, mat.shape, 1)
    zero = jnp.zeros_like(mat)
    return jnp.concatenate(
        [jnp.where(lane < HDIM, mat, zero), jnp.where(lane < HDIM, zero, mat)], axis=0
    )


def pick_heads(mat):
    half = mat.shape[0] // 2
    lane = lax.broadcasted_iota(jnp.int32, (half, mat.shape[1]), 1)
    return jnp.where(lane < HDIM, mat[:half], mat[half:])


class Gather:
    def __init__(self, view, place, middle, send, recv, slot, relayed=False):
        self.view, self.place, self.send, self.recv, self.slot = view, place, send, recv, slot
        self.middle, self.relayed = middle, relayed
        self.copies = []
        self.middle_copies = []

    def copy(self, index, block, target):
        return pltpu.make_async_remote_copy(
            src_ref=self.view(block),
            dst_ref=self.view(block),
            send_sem=self.send.at[self.slot, index],
            recv_sem=self.recv.at[self.slot, index],
            device_id={"tile": target},
            device_id_type=pl.DeviceIdType.MESH,
        )

    def go(self, index, block, target):
        made = self.copy(index, block, target)
        made.start()
        self.copies.append(made)

    def go_middle(self, index, out, block, target):
        made = pltpu.make_async_remote_copy(
            src_ref=self.view(block),
            dst_ref=self.view(block),
            send_sem=self.send.at[self.slot, out],
            recv_sem=self.recv.at[self.slot, index],
            device_id={"tile": target},
            device_id_type=pl.DeviceIdType.MESH,
        )

        @pl.when(self.middle)
        def _():
            made.start()

        self.middle_copies.append(made)

    def landed(self, index, block):
        self.copy(index, block, self.place(0, 0, 1)).wait_recv()

    def own_z(self, *which):
        block = self.place(0, 0, 0)
        for k in which or (1, 2, 3):
            if k == 3 and self.relayed:
                self.go_middle(3, 3, block, self.place(3, 0, 0))
            else:
                self.go(k, block, self.place(k, 0, 0))

    def own_core(self):
        self.go(8, self.place(0, 0, 0), self.place(0, 0, 1))

    def own_x(self):
        self.go(4, self.place(0, 0, 0), self.place(0, 1, 0))
        self.own_core()

    def own(self):
        self.own_z()
        self.own_x()

    def across(self, *which, wide=True):
        for k in which or ((2, 1, 3) if self.relayed else (1, 2, 3)):
            block = self.place(k, 0, 0)
            self.landed(k, block)
            if k == 2 and self.relayed:
                self.go_middle(3, 0, block, self.place(1, 0, 0))
            if wide:
                self.go(4 + k, block, self.place(0, 1, 0))
            self.go(8 + k, block, self.place(0, 0, 1))

    def over(self, *which):
        for k in which or (0, 1, 2, 3):
            block = self.place(k, 1, 0)
            self.landed(4 + k, block)
            self.go(12 + k, block, self.place(0, 0, 1))

    def finish_column(self, *which):
        for k in which or (0, 1, 2, 3):
            self.landed(8 + k, self.place(k, 0, 1))

    def finish_other(self, *which):
        for k in which or (0, 1, 2, 3):
            self.landed(12 + k, self.place(k, 1, 1))

    def drain(self):
        for made in self.copies:
            made.wait_send()
        for made in self.middle_copies:

            @pl.when(self.middle)
            def _(made=made):
                made.wait_send()


def fused_kernel(
    peers,
    fine_hbm,
    conv_hbm,
    qk_hbm,
    vw_hbm,
    ow_hbm,
    up_hbm,
    block_res,
    grad_conv_res,
    grad_fine_res,
    fine,
    conv,
    qk,
    vw,
    ow,
    up,
    block_out,
    grad_conv,
    grad_fine,
    in_sem,
    out_sem,
    above,
    hid_all,
    kv_all,
    q_all,
    d_all,
    dh_all,
    mid_t,
    low_t,
    stats,
    exp_buf,
    st_buf,
    dpt_buf,
    kv_w,
    acc,
    send,
    recv,
    stat_send,
    stat_recv,
    halo_send,
    halo_recv,
    strip_sum,
    strip_out,
    strip_in,
    fin_all,
    scores,
    dp_buf,
):
    me = lax.axis_index("tile")
    n = up.shape[0]
    chans = up.shape[1]
    full = n * peers
    pair = 2 * n
    lower = lax.rem(me + 1, peers)
    core = lax.rem(me, 2)
    col = lax.rem(lax.div(me, 2), 2)
    level = lax.div(me, 4)
    middle = lax.rem(level + 1, 4) >= 2
    levels = (level, level + 1 - 2 * lax.rem(level, 2), lax.rem(level + 2, 4), 3 - level)

    def place(k, flip_x, flip_core):
        x = 1 - col if flip_x else col
        c = 1 - core if flip_core else core
        return levels[k] * 4 + x * 2 + c

    def chip(k, flip_x):
        return levels[k] * 4 + (1 - col if flip_x else col) * 2

    barrier = pltpu.get_barrier_semaphore()
    for step in range(1, peers):
        pl.semaphore_signal(
            barrier,
            inc=1,
            device_id={"tile": lax.rem(me + step, peers)},
            device_id_type=pl.DeviceIdType.MESH,
        )
    moves = (
        (up_hbm, up), (ow_hbm, ow), (fine_hbm, fine), (conv_hbm, conv), (qk_hbm, qk), (vw_hbm, vw)
    )
    loads = [pltpu.make_async_copy(a, b, in_sem.at[i]) for i, (a, b) in enumerate(moves)]
    for load in loads:
        load.start()
    stores = []

    def store(source, target):
        made = pltpu.make_async_copy(source, target, out_sem.at[len(stores)])
        made.start()
        stores.append(made)

    def rows(ref):
        return lambda t: ref.at[pl.ds(pl.multiple_of(t * n, n), n), :]

    def cols(ref, part, shift):
        lines = pl.ds(part * chans, chans)
        return lambda t: ref.at[t + shift, lines, :]

    def both(t):
        return pl.ds(pl.multiple_of(t * n, pair), pair)

    mine = pl.ds(pl.multiple_of(me * n, n), n)
    halo = pltpu.make_async_remote_copy(
        src_ref=fine_hbm.at[1],
        dst_ref=above,
        send_sem=halo_send,
        recv_sem=halo_recv,
        device_id={"tile": lower},
        device_id_type=pl.DeviceIdType.MESH,
    )
    pl.semaphore_wait(barrier, peers - 1)
    halo.start()
    views = (cols(low_t, 1, 1), cols(low_t, 0, 1))
    parts = [Gather(view, place, middle, send, recv, i, True) for i, view in enumerate(views)]
    mid_gather = Gather(lambda t: mid_t.at[t], place, middle, send, recv, 2)
    fin_gather = Gather(lambda t: fin_all.at[t], place, middle, send, recv, 3)
    hid_gather = Gather(rows(hid_all), place, middle, send, recv, 4)
    d_gather = Gather(rows(d_all), place, middle, send, recv, 5)
    dh_gather = Gather(rows(dh_all), place, middle, send, recv, 6)

    loads[0].wait()
    loads[1].wait()
    dattended = mm(up[...], ow[...], NT).astype(jnp.bfloat16)
    d_all[mine, :] = dattended
    d_gather.own()

    line = lax.broadcasted_iota(jnp.int32, (2 * n, 2 * n), 0)
    cell = lax.broadcasted_iota(jnp.int32, (2 * n, 2 * n), 1)
    wanted = jnp.where(line < n, 2 * line, 2 * (line - n) + 1)
    order = jnp.where(cell == wanted, 1.0, 0.0).astype(jnp.bfloat16)

    def apart(row):
        sorted_row = mm(order, row).astype(jnp.bfloat16)
        return sorted_row[:n], sorted_row[n:]

    loads[2].wait()
    mid_even, mid_odd = apart(fine[0])
    low_even, low_odd = apart(fine[1])
    mid_t[me, :chans, :] = mid_even.T

    for load in loads[3:]:
        load.wait()
    mid_t[me, chans:, :] = mid_odd.T
    low_t[me + 1, :chans, :] = low_even.T
    low_t[me + 1, chans:, :] = low_odd.T
    mid_gather.own_x()
    for part in parts:
        part.own_x()
    low_t[0] = jnp.zeros_like(low_t[0])
    kv_w[:, :HD] = qk[1]
    kv_w[:, HD:] = vw[...]

    def conv_row(a, even, odd):
        return mm(even, conv[a, 1]) + mm(odd, conv[a, 2]), mm(odd, conv[a, 0])

    mid, mid_late = conv_row(1, mid_even, mid_odd)
    low, low_late = conv_row(2, low_even, low_odd)
    halo.wait_recv()
    top_even, top_odd = apart(jnp.where(me == 0, jnp.zeros_like(above[...]), above[...]))
    top, top_late = conv_row(0, top_even, top_odd)
    late = top_late + mid_late + low_late
    row_at = lax.broadcasted_iota(jnp.int32, (n, chans), 0)
    late = jnp.where(row_at == 0, 0.0, pltpu.roll(late, 1, 0))
    hidden = (top + mid + low + late).astype(jnp.bfloat16)
    hid_all[mine, :] = hidden
    hid_gather.own()

    def scaled_query(mat):
        full_query = mm(mat, qk[0]).astype(jnp.bfloat16)
        return (full_query.astype(jnp.float32) * HDIM**-0.5).astype(jnp.bfloat16)

    key_value = mm(hidden, kv_w[...]).astype(jnp.bfloat16)
    q2 = two_heads(scaled_query(hidden))
    d2 = two_heads(dattended)

    def project(k, flip_x):
        span = both(chip(k, flip_x))
        kv_all[span, :] = mm(hid_all[span, :], kv_w[...]).astype(jnp.bfloat16)

    def attend(flip_x):
        for k in range(4):
            keys = kv_all[both(chip(k, flip_x)), :HD]
            scores[:, k * pair : (k + 1) * pair] = mm(q2, keys, NT)
        block = scores[...]
        high = jnp.max(block, axis=1, keepdims=True)
        expd = jnp.exp(block - high)
        exp_buf[:, 4 * flip_x * pair : 4 * (flip_x + 1) * pair] = expd
        total = jnp.sum(expd, axis=1, keepdims=True)
        mixed = jnp.zeros((pair, HD), jnp.float32)
        for k in range(4):
            weights = expd[:, k * pair : (k + 1) * pair].astype(jnp.bfloat16)
            mixed = mixed + mm(weights, kv_all[both(chip(k, flip_x)), HD:])
        return high, total, mixed

    k2 = two_heads(key_value[:, :HD])
    v2 = two_heads(key_value[:, HD:])

    def prepare_queries(flip_x):
        for k in range(4):
            j = 4 * flip_x + k
            span = both(chip(k, flip_x))
            queries = scaled_query(hid_all[span, :])
            q_all[span, :] = queries
            st_buf[:, j * pair : (j + 1) * pair] = mm(k2, queries, NT)

    def prepare_grads(flip_x):
        for k in range(4):
            j = 4 * flip_x + k
            dpt_buf[:, j * pair : (j + 1) * pair] = mm(v2, d_all[both(chip(k, flip_x)), :], NT)

    def prepare_probs(flip_x):
        for k in range(4):
            j = 4 * flip_x + k
            dp_buf[:, j * pair : (j + 1) * pair] = mm(d2, kv_all[both(chip(k, flip_x)), HD:], NT)

    d_gather.across()

    hid_gather.across()
    parts[0].own_z(2, 1)
    parts[1].own_z(2, 1)
    mid_gather.over(0)
    d_gather.over()
    hid_gather.over(0)
    hid_gather.finish_column()
    for k in range(4):
        project(k, 0)
    high_a, total_a, mixed_a = attend(0)
    parts[0].own_z(3)
    parts[1].own_z(3)
    hid_gather.over(1)

    prepare_queries(0)
    hid_gather.over(2)

    d_gather.finish_column()
    d_gather.finish_other()
    prepare_grads(0)
    prepare_probs(0)
    hid_gather.over(3)
    parts[0].across(2, 1)
    prepare_grads(1)
    hid_gather.finish_other()
    for k in range(4):
        project(k, 1)

    high_b, total_b, mixed_b = attend(1)
    high = jnp.maximum(high_a, high_b)
    part_a = jnp.exp(high_a - high)
    part_b = jnp.exp(high_b - high)
    total = total_a * part_a + total_b * part_b
    lse = high + jnp.log(total)
    inverse = 1.0 / total
    part_a = part_a * inverse
    part_b = part_b * inverse
    attended = pick_heads(mixed_a * part_a + mixed_b * part_b).astype(jnp.bfloat16)
    product = dattended.astype(jnp.float32) * attended.astype(jnp.float32)
    delta = jnp.sum(two_heads(product), axis=1, keepdims=True)
    lane = lax.broadcasted_iota(jnp.int32, (2 * n, 128), 1)
    packed = jnp.where(lane == 0, lse, jnp.where(lane == 1, delta, 0.0)).T
    stats[me] = packed[:2]
    stat_copies = []
    for step in range(1, peers):
        made = pltpu.make_async_remote_copy(
            src_ref=stats.at[me],
            dst_ref=stats.at[me],
            send_sem=stat_send.at[step],
            recv_sem=stat_recv.at[step],
            device_id={"tile": lax.rem(me + step, peers)},
            device_id_type=pl.DeviceIdType.MESH,
        )
        made.start()
        stat_copies.append(made)
    parts[0].across(3)
    parts[1].across(2, 1)
    block_out[...] = (hidden.astype(jnp.float32) + mm(attended, ow[...])).astype(jnp.bfloat16)
    store(block_out, block_res)
    prepare_queries(1)
    prepare_probs(1)
    dquery = jnp.zeros((pair, HD), jnp.float32)
    for flip_x in (0, 1):
        part = part_b if flip_x else part_a
        for k in range(4):
            j = 4 * flip_x + k
            span = both(chip(k, flip_x))
            prob = exp_buf[:, j * pair : (j + 1) * pair] * part
            dprob = dp_buf[:, j * pair : (j + 1) * pair]
            dscore = (prob * (dprob - delta)).astype(jnp.bfloat16)
            dquery = dquery + mm(dscore, kv_all[span, :HD])
    dquery = (pick_heads(dquery) * HDIM**-0.5).astype(jnp.bfloat16)
    grad_h = up[...].astype(jnp.float32) + mm(dquery, qk[0], NT)


    for step in range(1, peers):
        block = lax.rem(me - step + peers, peers)
        pltpu.make_async_remote_copy(
            src_ref=stats.at[block],
            dst_ref=stats.at[block],
            send_sem=stat_send.at[step],
            recv_sem=stat_recv.at[step],
            device_id={"tile": lower},
            device_id_type=pl.DeviceIdType.MESH,
        ).wait_recv()
    dk = jnp.zeros((2 * n, HD), jnp.float32)
    dv = jnp.zeros((2 * n, HD), jnp.float32)
    for flip_x in (0, 1):
        for k in range(4):
            j = 4 * flip_x + k
            at = chip(k, flip_x)
            span = both(at)

            def stat_rows(kind):
                heads = []
                for h in range(HEADS):
                    lines = [stats[at + c, kind : kind + 1, h * n : (h + 1) * n] for c in (0, 1)]
                    heads.append(jnp.broadcast_to(jnp.concatenate(lines, axis=1), (n, pair)))
                return jnp.concatenate(heads, axis=0)

            lanes = slice(j * pair, (j + 1) * pair)
            prob_t = jnp.exp(st_buf[:, lanes] - stat_rows(0))
            dscore_t = (prob_t * (dpt_buf[:, lanes] - stat_rows(1))).astype(jnp.bfloat16)
            dv = dv + mm(prob_t.astype(jnp.bfloat16), d_all[span, :])
            dk = dk + mm(dscore_t, q_all[span, :])
    dkeys = pick_heads(dk).astype(jnp.bfloat16)
    dvalues = pick_heads(dv).astype(jnp.bfloat16)
    grad_h = grad_h + mm(dkeys, qk[1], NT) + mm(dvalues, vw[...], NT)
    dhidden = grad_h.astype(jnp.bfloat16)
    dh_all[mine, :] = dhidden
    dh_gather.own()


    def back_row(a, grads):
        even = mm(grads, conv[a, 1], NT)
        later = mm(grads, conv[a, 0], NT)
        later = jnp.where(row_at == n - 1, 0.0, pltpu.roll(later, n - 1, 0))
        return even, mm(grads, conv[a, 2], NT) + later

    even_mid, odd_mid = back_row(1, dhidden)
    grad_fine[0, :, :chans] = even_mid.astype(jnp.bfloat16)
    grad_fine[0, :, chans:] = odd_mid.astype(jnp.bfloat16)
    even_low, odd_low = back_row(2, dhidden)
    norm = 1.0 / math.sqrt(full)
    pair_at = lax.broadcasted_iota(jnp.int32, (pair, chans), 0)
    edge = jnp.logical_or(pair_at == n - 1, pair_at == pair - 1)

    def kernel_grads(flip_x, which, last, first):
        straight = []
        moved = []
        for k in which:
            block = dh_all[both(chip(k, flip_x)), :]
            rolled = pltpu.roll(block.astype(jnp.float32), pair - 1, 0)
            straight.append(block)
            moved.append(jnp.where(edge, 0.0, rolled).astype(jnp.bfloat16))
        straight = jnp.concatenate(straight, axis=0)
        moved = jnp.concatenate(moved, axis=0)

        def features(part, shift):
            picks = []
            for k in which:
                at = chip(k, flip_x) + shift
                picks.append(low_t[at, part * chans : (part + 1) * chans, :])
                picks.append(low_t[at + 1, part * chans : (part + 1) * chans, :])
            return jnp.concatenate(picks, axis=1)

        for a, shift in ((2, 1), (0, 0)):
            for b in (1, 2, 0):
                part = mm(features(0 if b == 1 else 1, shift), straight if b else moved)
                tap = 3 * a + b
                if not first:
                    part = part + acc[tap]
                if last:
                    grad_conv[tap] = part * norm
                    store(grad_conv.at[tap], grad_conv_res.at[tap])
                else:
                    acc[tap] = part

    strip = chans // 4
    slim = strip // 4
    strip_at = pl.multiple_of((col * 2 + core) * strip, strip)
    strip_copies = []

    def strip_copy(k, target_level):
        return pltpu.make_async_remote_copy(
            src_ref=strip_out.at[target_level],
            dst_ref=strip_in.at[level],
            send_sem=stat_send.at[peers + k],
            recv_sem=stat_recv.at[peers + k],
            device_id={"tile": place(k, 0, 0)},
            device_id_type=pl.DeviceIdType.MESH,
        )

    def strips():
        at = level * 4
        block = dh_all[pl.ds(pl.multiple_of(at * n, 4 * n), 4 * n), :]
        block_row = lax.broadcasted_iota(jnp.int32, block.shape, 0)
        rolled = pltpu.roll(block.astype(jnp.float32), 4 * n - 1, 0)
        rolled = jnp.where(lax.rem(block_row, n) == n - 1, 0.0, rolled).astype(jnp.bfloat16)
        for b, part, grads in ((0, 1, rolled), (1, 0, block), (2, 1, block)):
            lines = pl.ds(pl.multiple_of(part * chans + strip_at, strip), strip)
            picks = jnp.concatenate([mid_t[at + i, lines, :] for i in range(4)], axis=1)
            sums = mm(picks, grads)
            for i in range(4):
                piece = sums[i * slim : (i + 1) * slim]
                strip_sum[i, b * slim : (b + 1) * slim, :] = piece
                strip_out[i, b * slim : (b + 1) * slim, :] = piece.astype(jnp.bfloat16)
        for k in (2, 3, 1):
            made = strip_copy(k, levels[k])
            made.start()
            strip_copies.append(made)

    def strips_sum():
        total = strip_sum[level]
        for k in (1, 2, 3):
            strip_copy(k, levels[k]).wait_recv()
        for k in (1, 2, 3):
            total = total + strip_in[levels[k]].astype(jnp.float32)
        fin_all[me] = (total * norm).astype(jnp.bfloat16)

    def strips_end():
        for b in range(3):
            for i in range(4):
                for r in range(4):
                    rows_at = r * strip + i * slim
                    piece = fin_all[i * 4 + r, b * slim : (b + 1) * slim, :]
                    grad_conv[3 + b, rows_at : rows_at + slim, :] = piece.astype(jnp.float32)
            store(grad_conv.at[3 + b], grad_conv_res.at[3 + b])

    parts[1].across(3)
    dh_gather.across(1)
    dh_gather.over(0)

    dh_gather.finish_column(0)
    dh_gather.finish_other(0)
    mid_gather.finish_column(0)
    mid_gather.finish_other(0)
    strips()

    dh_gather.across(2, 3)

    for part in parts:
        part.over()
    dh_gather.over(1)
    dh_gather.finish_column(1, 2, 3)
    for part in parts:
        part.finish_column()
        part.finish_other()
    kernel_grads(0, (0, 1, 2, 3), False, True)
    dh_gather.over(2)
    strips_sum()
    fin_gather.own()
    dh_gather.finish_other(1, 2)
    kernel_grads(1, (0, 1, 2), False, False)
    dh_gather.over(3)
    dh_gather.finish_other(3)
    kernel_grads(1, (3,), True, False)
    fin_gather.across()

    below = dh_all[pl.ds(pl.multiple_of(lower * n, n), n), :]
    below = jnp.where(me == peers - 1, jnp.zeros_like(below), below)
    even_top, odd_top = back_row(0, below)
    grad_fine[1, :, :chans] = (even_low + even_top).astype(jnp.bfloat16)
    grad_fine[1, :, chans:] = (odd_low + odd_top).astype(jnp.bfloat16)
    store(grad_fine, grad_fine_res)

    fin_gather.over()
    fin_gather.finish_column()
    fin_gather.finish_other()
    strips_end()
    for made in strip_copies:
        made.wait_send()
    halo.wait_send()
    for gather in (*parts, mid_gather, fin_gather, hid_gather, d_gather, dh_gather):
        gather.drain()
    for made in stat_copies:
        made.wait_send()
    for made in stores:
        made.wait()


def emit_kernel(count, *refs):
    sources, targets, sem = refs[:count], refs[count : 2 * count], refs[2 * count]
    moves = []
    for source, target in zip(sources, targets):
        pieces = source.shape[0] if len(source.shape) > 2 else 1
        for i in range(pieces):
            a, b = (source.at[i], target.at[i]) if pieces > 1 else (source, target)
            moves.append(pltpu.make_async_copy(a, b, sem.at[len(moves)]))
    for move in moves:
        move.start()
    for move in moves:
        move.wait()


def emit(*arrays):
    where = pl.BlockSpec(memory_space=pl.ANY)
    return pl.pallas_call(
        functools.partial(emit_kernel, len(arrays)),
        out_shape=tuple(jax.ShapeDtypeStruct(v.shape, v.dtype) for v in arrays),
        in_specs=[where] * len(arrays),
        out_specs=(where,) * len(arrays),
        scratch_shapes=[pltpu.SemaphoreType.DMA((16,))],
        compiler_params=pltpu.CompilerParams(vmem_limit_bytes=2**20),
    )(*arrays)


def fused_body(fine, conv_weight, qk_weight, v_weight, o_weight, upstream):
    peers = lax.axis_size("tile")
    n, chans = upstream.shape
    full = n * peers
    hbm = pl.BlockSpec(memory_space=pltpu.HBM)
    free = pl.BlockSpec(memory_space=pl.ANY)
    dma = pltpu.SemaphoreType.DMA
    low = jnp.bfloat16
    sources = (fine, conv_weight, qk_weight, v_weight, o_weight, upstream)
    block_out, grad_conv, grad_fine = pl.pallas_call(
        functools.partial(fused_kernel, peers),
        out_shape=(
            jax.ShapeDtypeStruct((n, chans), low),
            jax.ShapeDtypeStruct((9, chans, chans), jnp.float32),
            jax.ShapeDtypeStruct((2, n, 2 * chans), low),
        ),
        in_specs=[hbm] * 6,
        out_specs=(free, free, free),
        scratch_shapes=[
            pltpu.VMEM(fine.shape, low),
            pltpu.VMEM(conv_weight.shape, low),
            pltpu.VMEM(qk_weight.shape, low),
            pltpu.VMEM(v_weight.shape, low),
            pltpu.VMEM(o_weight.shape, low),
            pltpu.VMEM(upstream.shape, low),
            pltpu.VMEM((n, chans), low),
            pltpu.VMEM((9, chans, chans), jnp.float32),
            pltpu.VMEM((2, n, 2 * chans), low),
            dma((6,)),
            dma((11,)),
            pltpu.VMEM((2 * n, chans), low),
            pltpu.VMEM((full, chans), low),
            pltpu.VMEM((full, 2 * HD), low),
            pltpu.VMEM((full, HD), low),
            pltpu.VMEM((full, HD), low),
            pltpu.VMEM((full, chans), low),
            pltpu.VMEM((peers, 2 * chans, n), low),
            pltpu.VMEM((peers + 1, 2 * chans, n), low),
            pltpu.VMEM((peers, 2, 2 * n), jnp.float32),
            pltpu.VMEM((2 * n, full), jnp.float32),
            pltpu.VMEM((2 * n, full), jnp.float32),
            pltpu.VMEM((2 * n, full), jnp.float32),
            pltpu.VMEM((chans, 2 * HD), low),
            pltpu.VMEM((9, chans, chans), jnp.float32),
            dma((7, 16)),
            dma((7, 16)),
            dma((peers + 4,)),
            dma((peers + 4,)),
            dma,
            dma,
            pltpu.VMEM((4, 3 * chans // 16, chans), jnp.float32),
            pltpu.VMEM((4, 3 * chans // 16, chans), low),
            pltpu.VMEM((4, 3 * chans // 16, chans), low),
            pltpu.VMEM((peers, 3 * chans // 16, chans), low),
            pltpu.VMEM((2 * n, full // 2), jnp.float32),
            pltpu.VMEM((2 * n, full), jnp.float32),
        ],
        compiler_params=pltpu.CompilerParams(
            collective_id=0, has_side_effects=True, vmem_limit_bytes=36 * 2**20
        ),
    )(*[pltpu.with_memory_space_constraint(v, pltpu.HBM) for v in sources])
    block_out, grad_conv, grad_fine = emit(block_out, grad_conv, grad_fine.reshape(fine.shape))
    return block_out, grad_conv.reshape(3, 3, chans, chans), grad_fine


def solution(mesh):
    def whole(fine, *rest):
        devices = mesh.shape["groups"] * mesh.shape["tile"]
        one_row = fine.shape[0] == 2 * devices and fine.shape[1] == 256 and fine.shape[2] == 256
        fits = mesh.shape["tile"] == 16
        return jax.shard_map(
            fused_body if one_row and fits else body,
            mesh=mesh,
            in_specs=(
                P(("groups", "tile"), None, None),
                P(),
                P(),
                P(),
                P(),
                P(("groups", "tile"), None),
            ),
            out_specs=(
                P(("groups", "tile"), None),
                P("groups", None, None, None),
                P(("groups", "tile"), None, None),
            ),
            check_vma=False,
        )(fine, *rest)

    return whole
```

```python
import functools
import math

import jax
import jax.numpy as jnp
from jax import lax
from jax.experimental import pallas as pl
from jax.experimental.pallas import tpu as pltpu
from jax.sharding import PartitionSpec as P

HEADS = 2
HDIM = 64
HD = 128


def shifted(x, axis, by):
    peers = lax.axis_size(axis)
    pairs = [(i, i + by) for i in range(peers) if 0 <= i + by < peers]
    return lax.ppermute(x, axis, pairs)


def head_view(mat):
    return mat.reshape(mat.shape[0], HEADS, HDIM)


def score_block(queries, keys):
    product = jnp.einsum(
        "qhd,khd->hqk", head_view(queries), head_view(keys), preferred_element_type=jnp.float32
    )
    return product * HDIM ** (-0.5)


def dot_back(left, right):
    return lax.dot_general(
        left, right, (((1,), (1,)), ((), ())), preferred_element_type=jnp.float32
    )


def dot_over(left, right):
    return lax.dot_general(
        left, right, (((0,), (0,)), ((), ())), preferred_element_type=jnp.float32
    )


def body(fine, conv_weight, qk_weight, v_weight, o_weight, upstream):
    rows = fine.shape[0] // 2
    cols = fine.shape[1] // 2
    chans = fine.shape[2]
    local = rows * cols
    scale = HDIM ** (-0.5)
    above = shifted(fine[-1:], "tile", 1)
    padded = jnp.pad(jnp.concatenate([above, fine], axis=0), ((0, 0), (1, 0), (0, 0)))
    taps = []
    total = jnp.zeros((local, chans), jnp.float32)
    for a in range(3):
        for b in range(3):
            tap = padded[a : a + 2 * rows : 2, b : b + 2 * cols : 2].reshape(local, chans)
            taps.append(tap)
            total = total + jnp.dot(tap, conv_weight[a, b], preferred_element_type=jnp.float32)
    hidden = total.astype(jnp.bfloat16)
    query = jnp.dot(hidden, qk_weight[0], preferred_element_type=jnp.float32).astype(jnp.bfloat16)
    key_loc = jnp.dot(hidden, qk_weight[1], preferred_element_type=jnp.float32).astype(jnp.bfloat16)
    value_loc = jnp.dot(hidden, v_weight, preferred_element_type=jnp.float32).astype(jnp.bfloat16)
    keys_all, values_all = (
        lax.all_gather(key_loc, "tile", axis=0, tiled=True),
        lax.all_gather(value_loc, "tile", axis=0, tiled=True),
    )
    everyone = keys_all.shape[0]
    block = math.gcd(everyone, 2048)
    steps_total = everyone // block

    def stats_step(index, carry):
        top, summed = carry
        scores = score_block(query, lax.dynamic_slice_in_dim(keys_all, index * block, block, 0))
        new_top = jnp.maximum(top, jnp.max(scores, axis=2))
        summed = summed * jnp.exp(top - new_top) + jnp.sum(
            jnp.exp(scores - new_top[:, :, None]), axis=2
        )
        return (new_top, summed)

    start_top = jnp.full((HEADS, local), -jnp.inf, jnp.float32)
    top, summed = lax.fori_loop(
        0, steps_total, stats_step, (start_top, jnp.zeros((HEADS, local), jnp.float32))
    )
    lse = top + jnp.log(summed)

    def value_step(index, acc):
        scores = score_block(query, lax.dynamic_slice_in_dim(keys_all, index * block, block, 0))
        weights = jnp.exp(scores - lse[:, :, None]).astype(jnp.bfloat16)
        v_part = head_view(lax.dynamic_slice_in_dim(values_all, index * block, block, 0))
        return acc + jnp.einsum("hqk,khd->qhd", weights, v_part, preferred_element_type=jnp.float32)

    mixed = lax.fori_loop(0, steps_total, value_step, jnp.zeros((local, HEADS, HDIM), jnp.float32))
    attended = mixed.reshape(local, HD).astype(jnp.bfloat16)
    block_out = (
        hidden.astype(jnp.float32) + jnp.dot(attended, o_weight, preferred_element_type=jnp.float32)
    ).astype(jnp.bfloat16)
    dattended = dot_back(upstream, o_weight).astype(jnp.bfloat16)
    product = dattended.astype(jnp.float32) * attended.astype(jnp.float32)
    delta = jnp.sum(product.reshape(local, HEADS, HDIM), axis=2).T

    def query_step(index, acc):
        k_part = lax.dynamic_slice_in_dim(keys_all, index * block, block, 0)
        v_part = lax.dynamic_slice_in_dim(values_all, index * block, block, 0)
        prob = jnp.exp(score_block(query, k_part) - lse[:, :, None])
        dprob = jnp.einsum(
            "qhd,khd->hqk",
            head_view(dattended),
            head_view(v_part),
            preferred_element_type=jnp.float32,
        )
        dscore = (prob * (dprob - delta[:, :, None]) * scale).astype(jnp.bfloat16)
        return acc + jnp.einsum(
            "hqk,khd->qhd", dscore, head_view(k_part), preferred_element_type=jnp.float32
        )

    dq_acc = lax.fori_loop(0, steps_total, query_step, jnp.zeros((local, HEADS, HDIM), jnp.float32))
    dquery = dq_acc.reshape(local, HD).astype(jnp.bfloat16)
    lse_all, delta_all = (
        lax.all_gather(lse.T, "tile", axis=0, tiled=True),
        lax.all_gather(delta.T, "tile", axis=0, tiled=True),
    )
    empty = jnp.zeros((local, HEADS, HDIM), jnp.float32)
    q_in = lax.all_gather(query, "tile", axis=0, tiled=True)
    d_in = lax.all_gather(dattended, "tile", axis=0, tiled=True)
    incoming = q_in.shape[0]
    sub = math.gcd(incoming, 2048)

    def inner(index, acc):
        dk_acc, dv_acc = acc
        at = index * sub
        q_part = lax.dynamic_slice_in_dim(q_in, at, sub, 0)
        d_part = lax.dynamic_slice_in_dim(d_in, at, sub, 0)
        l_part = lax.dynamic_slice_in_dim(lse_all, at, sub, 0).T
        e_part = lax.dynamic_slice_in_dim(delta_all, at, sub, 0).T
        prob = jnp.exp(score_block(q_part, key_loc) - l_part[:, :, None])
        dv_acc = dv_acc + jnp.einsum(
            "hqk,qhd->khd",
            prob.astype(jnp.bfloat16),
            head_view(d_part),
            preferred_element_type=jnp.float32,
        )
        dprob = jnp.einsum(
            "qhd,khd->hqk",
            head_view(d_part),
            head_view(value_loc),
            preferred_element_type=jnp.float32,
        )
        dscore = (prob * (dprob - e_part[:, :, None]) * scale).astype(jnp.bfloat16)
        dk_acc = dk_acc + jnp.einsum(
            "hqk,qhd->khd", dscore, head_view(q_part), preferred_element_type=jnp.float32
        )
        return (dk_acc, dv_acc)

    dk_acc, dv_acc = lax.fori_loop(0, incoming // sub, inner, (empty, empty))
    dkeys = dk_acc.reshape(local, HD).astype(jnp.bfloat16)
    dvalues = dv_acc.reshape(local, HD).astype(jnp.bfloat16)
    dhidden = upstream.astype(jnp.float32)
    dhidden = dhidden + dot_back(dquery, qk_weight[0])
    dhidden = dhidden + dot_back(dkeys, qk_weight[1])
    dhidden = dhidden + dot_back(dvalues, v_weight)
    dhidden = dhidden.astype(jnp.bfloat16)
    kernel_rows = []
    dpadded = jnp.zeros((2 * rows + 1, 2 * cols + 1, chans), jnp.float32)
    for a in range(3):
        row_list = []
        for b in range(3):
            row_list.append(dot_over(taps[3 * a + b], dhidden))
            back = dot_back(dhidden, conv_weight[a, b])
            dpadded = dpadded.at[a : a + 2 * rows : 2, b : b + 2 * cols : 2].add(
                back.reshape(rows, cols, chans)
            )
        kernel_rows.append(jnp.stack(row_list))
    kernel_local = jnp.stack(kernel_rows)
    grad_conv = lax.psum(kernel_local, "tile") * (1.0 / math.sqrt(everyone))
    below = shifted(dpadded[0:1, 1:].astype(jnp.bfloat16), "tile", -1).astype(jnp.float32)
    grad_fine = dpadded[1:, 1:]
    grad_fine = grad_fine.at[-1:].add(below)
    return (block_out, grad_conv, grad_fine.astype(jnp.bfloat16))


NT = (((1,), (1,)), ((), ()))
NN = (((1,), (0,)), ((), ()))


def mm(left, right, dims=NN):
    return lax.dot_general(left, right, dims, preferred_element_type=jnp.float32)


def two_heads(mat):
    lane = lax.broadcasted_iota(jnp.int32, mat.shape, 1)
    zero = jnp.zeros_like(mat)
    return jnp.concatenate(
        [jnp.where(lane < HDIM, mat, zero), jnp.where(lane < HDIM, zero, mat)], axis=0
    )


def pick_heads(mat):
    half = mat.shape[0] // 2
    lane = lax.broadcasted_iota(jnp.int32, (half, mat.shape[1]), 1)
    return jnp.where(lane < HDIM, mat[:half], mat[half:])


class Gather:
    def __init__(self, view, place, middle, send, recv, slot, relayed=False):
        self.view, self.place, self.send, self.recv, self.slot = view, place, send, recv, slot
        self.middle, self.relayed = middle, relayed
        self.copies = []
        self.middle_copies = []

    def copy(self, index, block, target):
        return pltpu.make_async_remote_copy(
            src_ref=self.view(block),
            dst_ref=self.view(block),
            send_sem=self.send.at[self.slot, index],
            recv_sem=self.recv.at[self.slot, index],
            device_id={"tile": target},
            device_id_type=pl.DeviceIdType.MESH,
        )

    def go(self, index, block, target):
        made = self.copy(index, block, target)
        made.start()
        self.copies.append(made)

    def go_middle(self, index, out, block, target):
        made = pltpu.make_async_remote_copy(
            src_ref=self.view(block),
            dst_ref=self.view(block),
            send_sem=self.send.at[self.slot, out],
            recv_sem=self.recv.at[self.slot, index],
            device_id={"tile": target},
            device_id_type=pl.DeviceIdType.MESH,
        )

        @pl.when(self.middle)
        def _():
            made.start()

        self.middle_copies.append(made)

    def landed(self, index, block):
        self.copy(index, block, self.place(0, 0, 1)).wait_recv()

    def own_z(self, *which):
        block = self.place(0, 0, 0)
        for k in which or (1, 2, 3):
            if k == 3 and self.relayed:
                self.go_middle(3, 3, block, self.place(3, 0, 0))
            else:
                self.go(k, block, self.place(k, 0, 0))

    def own_core(self):
        self.go(8, self.place(0, 0, 0), self.place(0, 0, 1))

    def own_x(self):
        self.go(4, self.place(0, 0, 0), self.place(0, 1, 0))
        self.own_core()

    def own_diagonal(self, *which):
        for k in which or (1, 2, 3):
            self.go(4 + k, self.place(0, 0, 0), self.place(k, 1, 0))

    def own(self):
        self.own_z()
        self.own_x()

    def across(self, *which, wide=True):
        for k in which or ((2, 1, 3) if self.relayed else (1, 2, 3)):
            block = self.place(k, 0, 0)
            self.landed(k, block)
            if k == 2 and self.relayed:
                self.go_middle(3, 0, block, self.place(1, 0, 0))
            if wide:
                self.go(4 + k, block, self.place(0, 1, 0))
            self.go(8 + k, block, self.place(0, 0, 1))

    def over(self, *which):
        for k in which or (0, 1, 2, 3):
            block = self.place(k, 1, 0)
            self.landed(4 + k, block)
            self.go(12 + k, block, self.place(0, 0, 1))

    def finish_column(self, *which):
        for k in which or (0, 1, 2, 3):
            self.landed(8 + k, self.place(k, 0, 1))

    def finish_other(self, *which):
        for k in which or (0, 1, 2, 3):
            self.landed(12 + k, self.place(k, 1, 1))

    def drain(self):
        for made in self.copies:
            made.wait_send()
        for made in self.middle_copies:

            @pl.when(self.middle)
            def _(made=made):
                made.wait_send()


def fused_kernel(
    peers,
    fine_hbm,
    conv_hbm,
    qk_hbm,
    vw_hbm,
    ow_hbm,
    up_hbm,
    block_res,
    grad_conv_res,
    grad_fine_res,
    strips_res,
    fine,
    conv,
    qk,
    vw,
    ow,
    up,
    block_out,
    grad_conv,
    grad_fine,
    in_sem,
    out_sem,
    above,
    hid_all,
    kv_all,
    q_all,
    d_all,
    dh_all,
    mid_t,
    low_t,
    stats,
    exp_buf,
    st_buf,
    dpt_buf,
    kv_w,
    acc,
    send,
    recv,
    stat_send,
    stat_recv,
    halo_send,
    halo_recv,
    strip_sum,
    strip_out,
    strip_in,
    fin_all,
    scores,
    dp_buf,
):
    me = lax.axis_index("tile")
    n = up.shape[0]
    chans = up.shape[1]
    full = n * peers
    pair = 2 * n
    lower = lax.rem(me + 1, peers)
    core = lax.rem(me, 2)
    col = lax.rem(lax.div(me, 2), 2)
    level = lax.div(me, 4)
    middle = lax.rem(level + 1, 4) >= 2
    levels = (level, level + 1 - 2 * lax.rem(level, 2), lax.rem(level + 2, 4), 3 - level)

    def place(k, flip_x, flip_core):
        x = 1 - col if flip_x else col
        c = 1 - core if flip_core else core
        return levels[k] * 4 + x * 2 + c

    def chip(k, flip_x):
        return levels[k] * 4 + (1 - col if flip_x else col) * 2

    barrier = pltpu.get_barrier_semaphore()
    for step in range(1, peers):
        pl.semaphore_signal(
            barrier,
            inc=1,
            device_id={"tile": lax.rem(me + step, peers)},
            device_id_type=pl.DeviceIdType.MESH,
        )
    moves = (
        (up_hbm, up), (ow_hbm, ow), (fine_hbm, fine), (conv_hbm, conv), (qk_hbm, qk), (vw_hbm, vw)
    )
    loads = [pltpu.make_async_copy(a, b, in_sem.at[i]) for i, (a, b) in enumerate(moves)]
    for load in loads:
        load.start()
    stores = []

    def store(source, target):
        made = pltpu.make_async_copy(source, target, out_sem.at[len(stores)])
        made.start()
        stores.append(made)

    def rows(ref):
        return lambda t: ref.at[pl.ds(pl.multiple_of(t * n, n), n), :]

    def cols(ref, part, shift):
        lines = pl.ds(part * chans, chans)
        return lambda t: ref.at[t + shift, lines, :]

    def both(t):
        return pl.ds(pl.multiple_of(t * n, pair), pair)

    mine = pl.ds(pl.multiple_of(me * n, n), n)
    halo = pltpu.make_async_remote_copy(
        src_ref=fine_hbm.at[1],
        dst_ref=above,
        send_sem=halo_send,
        recv_sem=halo_recv,
        device_id={"tile": lower},
        device_id_type=pl.DeviceIdType.MESH,
    )
    pl.semaphore_wait(barrier, peers - 1)
    halo.start()
    views = (cols(low_t, 1, 1), cols(low_t, 0, 1))
    parts = [Gather(view, place, middle, send, recv, i, True) for i, view in enumerate(views)]
    mid_gather = Gather(lambda t: mid_t.at[t], place, middle, send, recv, 2)
    fin_gather = Gather(lambda t: fin_all.at[t], place, middle, send, recv, 3)
    hid_gather = Gather(rows(hid_all), place, middle, send, recv, 4)
    d_gather = Gather(rows(d_all), place, middle, send, recv, 5)
    dh_gather = Gather(rows(dh_all), place, middle, send, recv, 6)

    loads[0].wait()
    loads[1].wait()
    dattended = mm(up[...], ow[...], NT).astype(jnp.bfloat16)
    d_all[mine, :] = dattended
    d_gather.own()

    line = lax.broadcasted_iota(jnp.int32, (2 * n, 2 * n), 0)
    cell = lax.broadcasted_iota(jnp.int32, (2 * n, 2 * n), 1)
    wanted = jnp.where(line < n, 2 * line, 2 * (line - n) + 1)
    order = jnp.where(cell == wanted, 1.0, 0.0).astype(jnp.bfloat16)

    def apart(row):
        sorted_row = mm(order, row).astype(jnp.bfloat16)
        return sorted_row[:n], sorted_row[n:]

    loads[2].wait()
    mid_even, mid_odd = apart(fine[0])
    low_even, low_odd = apart(fine[1])
    mid_t[me, :chans, :] = mid_even.T

    for load in loads[3:]:
        load.wait()
    mid_t[me, chans:, :] = mid_odd.T
    low_t[me + 1, :chans, :] = low_even.T
    low_t[me + 1, chans:, :] = low_odd.T
    mid_gather.own_x()
    for part in parts:
        part.own_x()
    low_t[0] = jnp.zeros_like(low_t[0])
    kv_w[:, :HD] = qk[1]
    kv_w[:, HD:] = vw[...]

    def conv_row(a, even, odd):
        return mm(even, conv[a, 1]) + mm(odd, conv[a, 2]), mm(odd, conv[a, 0])

    mid, mid_late = conv_row(1, mid_even, mid_odd)
    low, low_late = conv_row(2, low_even, low_odd)
    halo.wait_recv()
    top_even, top_odd = apart(jnp.where(me == 0, jnp.zeros_like(above[...]), above[...]))
    top, top_late = conv_row(0, top_even, top_odd)
    late = top_late + mid_late + low_late
    row_at = lax.broadcasted_iota(jnp.int32, (n, chans), 0)
    late = jnp.where(row_at == 0, 0.0, pltpu.roll(late, 1, 0))
    hidden = (top + mid + low + late).astype(jnp.bfloat16)
    hid_all[mine, :] = hidden
    hid_gather.own()

    def scaled_query(mat):
        full_query = mm(mat, qk[0]).astype(jnp.bfloat16)
        return (full_query.astype(jnp.float32) * HDIM**-0.5).astype(jnp.bfloat16)

    key_value = mm(hidden, kv_w[...]).astype(jnp.bfloat16)
    q2 = two_heads(scaled_query(hidden))
    d2 = two_heads(dattended)

    def project(k, flip_x):
        span = both(chip(k, flip_x))
        kv_all[span, :] = mm(hid_all[span, :], kv_w[...]).astype(jnp.bfloat16)

    def attend(flip_x, which):
        first = 4 * flip_x + which[0]
        lanes = slice(first * pair, (first + len(which)) * pair)
        for i, k in enumerate(which):
            keys = kv_all[both(chip(k, flip_x)), :HD]
            scores[:, i * pair : (i + 1) * pair] = mm(q2, keys, NT)
        block = scores[:, : len(which) * pair]
        high = jnp.max(block, axis=1, keepdims=True)
        expd = jnp.exp(block - high)
        exp_buf[:, lanes] = expd
        total = jnp.sum(expd, axis=1, keepdims=True)
        mixed = jnp.zeros((pair, HD), jnp.float32)
        for i, k in enumerate(which):
            weights = expd[:, i * pair : (i + 1) * pair].astype(jnp.bfloat16)
            mixed = mixed + mm(weights, kv_all[both(chip(k, flip_x)), HD:])
        groups.append((high, total, mixed, len(which)))

    groups = []
    k2 = two_heads(key_value[:, :HD])
    v2 = two_heads(key_value[:, HD:])

    def prepare_queries(flip_x):
        for k in range(4):
            j = 4 * flip_x + k
            span = both(chip(k, flip_x))
            queries = scaled_query(hid_all[span, :])
            q_all[span, :] = queries
            st_buf[:, j * pair : (j + 1) * pair] = mm(k2, queries, NT)

    def prepare_grads(flip_x):
        for k in range(4):
            j = 4 * flip_x + k
            dpt_buf[:, j * pair : (j + 1) * pair] = mm(v2, d_all[both(chip(k, flip_x)), :], NT)

    def prepare_probs(flip_x):
        for k in range(4):
            j = 4 * flip_x + k
            dp_buf[:, j * pair : (j + 1) * pair] = mm(d2, kv_all[both(chip(k, flip_x)), HD:], NT)

    d_gather.across()

    hid_gather.across()
    parts[0].own_z(2, 1)
    parts[1].own_z(2, 1)
    mid_gather.over(0)
    d_gather.over()
    hid_gather.over(0)
    hid_gather.finish_column()
    for k in range(4):
        project(k, 0)
    attend(0, (0, 1, 2, 3))
    parts[0].own_z(3)
    parts[1].own_z(3)
    hid_gather.over(1)

    prepare_queries(0)
    hid_gather.over(2)

    d_gather.finish_column()
    d_gather.finish_other()
    prepare_grads(0)
    prepare_probs(0)
    hid_gather.over(3)
    parts[0].across(2, 1)
    prepare_grads(1)
    hid_gather.finish_other()
    for k in range(4):
        project(k, 1)

    attend(1, (0, 1, 2, 3))
    high = functools.reduce(jnp.maximum, [g[0] for g in groups])
    shares = [jnp.exp(g[0] - high) for g in groups]
    total = sum(g[1] * share for g, share in zip(groups, shares))
    lse = high + jnp.log(total)
    inverse = 1.0 / total
    shares = [share * inverse for share in shares]
    attended = pick_heads(sum(g[2] * share for g, share in zip(groups, shares)))
    attended = attended.astype(jnp.bfloat16)
    factors = [share for g, share in zip(groups, shares) for _ in range(g[3])]
    product = dattended.astype(jnp.float32) * attended.astype(jnp.float32)
    delta = jnp.sum(two_heads(product), axis=1, keepdims=True)
    lane = lax.broadcasted_iota(jnp.int32, (2 * n, 128), 1)
    packed = jnp.where(lane == 0, lse, jnp.where(lane == 1, delta, 0.0)).T
    stats[me] = packed[:2]
    stat_copies = []
    for step in range(1, peers):
        made = pltpu.make_async_remote_copy(
            src_ref=stats.at[me],
            dst_ref=stats.at[me],
            send_sem=stat_send.at[step],
            recv_sem=stat_recv.at[step],
            device_id={"tile": lax.rem(me + step, peers)},
            device_id_type=pl.DeviceIdType.MESH,
        )
        made.start()
        stat_copies.append(made)
    parts[0].across(3)
    parts[1].across(2, 1)
    block_out[...] = (hidden.astype(jnp.float32) + mm(attended, ow[...])).astype(jnp.bfloat16)
    store(block_out, block_res)
    prepare_queries(1)
    prepare_probs(1)
    dquery = jnp.zeros((pair, HD), jnp.float32)
    for flip_x in (0, 1):
        for k in range(4):
            j = 4 * flip_x + k
            span = both(chip(k, flip_x))
            prob = exp_buf[:, j * pair : (j + 1) * pair] * factors[j]
            dprob = dp_buf[:, j * pair : (j + 1) * pair]
            dscore = (prob * (dprob - delta)).astype(jnp.bfloat16)
            dquery = dquery + mm(dscore, kv_all[span, :HD])
    dquery = (pick_heads(dquery) * HDIM**-0.5).astype(jnp.bfloat16)
    grad_h = up[...].astype(jnp.float32) + mm(dquery, qk[0], NT)


    for step in range(1, peers):
        block = lax.rem(me - step + peers, peers)
        pltpu.make_async_remote_copy(
            src_ref=stats.at[block],
            dst_ref=stats.at[block],
            send_sem=stat_send.at[step],
            recv_sem=stat_recv.at[step],
            device_id={"tile": lower},
            device_id_type=pl.DeviceIdType.MESH,
        ).wait_recv()
    dk = jnp.zeros((2 * n, HD), jnp.float32)
    dv = jnp.zeros((2 * n, HD), jnp.float32)
    for flip_x in (0, 1):
        for k in range(4):
            j = 4 * flip_x + k
            at = chip(k, flip_x)
            span = both(at)

            def stat_rows(kind):
                heads = []
                for h in range(HEADS):
                    lines = [stats[at + c, kind : kind + 1, h * n : (h + 1) * n] for c in (0, 1)]
                    heads.append(jnp.broadcast_to(jnp.concatenate(lines, axis=1), (n, pair)))
                return jnp.concatenate(heads, axis=0)

            lanes = slice(j * pair, (j + 1) * pair)
            prob_t = jnp.exp(st_buf[:, lanes] - stat_rows(0))
            dscore_t = (prob_t * (dpt_buf[:, lanes] - stat_rows(1))).astype(jnp.bfloat16)
            dv = dv + mm(prob_t.astype(jnp.bfloat16), d_all[span, :])
            dk = dk + mm(dscore_t, q_all[span, :])
    dkeys = pick_heads(dk).astype(jnp.bfloat16)
    dvalues = pick_heads(dv).astype(jnp.bfloat16)
    grad_h = grad_h + mm(dkeys, qk[1], NT) + mm(dvalues, vw[...], NT)
    dhidden = grad_h.astype(jnp.bfloat16)
    dh_all[mine, :] = dhidden
    dh_gather.own()


    def back_row(a, grads):
        even = mm(grads, conv[a, 1], NT)
        later = mm(grads, conv[a, 0], NT)
        later = jnp.where(row_at == n - 1, 0.0, pltpu.roll(later, n - 1, 0))
        return even, mm(grads, conv[a, 2], NT) + later

    even_mid, odd_mid = back_row(1, dhidden)
    grad_fine[0, :, :chans] = even_mid.astype(jnp.bfloat16)
    grad_fine[0, :, chans:] = odd_mid.astype(jnp.bfloat16)
    even_low, odd_low = back_row(2, dhidden)
    norm = 1.0 / math.sqrt(full)
    pair_at = lax.broadcasted_iota(jnp.int32, (pair, chans), 0)
    edge = jnp.logical_or(pair_at == n - 1, pair_at == pair - 1)

    def kernel_grads(flip_x, which, last, first):
        straight = []
        moved = []
        for k in which:
            block = dh_all[both(chip(k, flip_x)), :]
            rolled = pltpu.roll(block.astype(jnp.float32), pair - 1, 0)
            straight.append(block)
            moved.append(jnp.where(edge, 0.0, rolled).astype(jnp.bfloat16))
        straight = jnp.concatenate(straight, axis=0)
        moved = jnp.concatenate(moved, axis=0)

        def features(part, shift):
            picks = []
            for k in which:
                at = chip(k, flip_x) + shift
                picks.append(low_t[at, part * chans : (part + 1) * chans, :])
                picks.append(low_t[at + 1, part * chans : (part + 1) * chans, :])
            return jnp.concatenate(picks, axis=1)

        for a, shift in ((2, 1), (0, 0)):
            for b in (1, 2, 0):
                part = mm(features(0 if b == 1 else 1, shift), straight if b else moved)
                slot = 3 * (a // 2) + b
                if not first:
                    part = part + acc[slot]
                if last:
                    grad_conv[slot] = part * norm
                    store(grad_conv.at[slot], grad_conv_res.at[slot])
                else:
                    acc[slot] = part

    strip = chans // 4
    slim = strip // 4
    strip_at = pl.multiple_of((col * 2 + core) * strip, strip)
    strip_copies = []

    def strip_copy(k, target_level):
        return pltpu.make_async_remote_copy(
            src_ref=strip_out.at[target_level],
            dst_ref=strip_in.at[level],
            send_sem=stat_send.at[peers + k],
            recv_sem=stat_recv.at[peers + k],
            device_id={"tile": place(k, 0, 0)},
            device_id_type=pl.DeviceIdType.MESH,
        )

    def strips():
        at = level * 4
        block = dh_all[pl.ds(pl.multiple_of(at * n, 4 * n), 4 * n), :]
        block_row = lax.broadcasted_iota(jnp.int32, block.shape, 0)
        rolled = pltpu.roll(block.astype(jnp.float32), 4 * n - 1, 0)
        rolled = jnp.where(lax.rem(block_row, n) == n - 1, 0.0, rolled).astype(jnp.bfloat16)
        for b, part, grads in ((0, 1, rolled), (1, 0, block), (2, 1, block)):
            lines = pl.ds(pl.multiple_of(part * chans + strip_at, strip), strip)
            picks = jnp.concatenate([mid_t[at + i, lines, :] for i in range(4)], axis=1)
            sums = mm(picks, grads)
            for i in range(4):
                piece = sums[i * slim : (i + 1) * slim]
                strip_sum[i, b * slim : (b + 1) * slim, :] = piece
                strip_out[i, b * slim : (b + 1) * slim, :] = piece.astype(jnp.bfloat16)
        for k in (2, 3, 1):
            made = strip_copy(k, levels[k])
            made.start()
            strip_copies.append(made)

    def strips_sum():
        total = strip_sum[level]
        for k in (1, 2, 3):
            strip_copy(k, levels[k]).wait_recv()
        for k in (1, 2, 3):
            total = total + strip_in[levels[k]].astype(jnp.float32)
        fin_all[me] = (total * norm).astype(jnp.bfloat16)

    def strips_end():
        store(fin_all, strips_res)

    parts[1].across(3)
    dh_gather.across(1)
    dh_gather.over(0)

    dh_gather.finish_column(0)
    dh_gather.finish_other(0)
    mid_gather.finish_column(0)
    mid_gather.finish_other(0)
    strips()

    dh_gather.across(2, 3)

    for part in parts:
        part.over()
    dh_gather.over(1)
    dh_gather.finish_column(1, 2, 3)
    for part in parts:
        part.finish_column()
        part.finish_other()
    kernel_grads(0, (0, 1, 2, 3), False, True)
    dh_gather.over(2)
    strips_sum()
    fin_gather.own()
    fin_gather.own_diagonal()
    dh_gather.finish_other(1, 2)
    kernel_grads(1, (0, 1, 2), False, False)
    dh_gather.over(3)
    dh_gather.finish_other(3)
    kernel_grads(1, (3,), True, False)
    fin_gather.across(wide=False)

    below = dh_all[pl.ds(pl.multiple_of(lower * n, n), n), :]
    below = jnp.where(me == peers - 1, jnp.zeros_like(below), below)
    even_top, odd_top = back_row(0, below)
    grad_fine[1, :, :chans] = (even_low + even_top).astype(jnp.bfloat16)
    grad_fine[1, :, chans:] = (odd_low + odd_top).astype(jnp.bfloat16)
    store(grad_fine, grad_fine_res)

    fin_gather.over()
    fin_gather.finish_column()
    fin_gather.finish_other()
    strips_end()
    for made in strip_copies:
        made.wait_send()
    halo.wait_send()
    for gather in (*parts, mid_gather, fin_gather, hid_gather, d_gather, dh_gather):
        gather.drain()
    for made in stat_copies:
        made.wait_send()
    for made in stores:
        made.wait()


def emit_kernel(
    block_in, taps_in, fine_in, strips_in, block_out, taps_out, fine_out, gathered, middle_taps, sem
):
    moves = [pltpu.make_async_copy(strips_in, gathered, sem.at[12])]
    for i in range(6):
        moves.append(pltpu.make_async_copy(taps_in.at[i], taps_out.at[i + i // 3 * 3], sem.at[i]))
    moves.append(pltpu.make_async_copy(block_in, block_out, sem.at[6]))
    for i in range(2):
        moves.append(pltpu.make_async_copy(fine_in.at[i], fine_out.at[i], sem.at[7 + i]))
    for move in moves:
        move.start()
    moves[0].wait()
    slim = gathered.shape[1] // 3
    for b in range(3):
        for i in range(4):
            for r in range(4):
                at = (4 * r + i) * slim
                piece = gathered[i * 4 + r, b * slim : (b + 1) * slim, :]
                middle_taps[b, at : at + slim, :] = piece.astype(jnp.float32)
        move = pltpu.make_async_copy(middle_taps.at[b], taps_out.at[3 + b], sem.at[9 + b])
        move.start()
        moves.append(move)
    for move in moves[1:]:
        move.wait()


def emit(block_out, taps, fine, strips):
    where = pl.BlockSpec(memory_space=pl.ANY)
    chans = taps.shape[1]
    return pl.pallas_call(
        emit_kernel,
        out_shape=(
            jax.ShapeDtypeStruct(block_out.shape, block_out.dtype),
            jax.ShapeDtypeStruct((9, chans, chans), taps.dtype),
            jax.ShapeDtypeStruct(fine.shape, fine.dtype),
        ),
        in_specs=[where] * 4,
        out_specs=(where,) * 3,
        scratch_shapes=[
            pltpu.VMEM(strips.shape, strips.dtype),
            pltpu.VMEM((3, chans, chans), taps.dtype),
            pltpu.SemaphoreType.DMA((16,)),
        ],
        compiler_params=pltpu.CompilerParams(vmem_limit_bytes=4 * 2**20),
    )(block_out, taps, fine, strips)


def fused_body(fine, conv_weight, qk_weight, v_weight, o_weight, upstream):
    peers = lax.axis_size("tile")
    n, chans = upstream.shape
    full = n * peers
    hbm = pl.BlockSpec(memory_space=pltpu.HBM)
    free = pl.BlockSpec(memory_space=pl.ANY)
    dma = pltpu.SemaphoreType.DMA
    low = jnp.bfloat16
    sources = (fine, conv_weight, qk_weight, v_weight, o_weight, upstream)
    block_out, taps, grad_fine, strips = pl.pallas_call(
        functools.partial(fused_kernel, peers),
        out_shape=(
            jax.ShapeDtypeStruct((n, chans), low),
            jax.ShapeDtypeStruct((6, chans, chans), jnp.float32),
            jax.ShapeDtypeStruct((2, n, 2 * chans), low),
            jax.ShapeDtypeStruct((peers, 3 * chans // 16, chans), low),
        ),
        in_specs=[hbm] * 6,
        out_specs=(free,) * 4,
        scratch_shapes=[
            pltpu.VMEM(fine.shape, low),
            pltpu.VMEM(conv_weight.shape, low),
            pltpu.VMEM(qk_weight.shape, low),
            pltpu.VMEM(v_weight.shape, low),
            pltpu.VMEM(o_weight.shape, low),
            pltpu.VMEM(upstream.shape, low),
            pltpu.VMEM((n, chans), low),
            pltpu.VMEM((6, chans, chans), jnp.float32),
            pltpu.VMEM((2, n, 2 * chans), low),
            dma((6,)),
            dma((11,)),
            pltpu.VMEM((2 * n, chans), low),
            pltpu.VMEM((full, chans), low),
            pltpu.VMEM((full, 2 * HD), low),
            pltpu.VMEM((full, HD), low),
            pltpu.VMEM((full, HD), low),
            pltpu.VMEM((full, chans), low),
            pltpu.VMEM((peers, 2 * chans, n), low),
            pltpu.VMEM((peers + 1, 2 * chans, n), low),
            pltpu.VMEM((peers, 2, 2 * n), jnp.float32),
            pltpu.VMEM((2 * n, full), jnp.float32),
            pltpu.VMEM((2 * n, full), jnp.float32),
            pltpu.VMEM((2 * n, full), jnp.float32),
            pltpu.VMEM((chans, 2 * HD), low),
            pltpu.VMEM((6, chans, chans), jnp.float32),
            dma((7, 16)),
            dma((7, 16)),
            dma((peers + 4,)),
            dma((peers + 4,)),
            dma,
            dma,
            pltpu.VMEM((4, 3 * chans // 16, chans), jnp.float32),
            pltpu.VMEM((4, 3 * chans // 16, chans), low),
            pltpu.VMEM((4, 3 * chans // 16, chans), low),
            pltpu.VMEM((peers, 3 * chans // 16, chans), low),
            pltpu.VMEM((2 * n, full // 2), jnp.float32),
            pltpu.VMEM((2 * n, full), jnp.float32),
        ],
        compiler_params=pltpu.CompilerParams(
            collective_id=0, has_side_effects=True, vmem_limit_bytes=36 * 2**20
        ),
    )(*[pltpu.with_memory_space_constraint(v, pltpu.HBM) for v in sources])
    results = emit(block_out, taps, grad_fine.reshape(fine.shape), strips)
    block_out, grad_conv, grad_fine = results
    return block_out, grad_conv.reshape(3, 3, chans, chans), grad_fine


def solution(mesh):
    def whole(fine, *rest):
        devices = mesh.shape["groups"] * mesh.shape["tile"]
        one_row = fine.shape[0] == 2 * devices and fine.shape[1] == 256 and fine.shape[2] == 256
        fits = mesh.shape["tile"] == 16
        return jax.shard_map(
            fused_body if one_row and fits else body,
            mesh=mesh,
            in_specs=(
                P(("groups", "tile"), None, None),
                P(),
                P(),
                P(),
                P(),
                P(("groups", "tile"), None),
            ),
            out_specs=(
                P(("groups", "tile"), None),
                P("groups", None, None, None),
                P(("groups", "tile"), None, None),
            ),
            check_vma=False,
        )(fine, *rest)

    return whole
```

```python
import functools
import math

import jax
import jax.numpy as jnp
from jax import lax
from jax.experimental import pallas as pl
from jax.experimental.pallas import tpu as pltpu
from jax.sharding import PartitionSpec as P

HEADS = 2
HDIM = 64
HD = 128


def shifted(x, axis, by):
    peers = lax.axis_size(axis)
    pairs = [(i, i + by) for i in range(peers) if 0 <= i + by < peers]
    return lax.ppermute(x, axis, pairs)


def head_view(mat):
    return mat.reshape(mat.shape[0], HEADS, HDIM)


def score_block(queries, keys):
    product = jnp.einsum(
        "qhd,khd->hqk", head_view(queries), head_view(keys), preferred_element_type=jnp.float32
    )
    return product * HDIM ** (-0.5)


def dot_back(left, right):
    return lax.dot_general(
        left, right, (((1,), (1,)), ((), ())), preferred_element_type=jnp.float32
    )


def dot_over(left, right):
    return lax.dot_general(
        left, right, (((0,), (0,)), ((), ())), preferred_element_type=jnp.float32
    )


def body(fine, conv_weight, qk_weight, v_weight, o_weight, upstream):
    rows = fine.shape[0] // 2
    cols = fine.shape[1] // 2
    chans = fine.shape[2]
    local = rows * cols
    scale = HDIM ** (-0.5)
    above = shifted(fine[-1:], "tile", 1)
    padded = jnp.pad(jnp.concatenate([above, fine], axis=0), ((0, 0), (1, 0), (0, 0)))
    taps = []
    total = jnp.zeros((local, chans), jnp.float32)
    for a in range(3):
        for b in range(3):
            tap = padded[a : a + 2 * rows : 2, b : b + 2 * cols : 2].reshape(local, chans)
            taps.append(tap)
            total = total + jnp.dot(tap, conv_weight[a, b], preferred_element_type=jnp.float32)
    hidden = total.astype(jnp.bfloat16)
    query = jnp.dot(hidden, qk_weight[0], preferred_element_type=jnp.float32).astype(jnp.bfloat16)
    key_loc = jnp.dot(hidden, qk_weight[1], preferred_element_type=jnp.float32).astype(jnp.bfloat16)
    value_loc = jnp.dot(hidden, v_weight, preferred_element_type=jnp.float32).astype(jnp.bfloat16)
    keys_all, values_all = (
        lax.all_gather(key_loc, "tile", axis=0, tiled=True),
        lax.all_gather(value_loc, "tile", axis=0, tiled=True),
    )
    everyone = keys_all.shape[0]
    block = math.gcd(everyone, 2048)
    steps_total = everyone // block

    def stats_step(index, carry):
        top, summed = carry
        scores = score_block(query, lax.dynamic_slice_in_dim(keys_all, index * block, block, 0))
        new_top = jnp.maximum(top, jnp.max(scores, axis=2))
        summed = summed * jnp.exp(top - new_top) + jnp.sum(
            jnp.exp(scores - new_top[:, :, None]), axis=2
        )
        return (new_top, summed)

    start_top = jnp.full((HEADS, local), -jnp.inf, jnp.float32)
    top, summed = lax.fori_loop(
        0, steps_total, stats_step, (start_top, jnp.zeros((HEADS, local), jnp.float32))
    )
    lse = top + jnp.log(summed)

    def value_step(index, acc):
        scores = score_block(query, lax.dynamic_slice_in_dim(keys_all, index * block, block, 0))
        weights = jnp.exp(scores - lse[:, :, None]).astype(jnp.bfloat16)
        v_part = head_view(lax.dynamic_slice_in_dim(values_all, index * block, block, 0))
        return acc + jnp.einsum("hqk,khd->qhd", weights, v_part, preferred_element_type=jnp.float32)

    mixed = lax.fori_loop(0, steps_total, value_step, jnp.zeros((local, HEADS, HDIM), jnp.float32))
    attended = mixed.reshape(local, HD).astype(jnp.bfloat16)
    block_out = (
        hidden.astype(jnp.float32) + jnp.dot(attended, o_weight, preferred_element_type=jnp.float32)
    ).astype(jnp.bfloat16)
    dattended = dot_back(upstream, o_weight).astype(jnp.bfloat16)
    product = dattended.astype(jnp.float32) * attended.astype(jnp.float32)
    delta = jnp.sum(product.reshape(local, HEADS, HDIM), axis=2).T

    def query_step(index, acc):
        k_part = lax.dynamic_slice_in_dim(keys_all, index * block, block, 0)
        v_part = lax.dynamic_slice_in_dim(values_all, index * block, block, 0)
        prob = jnp.exp(score_block(query, k_part) - lse[:, :, None])
        dprob = jnp.einsum(
            "qhd,khd->hqk",
            head_view(dattended),
            head_view(v_part),
            preferred_element_type=jnp.float32,
        )
        dscore = (prob * (dprob - delta[:, :, None]) * scale).astype(jnp.bfloat16)
        return acc + jnp.einsum(
            "hqk,khd->qhd", dscore, head_view(k_part), preferred_element_type=jnp.float32
        )

    dq_acc = lax.fori_loop(0, steps_total, query_step, jnp.zeros((local, HEADS, HDIM), jnp.float32))
    dquery = dq_acc.reshape(local, HD).astype(jnp.bfloat16)
    lse_all, delta_all = (
        lax.all_gather(lse.T, "tile", axis=0, tiled=True),
        lax.all_gather(delta.T, "tile", axis=0, tiled=True),
    )
    empty = jnp.zeros((local, HEADS, HDIM), jnp.float32)
    q_in = lax.all_gather(query, "tile", axis=0, tiled=True)
    d_in = lax.all_gather(dattended, "tile", axis=0, tiled=True)
    incoming = q_in.shape[0]
    sub = math.gcd(incoming, 2048)

    def inner(index, acc):
        dk_acc, dv_acc = acc
        at = index * sub
        q_part = lax.dynamic_slice_in_dim(q_in, at, sub, 0)
        d_part = lax.dynamic_slice_in_dim(d_in, at, sub, 0)
        l_part = lax.dynamic_slice_in_dim(lse_all, at, sub, 0).T
        e_part = lax.dynamic_slice_in_dim(delta_all, at, sub, 0).T
        prob = jnp.exp(score_block(q_part, key_loc) - l_part[:, :, None])
        dv_acc = dv_acc + jnp.einsum(
            "hqk,qhd->khd",
            prob.astype(jnp.bfloat16),
            head_view(d_part),
            preferred_element_type=jnp.float32,
        )
        dprob = jnp.einsum(
            "qhd,khd->hqk",
            head_view(d_part),
            head_view(value_loc),
            preferred_element_type=jnp.float32,
        )
        dscore = (prob * (dprob - e_part[:, :, None]) * scale).astype(jnp.bfloat16)
        dk_acc = dk_acc + jnp.einsum(
            "hqk,qhd->khd", dscore, head_view(q_part), preferred_element_type=jnp.float32
        )
        return (dk_acc, dv_acc)

    dk_acc, dv_acc = lax.fori_loop(0, incoming // sub, inner, (empty, empty))
    dkeys = dk_acc.reshape(local, HD).astype(jnp.bfloat16)
    dvalues = dv_acc.reshape(local, HD).astype(jnp.bfloat16)
    dhidden = upstream.astype(jnp.float32)
    dhidden = dhidden + dot_back(dquery, qk_weight[0])
    dhidden = dhidden + dot_back(dkeys, qk_weight[1])
    dhidden = dhidden + dot_back(dvalues, v_weight)
    dhidden = dhidden.astype(jnp.bfloat16)
    kernel_rows = []
    dpadded = jnp.zeros((2 * rows + 1, 2 * cols + 1, chans), jnp.float32)
    for a in range(3):
        row_list = []
        for b in range(3):
            row_list.append(dot_over(taps[3 * a + b], dhidden))
            back = dot_back(dhidden, conv_weight[a, b])
            dpadded = dpadded.at[a : a + 2 * rows : 2, b : b + 2 * cols : 2].add(
                back.reshape(rows, cols, chans)
            )
        kernel_rows.append(jnp.stack(row_list))
    kernel_local = jnp.stack(kernel_rows)
    grad_conv = lax.psum(kernel_local, "tile") * (1.0 / math.sqrt(everyone))
    below = shifted(dpadded[0:1, 1:].astype(jnp.bfloat16), "tile", -1).astype(jnp.float32)
    grad_fine = dpadded[1:, 1:]
    grad_fine = grad_fine.at[-1:].add(below)
    return (block_out, grad_conv, grad_fine.astype(jnp.bfloat16))


NT = (((1,), (1,)), ((), ()))
NN = (((1,), (0,)), ((), ()))


def mm(left, right, dims=NN):
    return lax.dot_general(left, right, dims, preferred_element_type=jnp.float32)


def two_heads(mat):
    lane = lax.broadcasted_iota(jnp.int32, mat.shape, 1)
    zero = jnp.zeros_like(mat)
    return jnp.concatenate(
        [jnp.where(lane < HDIM, mat, zero), jnp.where(lane < HDIM, zero, mat)], axis=0
    )


def pick_heads(mat):
    half = mat.shape[0] // 2
    lane = lax.broadcasted_iota(jnp.int32, (half, mat.shape[1]), 1)
    return jnp.where(lane < HDIM, mat[:half], mat[half:])


class Gather:
    def __init__(self, view, place, middle, send, recv, slot, relayed=False):
        self.view, self.place, self.send, self.recv, self.slot = view, place, send, recv, slot
        self.middle, self.relayed = middle, relayed
        self.copies = []
        self.middle_copies = []

    def copy(self, index, block, target):
        return pltpu.make_async_remote_copy(
            src_ref=self.view(block),
            dst_ref=self.view(block),
            send_sem=self.send.at[self.slot, index],
            recv_sem=self.recv.at[self.slot, index],
            device_id={"tile": target},
            device_id_type=pl.DeviceIdType.MESH,
        )

    def go(self, index, block, target):
        made = self.copy(index, block, target)
        made.start()
        self.copies.append(made)

    def go_middle(self, index, out, block, target):
        made = pltpu.make_async_remote_copy(
            src_ref=self.view(block),
            dst_ref=self.view(block),
            send_sem=self.send.at[self.slot, out],
            recv_sem=self.recv.at[self.slot, index],
            device_id={"tile": target},
            device_id_type=pl.DeviceIdType.MESH,
        )

        @pl.when(self.middle)
        def _():
            made.start()

        self.middle_copies.append(made)

    def landed(self, index, block):
        self.copy(index, block, self.place(0, 0, 1)).wait_recv()

    def own_z(self, *which):
        block = self.place(0, 0, 0)
        for k in which or (1, 2, 3):
            if k == 3 and self.relayed:
                self.go_middle(3, 3, block, self.place(3, 0, 0))
            else:
                self.go(k, block, self.place(k, 0, 0))

    def own_core(self):
        self.go(8, self.place(0, 0, 0), self.place(0, 0, 1))

    def own_x(self):
        self.go(4, self.place(0, 0, 0), self.place(0, 1, 0))
        self.own_core()

    def own_diagonal(self, *which):
        for k in which or (1, 2, 3):
            self.go(4 + k, self.place(0, 0, 0), self.place(k, 1, 0))

    def own(self):
        self.own_z()
        self.own_x()

    def across(self, *which, wide=True):
        for k in which or ((2, 1, 3) if self.relayed else (1, 2, 3)):
            block = self.place(k, 0, 0)
            self.landed(k, block)
            if k == 2 and self.relayed:
                self.go_middle(3, 0, block, self.place(1, 0, 0))
            if wide:
                self.go(4 + k, block, self.place(0, 1, 0))
            self.go(8 + k, block, self.place(0, 0, 1))

    def over(self, *which):
        for k in which or (0, 1, 2, 3):
            block = self.place(k, 1, 0)
            self.landed(4 + k, block)
            self.go(12 + k, block, self.place(0, 0, 1))

    def finish_column(self, *which):
        for k in which or (0, 1, 2, 3):
            self.landed(8 + k, self.place(k, 0, 1))

    def finish_other(self, *which):
        for k in which or (0, 1, 2, 3):
            self.landed(12 + k, self.place(k, 1, 1))

    def drain(self):
        for made in self.copies:
            made.wait_send()
        for made in self.middle_copies:

            @pl.when(self.middle)
            def _(made=made):
                made.wait_send()


def fused_kernel(
    peers,
    fine_hbm,
    conv_hbm,
    qk_hbm,
    vw_hbm,
    ow_hbm,
    up_hbm,
    block_res,
    grad_conv_res,
    grad_fine_res,
    strips_res,
    fine,
    conv,
    qk,
    vw,
    ow,
    up,
    block_out,
    grad_conv,
    grad_fine,
    in_sem,
    out_sem,
    above,
    hid_all,
    kv_all,
    q_all,
    d_all,
    dh_all,
    mid_t,
    low_t,
    stats,
    exp_buf,
    st_buf,
    dpt_buf,
    kv_w,
    acc,
    send,
    recv,
    stat_send,
    stat_recv,
    halo_send,
    halo_recv,
    strip_sum,
    strip_out,
    strip_in,
    fin_all,
    scores,
    dp_buf,
):
    me = lax.axis_index("tile")
    n = up.shape[0]
    chans = up.shape[1]
    full = n * peers
    pair = 2 * n
    lower = lax.rem(me + 1, peers)
    core = lax.rem(me, 2)
    col = lax.rem(lax.div(me, 2), 2)
    level = lax.div(me, 4)
    middle = lax.rem(level + 1, 4) >= 2
    levels = (level, level + 1 - 2 * lax.rem(level, 2), lax.rem(level + 2, 4), 3 - level)

    def place(k, flip_x, flip_core):
        x = 1 - col if flip_x else col
        c = 1 - core if flip_core else core
        return levels[k] * 4 + x * 2 + c

    def chip(k, flip_x):
        return levels[k] * 4 + (1 - col if flip_x else col) * 2

    barrier = pltpu.get_barrier_semaphore()
    for step in range(1, peers):
        pl.semaphore_signal(
            barrier,
            inc=1,
            device_id={"tile": lax.rem(me + step, peers)},
            device_id_type=pl.DeviceIdType.MESH,
        )
    moves = (
        (up_hbm, up), (ow_hbm, ow), (fine_hbm, fine), (conv_hbm, conv), (qk_hbm, qk), (vw_hbm, vw)
    )
    loads = [pltpu.make_async_copy(a, b, in_sem.at[i]) for i, (a, b) in enumerate(moves)]
    for load in loads:
        load.start()
    stores = []

    def store(source, target):
        made = pltpu.make_async_copy(source, target, out_sem.at[len(stores)])
        made.start()
        stores.append(made)

    def rows(ref):
        return lambda t: ref.at[pl.ds(pl.multiple_of(t * n, n), n), :]

    def cols(ref, part, shift):
        lines = pl.ds(part * chans, chans)
        return lambda t: ref.at[t + shift, lines, :]

    def both(t):
        return pl.ds(pl.multiple_of(t * n, pair), pair)

    mine = pl.ds(pl.multiple_of(me * n, n), n)
    halo = pltpu.make_async_remote_copy(
        src_ref=fine_hbm.at[1],
        dst_ref=above,
        send_sem=halo_send,
        recv_sem=halo_recv,
        device_id={"tile": lower},
        device_id_type=pl.DeviceIdType.MESH,
    )
    pl.semaphore_wait(barrier, peers - 1)
    halo.start()
    views = (cols(low_t, 1, 1), cols(low_t, 0, 1))
    parts = [Gather(view, place, middle, send, recv, i, True) for i, view in enumerate(views)]
    mid_gather = Gather(lambda t: mid_t.at[t], place, middle, send, recv, 2)
    fin_gather = Gather(lambda t: fin_all.at[t], place, middle, send, recv, 3)
    hid_gather = Gather(rows(hid_all), place, middle, send, recv, 4)
    d_gather = Gather(rows(d_all), place, middle, send, recv, 5, True)
    dh_gather = Gather(rows(dh_all), place, middle, send, recv, 6)

    loads[0].wait()
    loads[1].wait()
    dattended = mm(up[...], ow[...], NT).astype(jnp.bfloat16)
    d_all[mine, :] = dattended
    d_gather.own()

    line = lax.broadcasted_iota(jnp.int32, (2 * n, 2 * n), 0)
    cell = lax.broadcasted_iota(jnp.int32, (2 * n, 2 * n), 1)
    wanted = jnp.where(line < n, 2 * line, 2 * (line - n) + 1)
    order = jnp.where(cell == wanted, 1.0, 0.0).astype(jnp.bfloat16)

    def apart(row):
        sorted_row = mm(order, row).astype(jnp.bfloat16)
        return sorted_row[:n], sorted_row[n:]

    loads[2].wait()
    mid_even, mid_odd = apart(fine[0])
    low_even, low_odd = apart(fine[1])
    mid_t[me, :chans, :] = mid_even.T

    for load in loads[3:]:
        load.wait()
    mid_t[me, chans:, :] = mid_odd.T
    low_t[me + 1, :chans, :] = low_even.T
    low_t[me + 1, chans:, :] = low_odd.T
    mid_gather.own_x()
    for part in parts:
        part.own_x()
    low_t[0] = jnp.zeros_like(low_t[0])
    kv_w[:, :HD] = qk[1]
    kv_w[:, HD:] = vw[...]

    def conv_row(a, even, odd):
        return mm(even, conv[a, 1]) + mm(odd, conv[a, 2]), mm(odd, conv[a, 0])

    mid, mid_late = conv_row(1, mid_even, mid_odd)
    low, low_late = conv_row(2, low_even, low_odd)
    halo.wait_recv()
    top_even, top_odd = apart(jnp.where(me == 0, jnp.zeros_like(above[...]), above[...]))
    top, top_late = conv_row(0, top_even, top_odd)
    late = top_late + mid_late + low_late
    row_at = lax.broadcasted_iota(jnp.int32, (n, chans), 0)
    late = jnp.where(row_at == 0, 0.0, pltpu.roll(late, 1, 0))
    hidden = (top + mid + low + late).astype(jnp.bfloat16)
    hid_all[mine, :] = hidden
    hid_gather.own()

    def scaled_query(mat):
        full_query = mm(mat, qk[0]).astype(jnp.bfloat16)
        return (full_query.astype(jnp.float32) * HDIM**-0.5).astype(jnp.bfloat16)

    key_value = mm(hidden, kv_w[...]).astype(jnp.bfloat16)
    q2 = two_heads(scaled_query(hidden))
    d2 = two_heads(dattended)

    def project(k, flip_x):
        span = both(chip(k, flip_x))
        kv_all[span, :] = mm(hid_all[span, :], kv_w[...]).astype(jnp.bfloat16)

    def attend(flip_x, which):
        first = 4 * flip_x + which[0]
        lanes = slice(first * pair, (first + len(which)) * pair)
        for i, k in enumerate(which):
            keys = kv_all[both(chip(k, flip_x)), :HD]
            scores[:, i * pair : (i + 1) * pair] = mm(q2, keys, NT)
        block = scores[:, : len(which) * pair]
        high = jnp.max(block, axis=1, keepdims=True)
        expd = jnp.exp(block - high)
        exp_buf[:, lanes] = expd
        total = jnp.sum(expd, axis=1, keepdims=True)
        mixed = jnp.zeros((pair, HD), jnp.float32)
        for i, k in enumerate(which):
            weights = expd[:, i * pair : (i + 1) * pair].astype(jnp.bfloat16)
            mixed = mixed + mm(weights, kv_all[both(chip(k, flip_x)), HD:])
        groups.append((high, total, mixed, len(which)))

    groups = []
    k2 = two_heads(key_value[:, :HD])
    v2 = two_heads(key_value[:, HD:])

    def prepare_queries(flip_x):
        for k in range(4):
            j = 4 * flip_x + k
            span = both(chip(k, flip_x))
            queries = scaled_query(hid_all[span, :])
            q_all[span, :] = queries
            st_buf[:, j * pair : (j + 1) * pair] = mm(k2, queries, NT)

    def prepare_grads(flip_x):
        for k in range(4):
            j = 4 * flip_x + k
            dpt_buf[:, j * pair : (j + 1) * pair] = mm(v2, d_all[both(chip(k, flip_x)), :], NT)

    def prepare_probs(flip_x):
        for k in range(4):
            j = 4 * flip_x + k
            dp_buf[:, j * pair : (j + 1) * pair] = mm(d2, kv_all[both(chip(k, flip_x)), HD:], NT)

    d_gather.across()

    hid_gather.across()
    parts[0].own_z(2, 1)
    parts[1].own_z(2, 1)
    mid_gather.over(0)
    d_gather.over()
    hid_gather.over(0)
    hid_gather.finish_column()
    for k in range(4):
        project(k, 0)
    attend(0, (0, 1, 2, 3))
    parts[0].own_z(3)
    parts[1].own_z(3)
    hid_gather.over(1)

    prepare_queries(0)
    hid_gather.over(2)

    d_gather.finish_column()
    d_gather.finish_other()
    prepare_grads(0)
    prepare_probs(0)
    hid_gather.over(3)
    parts[0].across(2, 1)
    prepare_grads(1)
    hid_gather.finish_other()
    for k in range(4):
        project(k, 1)

    attend(1, (0, 1, 2, 3))
    high = functools.reduce(jnp.maximum, [g[0] for g in groups])
    shares = [jnp.exp(g[0] - high) for g in groups]
    total = sum(g[1] * share for g, share in zip(groups, shares))
    lse = high + jnp.log(total)
    inverse = 1.0 / total
    shares = [share * inverse for share in shares]
    attended = pick_heads(sum(g[2] * share for g, share in zip(groups, shares)))
    attended = attended.astype(jnp.bfloat16)
    factors = [share for g, share in zip(groups, shares) for _ in range(g[3])]
    product = dattended.astype(jnp.float32) * attended.astype(jnp.float32)
    delta = jnp.sum(two_heads(product), axis=1, keepdims=True)
    lane = lax.broadcasted_iota(jnp.int32, (2 * n, 128), 1)
    packed = jnp.where(lane == 0, lse, jnp.where(lane == 1, delta, 0.0)).T
    stats[me] = packed[:2]
    stat_copies = []
    for step in range(1, peers):
        made = pltpu.make_async_remote_copy(
            src_ref=stats.at[me],
            dst_ref=stats.at[me],
            send_sem=stat_send.at[step],
            recv_sem=stat_recv.at[step],
            device_id={"tile": lax.rem(me + step, peers)},
            device_id_type=pl.DeviceIdType.MESH,
        )
        made.start()
        stat_copies.append(made)
    parts[0].across(3)
    parts[1].across(2, 1)
    block_out[...] = (hidden.astype(jnp.float32) + mm(attended, ow[...])).astype(jnp.bfloat16)
    store(block_out, block_res)
    prepare_queries(1)
    prepare_probs(1)
    dquery = jnp.zeros((pair, HD), jnp.float32)
    for flip_x in (0, 1):
        for k in range(4):
            j = 4 * flip_x + k
            span = both(chip(k, flip_x))
            prob = exp_buf[:, j * pair : (j + 1) * pair] * factors[j]
            dprob = dp_buf[:, j * pair : (j + 1) * pair]
            dscore = (prob * (dprob - delta)).astype(jnp.bfloat16)
            dquery = dquery + mm(dscore, kv_all[span, :HD])
    dquery = (pick_heads(dquery) * HDIM**-0.5).astype(jnp.bfloat16)
    grad_h = up[...].astype(jnp.float32) + mm(dquery, qk[0], NT)


    for step in range(1, peers):
        block = lax.rem(me - step + peers, peers)
        pltpu.make_async_remote_copy(
            src_ref=stats.at[block],
            dst_ref=stats.at[block],
            send_sem=stat_send.at[step],
            recv_sem=stat_recv.at[step],
            device_id={"tile": lower},
            device_id_type=pl.DeviceIdType.MESH,
        ).wait_recv()
    dk = jnp.zeros((2 * n, HD), jnp.float32)
    dv = jnp.zeros((2 * n, HD), jnp.float32)
    for flip_x in (0, 1):
        for k in range(4):
            j = 4 * flip_x + k
            at = chip(k, flip_x)
            span = both(at)

            def stat_rows(kind):
                heads = []
                for h in range(HEADS):
                    lines = [stats[at + c, kind : kind + 1, h * n : (h + 1) * n] for c in (0, 1)]
                    heads.append(jnp.broadcast_to(jnp.concatenate(lines, axis=1), (n, pair)))
                return jnp.concatenate(heads, axis=0)

            lanes = slice(j * pair, (j + 1) * pair)
            prob_t = jnp.exp(st_buf[:, lanes] - stat_rows(0))
            dscore_t = (prob_t * (dpt_buf[:, lanes] - stat_rows(1))).astype(jnp.bfloat16)
            dv = dv + mm(prob_t.astype(jnp.bfloat16), d_all[span, :])
            dk = dk + mm(dscore_t, q_all[span, :])
    dkeys = pick_heads(dk).astype(jnp.bfloat16)
    dvalues = pick_heads(dv).astype(jnp.bfloat16)
    grad_h = grad_h + mm(dkeys, qk[1], NT) + mm(dvalues, vw[...], NT)
    dhidden = grad_h.astype(jnp.bfloat16)
    dh_all[mine, :] = dhidden
    dh_gather.own()


    def back_row(a, grads):
        even = mm(grads, conv[a, 1], NT)
        later = mm(grads, conv[a, 0], NT)
        later = jnp.where(row_at == n - 1, 0.0, pltpu.roll(later, n - 1, 0))
        return even, mm(grads, conv[a, 2], NT) + later

    even_mid, odd_mid = back_row(1, dhidden)
    grad_fine[0, :, :chans] = even_mid.astype(jnp.bfloat16)
    grad_fine[0, :, chans:] = odd_mid.astype(jnp.bfloat16)
    even_low, odd_low = back_row(2, dhidden)
    norm = 1.0 / math.sqrt(full)
    pair_at = lax.broadcasted_iota(jnp.int32, (pair, chans), 0)
    edge = jnp.logical_or(pair_at == n - 1, pair_at == pair - 1)

    def kernel_grads(flip_x, which, last, first):
        straight = []
        moved = []
        for k in which:
            block = dh_all[both(chip(k, flip_x)), :]
            rolled = pltpu.roll(block.astype(jnp.float32), pair - 1, 0)
            straight.append(block)
            moved.append(jnp.where(edge, 0.0, rolled).astype(jnp.bfloat16))
        straight = jnp.concatenate(straight, axis=0)
        moved = jnp.concatenate(moved, axis=0)

        def features(part, shift):
            picks = []
            for k in which:
                at = chip(k, flip_x) + shift
                picks.append(low_t[at, part * chans : (part + 1) * chans, :])
                picks.append(low_t[at + 1, part * chans : (part + 1) * chans, :])
            return jnp.concatenate(picks, axis=1)

        for a, shift in ((2, 1), (0, 0)):
            for b in (1, 2, 0):
                part = mm(features(0 if b == 1 else 1, shift), straight if b else moved)
                slot = 3 * (a // 2) + b
                if not first:
                    part = part + acc[slot]
                if last:
                    grad_conv[slot] = part * norm
                    store(grad_conv.at[slot], grad_conv_res.at[slot])
                else:
                    acc[slot] = part

    strip = chans // 4
    slim = strip // 4
    strip_at = pl.multiple_of((col * 2 + core) * strip, strip)
    strip_copies = []

    def strip_copy(k, target_level):
        return pltpu.make_async_remote_copy(
            src_ref=strip_out.at[target_level],
            dst_ref=strip_in.at[level],
            send_sem=stat_send.at[peers + k],
            recv_sem=stat_recv.at[peers + k],
            device_id={"tile": place(k, 0, 0)},
            device_id_type=pl.DeviceIdType.MESH,
        )

    def strips():
        at = level * 4
        block = dh_all[pl.ds(pl.multiple_of(at * n, 4 * n), 4 * n), :]
        block_row = lax.broadcasted_iota(jnp.int32, block.shape, 0)
        rolled = pltpu.roll(block.astype(jnp.float32), 4 * n - 1, 0)
        rolled = jnp.where(lax.rem(block_row, n) == n - 1, 0.0, rolled).astype(jnp.bfloat16)
        for b, part, grads in ((0, 1, rolled), (1, 0, block), (2, 1, block)):
            lines = pl.ds(pl.multiple_of(part * chans + strip_at, strip), strip)
            picks = jnp.concatenate([mid_t[at + i, lines, :] for i in range(4)], axis=1)
            sums = mm(picks, grads)
            for i in range(4):
                piece = sums[i * slim : (i + 1) * slim]
                strip_sum[i, b * slim : (b + 1) * slim, :] = piece
                strip_out[i, b * slim : (b + 1) * slim, :] = piece.astype(jnp.bfloat16)
        for k in (2, 3, 1):
            made = strip_copy(k, levels[k])
            made.start()
            strip_copies.append(made)

    def strips_sum():
        total = strip_sum[level]
        for k in (1, 2, 3):
            strip_copy(k, levels[k]).wait_recv()
        for k in (1, 2, 3):
            total = total + strip_in[levels[k]].astype(jnp.float32)
        fin_all[me] = (total * norm).astype(jnp.bfloat16)

    def strips_end():
        store(fin_all, strips_res)

    parts[1].across(3)
    dh_gather.across(1)
    dh_gather.over(0)

    dh_gather.finish_column(0)
    dh_gather.finish_other(0)
    mid_gather.finish_column(0)
    mid_gather.finish_other(0)
    strips()

    dh_gather.across(2, 3)

    for part in parts:
        part.over()
    dh_gather.over(1)
    dh_gather.finish_column(1, 2, 3)
    for part in parts:
        part.finish_column()
        part.finish_other()
    kernel_grads(0, (0, 1, 2, 3), False, True)
    dh_gather.over(2)
    strips_sum()
    fin_gather.own()
    fin_gather.own_diagonal()
    dh_gather.finish_other(1, 2)
    kernel_grads(1, (0, 1, 2), False, False)
    dh_gather.over(3)
    dh_gather.finish_other(3)
    kernel_grads(1, (3,), True, False)
    fin_gather.across(wide=False)

    below = dh_all[pl.ds(pl.multiple_of(lower * n, n), n), :]
    below = jnp.where(me == peers - 1, jnp.zeros_like(below), below)
    even_top, odd_top = back_row(0, below)
    grad_fine[1, :, :chans] = (even_low + even_top).astype(jnp.bfloat16)
    grad_fine[1, :, chans:] = (odd_low + odd_top).astype(jnp.bfloat16)
    store(grad_fine, grad_fine_res)

    fin_gather.over()
    fin_gather.finish_column()
    fin_gather.finish_other()
    strips_end()
    for made in strip_copies:
        made.wait_send()
    halo.wait_send()
    for gather in (*parts, mid_gather, fin_gather, hid_gather, d_gather, dh_gather):
        gather.drain()
    for made in stat_copies:
        made.wait_send()
    for made in stores:
        made.wait()


def emit_kernel(
    block_in, taps_in, fine_in, strips_in, block_out, taps_out, fine_out, gathered, middle_taps, sem
):
    moves = [pltpu.make_async_copy(strips_in, gathered, sem.at[12])]
    for i in range(6):
        moves.append(pltpu.make_async_copy(taps_in.at[i], taps_out.at[i + i // 3 * 3], sem.at[i]))
    moves.append(pltpu.make_async_copy(block_in, block_out, sem.at[6]))
    for i in range(2):
        moves.append(pltpu.make_async_copy(fine_in.at[i], fine_out.at[i], sem.at[7 + i]))
    for move in moves:
        move.start()
    moves[0].wait()
    slim = gathered.shape[1] // 3
    for b in range(3):
        for i in range(4):
            for r in range(4):
                at = (4 * r + i) * slim
                piece = gathered[i * 4 + r, b * slim : (b + 1) * slim, :]
                middle_taps[b, at : at + slim, :] = piece.astype(jnp.float32)
        move = pltpu.make_async_copy(middle_taps.at[b], taps_out.at[3 + b], sem.at[9 + b])
        move.start()
        moves.append(move)
    for move in moves[1:]:
        move.wait()


def emit(block_out, taps, fine, strips):
    where = pl.BlockSpec(memory_space=pl.ANY)
    chans = taps.shape[1]
    return pl.pallas_call(
        emit_kernel,
        out_shape=(
            jax.ShapeDtypeStruct(block_out.shape, block_out.dtype),
            jax.ShapeDtypeStruct((9, chans, chans), taps.dtype),
            jax.ShapeDtypeStruct(fine.shape, fine.dtype),
        ),
        in_specs=[where] * 4,
        out_specs=(where,) * 3,
        scratch_shapes=[
            pltpu.VMEM(strips.shape, strips.dtype),
            pltpu.VMEM((3, chans, chans), taps.dtype),
            pltpu.SemaphoreType.DMA((16,)),
        ],
        compiler_params=pltpu.CompilerParams(vmem_limit_bytes=4 * 2**20),
    )(block_out, taps, fine, strips)


def fused_body(fine, conv_weight, qk_weight, v_weight, o_weight, upstream):
    peers = lax.axis_size("tile")
    n, chans = upstream.shape
    full = n * peers
    hbm = pl.BlockSpec(memory_space=pltpu.HBM)
    free = pl.BlockSpec(memory_space=pl.ANY)
    dma = pltpu.SemaphoreType.DMA
    low = jnp.bfloat16
    sources = (fine, conv_weight, qk_weight, v_weight, o_weight, upstream)
    block_out, taps, grad_fine, strips = pl.pallas_call(
        functools.partial(fused_kernel, peers),
        out_shape=(
            jax.ShapeDtypeStruct((n, chans), low),
            jax.ShapeDtypeStruct((6, chans, chans), jnp.float32),
            jax.ShapeDtypeStruct((2, n, 2 * chans), low),
            jax.ShapeDtypeStruct((peers, 3 * chans // 16, chans), low),
        ),
        in_specs=[hbm] * 6,
        out_specs=(free,) * 4,
        scratch_shapes=[
            pltpu.VMEM(fine.shape, low),
            pltpu.VMEM(conv_weight.shape, low),
            pltpu.VMEM(qk_weight.shape, low),
            pltpu.VMEM(v_weight.shape, low),
            pltpu.VMEM(o_weight.shape, low),
            pltpu.VMEM(upstream.shape, low),
            pltpu.VMEM((n, chans), low),
            pltpu.VMEM((6, chans, chans), jnp.float32),
            pltpu.VMEM((2, n, 2 * chans), low),
            dma((6,)),
            dma((11,)),
            pltpu.VMEM((2 * n, chans), low),
            pltpu.VMEM((full, chans), low),
            pltpu.VMEM((full, 2 * HD), low),
            pltpu.VMEM((full, HD), low),
            pltpu.VMEM((full, HD), low),
            pltpu.VMEM((full, chans), low),
            pltpu.VMEM((peers, 2 * chans, n), low),
            pltpu.VMEM((peers + 1, 2 * chans, n), low),
            pltpu.VMEM((peers, 2, 2 * n), jnp.float32),
            pltpu.VMEM((2 * n, full), jnp.float32),
            pltpu.VMEM((2 * n, full), jnp.float32),
            pltpu.VMEM((2 * n, full), jnp.float32),
            pltpu.VMEM((chans, 2 * HD), low),
            pltpu.VMEM((6, chans, chans), jnp.float32),
            dma((7, 16)),
            dma((7, 16)),
            dma((peers + 4,)),
            dma((peers + 4,)),
            dma,
            dma,
            pltpu.VMEM((4, 3 * chans // 16, chans), jnp.float32),
            pltpu.VMEM((4, 3 * chans // 16, chans), low),
            pltpu.VMEM((4, 3 * chans // 16, chans), low),
            pltpu.VMEM((peers, 3 * chans // 16, chans), low),
            pltpu.VMEM((2 * n, full // 2), jnp.float32),
            pltpu.VMEM((2 * n, full), jnp.float32),
        ],
        compiler_params=pltpu.CompilerParams(
            collective_id=0, has_side_effects=True, vmem_limit_bytes=36 * 2**20
        ),
    )(*[pltpu.with_memory_space_constraint(v, pltpu.HBM) for v in sources])
    results = emit(block_out, taps, grad_fine.reshape(fine.shape), strips)
    block_out, grad_conv, grad_fine = results
    return block_out, grad_conv.reshape(3, 3, chans, chans), grad_fine


def solution(mesh):
    def whole(fine, *rest):
        devices = mesh.shape["groups"] * mesh.shape["tile"]
        one_row = fine.shape[0] == 2 * devices and fine.shape[1] == 256 and fine.shape[2] == 256
        fits = mesh.shape["tile"] == 16
        return jax.shard_map(
            fused_body if one_row and fits else body,
            mesh=mesh,
            in_specs=(
                P(("groups", "tile"), None, None),
                P(),
                P(),
                P(),
                P(),
                P(("groups", "tile"), None),
            ),
            out_specs=(
                P(("groups", "tile"), None),
                P("groups", None, None, None),
                P(("groups", "tile"), None, None),
            ),
            check_vma=False,
        )(fine, *rest)

    return whole
```

```python
import functools
import math

import jax
import jax.numpy as jnp
from jax import lax
from jax.experimental import pallas as pl
from jax.experimental.pallas import tpu as pltpu
from jax.sharding import PartitionSpec as P

HEADS = 2
HDIM = 64
HD = 128


def shifted(x, axis, by):
    peers = lax.axis_size(axis)
    pairs = [(i, i + by) for i in range(peers) if 0 <= i + by < peers]
    return lax.ppermute(x, axis, pairs)


def head_view(mat):
    return mat.reshape(mat.shape[0], HEADS, HDIM)


def score_block(queries, keys):
    product = jnp.einsum(
        "qhd,khd->hqk", head_view(queries), head_view(keys), preferred_element_type=jnp.float32
    )
    return product * HDIM ** (-0.5)


def dot_back(left, right):
    return lax.dot_general(
        left, right, (((1,), (1,)), ((), ())), preferred_element_type=jnp.float32
    )


def dot_over(left, right):
    return lax.dot_general(
        left, right, (((0,), (0,)), ((), ())), preferred_element_type=jnp.float32
    )


def body(fine, conv_weight, qk_weight, v_weight, o_weight, upstream):
    rows = fine.shape[0] // 2
    cols = fine.shape[1] // 2
    chans = fine.shape[2]
    local = rows * cols
    scale = HDIM ** (-0.5)
    above = shifted(fine[-1:], "tile", 1)
    padded = jnp.pad(jnp.concatenate([above, fine], axis=0), ((0, 0), (1, 0), (0, 0)))
    taps = []
    total = jnp.zeros((local, chans), jnp.float32)
    for a in range(3):
        for b in range(3):
            tap = padded[a : a + 2 * rows : 2, b : b + 2 * cols : 2].reshape(local, chans)
            taps.append(tap)
            total = total + jnp.dot(tap, conv_weight[a, b], preferred_element_type=jnp.float32)
    hidden = total.astype(jnp.bfloat16)
    query = jnp.dot(hidden, qk_weight[0], preferred_element_type=jnp.float32).astype(jnp.bfloat16)
    key_loc = jnp.dot(hidden, qk_weight[1], preferred_element_type=jnp.float32).astype(jnp.bfloat16)
    value_loc = jnp.dot(hidden, v_weight, preferred_element_type=jnp.float32).astype(jnp.bfloat16)
    keys_all, values_all = (
        lax.all_gather(key_loc, "tile", axis=0, tiled=True),
        lax.all_gather(value_loc, "tile", axis=0, tiled=True),
    )
    everyone = keys_all.shape[0]
    block = math.gcd(everyone, 2048)
    steps_total = everyone // block

    def stats_step(index, carry):
        top, summed = carry
        scores = score_block(query, lax.dynamic_slice_in_dim(keys_all, index * block, block, 0))
        new_top = jnp.maximum(top, jnp.max(scores, axis=2))
        summed = summed * jnp.exp(top - new_top) + jnp.sum(
            jnp.exp(scores - new_top[:, :, None]), axis=2
        )
        return (new_top, summed)

    start_top = jnp.full((HEADS, local), -jnp.inf, jnp.float32)
    top, summed = lax.fori_loop(
        0, steps_total, stats_step, (start_top, jnp.zeros((HEADS, local), jnp.float32))
    )
    lse = top + jnp.log(summed)

    def value_step(index, acc):
        scores = score_block(query, lax.dynamic_slice_in_dim(keys_all, index * block, block, 0))
        weights = jnp.exp(scores - lse[:, :, None]).astype(jnp.bfloat16)
        v_part = head_view(lax.dynamic_slice_in_dim(values_all, index * block, block, 0))
        return acc + jnp.einsum("hqk,khd->qhd", weights, v_part, preferred_element_type=jnp.float32)

    mixed = lax.fori_loop(0, steps_total, value_step, jnp.zeros((local, HEADS, HDIM), jnp.float32))
    attended = mixed.reshape(local, HD).astype(jnp.bfloat16)
    block_out = (
        hidden.astype(jnp.float32) + jnp.dot(attended, o_weight, preferred_element_type=jnp.float32)
    ).astype(jnp.bfloat16)
    dattended = dot_back(upstream, o_weight).astype(jnp.bfloat16)
    product = dattended.astype(jnp.float32) * attended.astype(jnp.float32)
    delta = jnp.sum(product.reshape(local, HEADS, HDIM), axis=2).T

    def query_step(index, acc):
        k_part = lax.dynamic_slice_in_dim(keys_all, index * block, block, 0)
        v_part = lax.dynamic_slice_in_dim(values_all, index * block, block, 0)
        prob = jnp.exp(score_block(query, k_part) - lse[:, :, None])
        dprob = jnp.einsum(
            "qhd,khd->hqk",
            head_view(dattended),
            head_view(v_part),
            preferred_element_type=jnp.float32,
        )
        dscore = (prob * (dprob - delta[:, :, None]) * scale).astype(jnp.bfloat16)
        return acc + jnp.einsum(
            "hqk,khd->qhd", dscore, head_view(k_part), preferred_element_type=jnp.float32
        )

    dq_acc = lax.fori_loop(0, steps_total, query_step, jnp.zeros((local, HEADS, HDIM), jnp.float32))
    dquery = dq_acc.reshape(local, HD).astype(jnp.bfloat16)
    lse_all, delta_all = (
        lax.all_gather(lse.T, "tile", axis=0, tiled=True),
        lax.all_gather(delta.T, "tile", axis=0, tiled=True),
    )
    empty = jnp.zeros((local, HEADS, HDIM), jnp.float32)
    q_in = lax.all_gather(query, "tile", axis=0, tiled=True)
    d_in = lax.all_gather(dattended, "tile", axis=0, tiled=True)
    incoming = q_in.shape[0]
    sub = math.gcd(incoming, 2048)

    def inner(index, acc):
        dk_acc, dv_acc = acc
        at = index * sub
        q_part = lax.dynamic_slice_in_dim(q_in, at, sub, 0)
        d_part = lax.dynamic_slice_in_dim(d_in, at, sub, 0)
        l_part = lax.dynamic_slice_in_dim(lse_all, at, sub, 0).T
        e_part = lax.dynamic_slice_in_dim(delta_all, at, sub, 0).T
        prob = jnp.exp(score_block(q_part, key_loc) - l_part[:, :, None])
        dv_acc = dv_acc + jnp.einsum(
            "hqk,qhd->khd",
            prob.astype(jnp.bfloat16),
            head_view(d_part),
            preferred_element_type=jnp.float32,
        )
        dprob = jnp.einsum(
            "qhd,khd->hqk",
            head_view(d_part),
            head_view(value_loc),
            preferred_element_type=jnp.float32,
        )
        dscore = (prob * (dprob - e_part[:, :, None]) * scale).astype(jnp.bfloat16)
        dk_acc = dk_acc + jnp.einsum(
            "hqk,qhd->khd", dscore, head_view(q_part), preferred_element_type=jnp.float32
        )
        return (dk_acc, dv_acc)

    dk_acc, dv_acc = lax.fori_loop(0, incoming // sub, inner, (empty, empty))
    dkeys = dk_acc.reshape(local, HD).astype(jnp.bfloat16)
    dvalues = dv_acc.reshape(local, HD).astype(jnp.bfloat16)
    dhidden = upstream.astype(jnp.float32)
    dhidden = dhidden + dot_back(dquery, qk_weight[0])
    dhidden = dhidden + dot_back(dkeys, qk_weight[1])
    dhidden = dhidden + dot_back(dvalues, v_weight)
    dhidden = dhidden.astype(jnp.bfloat16)
    kernel_rows = []
    dpadded = jnp.zeros((2 * rows + 1, 2 * cols + 1, chans), jnp.float32)
    for a in range(3):
        row_list = []
        for b in range(3):
            row_list.append(dot_over(taps[3 * a + b], dhidden))
            back = dot_back(dhidden, conv_weight[a, b])
            dpadded = dpadded.at[a : a + 2 * rows : 2, b : b + 2 * cols : 2].add(
                back.reshape(rows, cols, chans)
            )
        kernel_rows.append(jnp.stack(row_list))
    kernel_local = jnp.stack(kernel_rows)
    grad_conv = lax.psum(kernel_local, "tile") * (1.0 / math.sqrt(everyone))
    below = shifted(dpadded[0:1, 1:].astype(jnp.bfloat16), "tile", -1).astype(jnp.float32)
    grad_fine = dpadded[1:, 1:]
    grad_fine = grad_fine.at[-1:].add(below)
    return (block_out, grad_conv, grad_fine.astype(jnp.bfloat16))


NT = (((1,), (1,)), ((), ()))
NN = (((1,), (0,)), ((), ()))


def mm(left, right, dims=NN):
    return lax.dot_general(left, right, dims, preferred_element_type=jnp.float32)


def two_heads(mat):
    lane = lax.broadcasted_iota(jnp.int32, mat.shape, 1)
    zero = jnp.zeros_like(mat)
    return jnp.concatenate(
        [jnp.where(lane < HDIM, mat, zero), jnp.where(lane < HDIM, zero, mat)], axis=0
    )


def pick_heads(mat):
    half = mat.shape[0] // 2
    lane = lax.broadcasted_iota(jnp.int32, (half, mat.shape[1]), 1)
    return jnp.where(lane < HDIM, mat[:half], mat[half:])


class Gather:
    def __init__(self, view, place, middle, send, recv, slot, relayed=False):
        self.view, self.place, self.send, self.recv, self.slot = view, place, send, recv, slot
        self.middle, self.relayed = middle, relayed
        self.copies = []
        self.middle_copies = []

    def copy(self, index, block, target):
        return pltpu.make_async_remote_copy(
            src_ref=self.view(block),
            dst_ref=self.view(block),
            send_sem=self.send.at[self.slot, index],
            recv_sem=self.recv.at[self.slot, index],
            device_id={"tile": target},
            device_id_type=pl.DeviceIdType.MESH,
        )

    def go(self, index, block, target):
        made = self.copy(index, block, target)
        made.start()
        self.copies.append(made)

    def go_middle(self, index, out, block, target):
        made = pltpu.make_async_remote_copy(
            src_ref=self.view(block),
            dst_ref=self.view(block),
            send_sem=self.send.at[self.slot, out],
            recv_sem=self.recv.at[self.slot, index],
            device_id={"tile": target},
            device_id_type=pl.DeviceIdType.MESH,
        )

        @pl.when(self.middle)
        def _():
            made.start()

        self.middle_copies.append(made)

    def landed(self, index, block):
        self.copy(index, block, self.place(0, 0, 1)).wait_recv()

    def own_z(self, *which):
        block = self.place(0, 0, 0)
        for k in which or (1, 2, 3):
            if k == 3 and self.relayed:
                self.go_middle(3, 3, block, self.place(3, 0, 0))
            else:
                self.go(k, block, self.place(k, 0, 0))

    def own_core(self):
        self.go(8, self.place(0, 0, 0), self.place(0, 0, 1))

    def own_x(self):
        self.go(4, self.place(0, 0, 0), self.place(0, 1, 0))
        self.own_core()

    def own_diagonal(self, *which):
        for k in which or (1, 2, 3):
            self.go(4 + k, self.place(0, 0, 0), self.place(k, 1, 0))

    def own(self):
        self.own_z()
        self.own_x()

    def across(self, *which, wide=True):
        for k in which or ((2, 1, 3) if self.relayed else (1, 2, 3)):
            block = self.place(k, 0, 0)
            self.landed(k, block)
            if k == 2 and self.relayed:
                self.go_middle(3, 0, block, self.place(1, 0, 0))
            if wide:
                self.go(4 + k, block, self.place(0, 1, 0))
            self.go(8 + k, block, self.place(0, 0, 1))

    def over(self, *which):
        for k in which or (0, 1, 2, 3):
            block = self.place(k, 1, 0)
            self.landed(4 + k, block)
            self.go(12 + k, block, self.place(0, 0, 1))

    def finish_column(self, *which):
        for k in which or (0, 1, 2, 3):
            self.landed(8 + k, self.place(k, 0, 1))

    def finish_other(self, *which):
        for k in which or (0, 1, 2, 3):
            self.landed(12 + k, self.place(k, 1, 1))

    def drain(self):
        for made in self.copies:
            made.wait_send()
        for made in self.middle_copies:

            @pl.when(self.middle)
            def _(made=made):
                made.wait_send()


def fused_kernel(
    peers,
    fine_hbm,
    conv_hbm,
    qk_hbm,
    vw_hbm,
    ow_hbm,
    up_hbm,
    block_res,
    grad_conv_res,
    grad_fine_res,
    strips_res,
    fine,
    conv,
    qk,
    vw,
    ow,
    up,
    block_out,
    grad_conv,
    grad_fine,
    in_sem,
    out_sem,
    above,
    hid_all,
    kv_all,
    q_all,
    d_all,
    dh_all,
    mid_t,
    low_t,
    stats,
    exp_buf,
    st_buf,
    dpt_buf,
    kv_w,
    acc,
    send,
    recv,
    stat_send,
    stat_recv,
    halo_send,
    halo_recv,
    strip_sum,
    strip_out,
    strip_in,
    fin_all,
    scores,
    dp_buf,
):
    me = lax.axis_index("tile")
    n = up.shape[0]
    chans = up.shape[1]
    full = n * peers
    pair = 2 * n
    lower = lax.rem(me + 1, peers)
    core = lax.rem(me, 2)
    col = lax.rem(lax.div(me, 2), 2)
    level = lax.div(me, 4)
    middle = lax.rem(level + 1, 4) >= 2
    levels = (level, level + 1 - 2 * lax.rem(level, 2), lax.rem(level + 2, 4), 3 - level)

    def place(k, flip_x, flip_core):
        x = 1 - col if flip_x else col
        c = 1 - core if flip_core else core
        return levels[k] * 4 + x * 2 + c

    def chip(k, flip_x):
        return levels[k] * 4 + (1 - col if flip_x else col) * 2

    barrier = pltpu.get_barrier_semaphore()
    for step in range(1, peers):
        pl.semaphore_signal(
            barrier,
            inc=1,
            device_id={"tile": lax.rem(me + step, peers)},
            device_id_type=pl.DeviceIdType.MESH,
        )
    moves = (
        (up_hbm, up), (ow_hbm, ow), (fine_hbm, fine), (conv_hbm, conv), (qk_hbm, qk), (vw_hbm, vw)
    )
    loads = [pltpu.make_async_copy(a, b, in_sem.at[i]) for i, (a, b) in enumerate(moves)]
    for load in loads:
        load.start()
    stores = []

    def store(source, target):
        made = pltpu.make_async_copy(source, target, out_sem.at[len(stores)])
        made.start()
        stores.append(made)

    def rows(ref):
        return lambda t: ref.at[pl.ds(pl.multiple_of(t * n, n), n), :]

    def cols(ref, part, shift):
        lines = pl.ds(part * chans, chans)
        return lambda t: ref.at[t + shift, lines, :]

    def both(t):
        return pl.ds(pl.multiple_of(t * n, pair), pair)

    mine = pl.ds(pl.multiple_of(me * n, n), n)
    halo = pltpu.make_async_remote_copy(
        src_ref=fine_hbm.at[1],
        dst_ref=above,
        send_sem=halo_send,
        recv_sem=halo_recv,
        device_id={"tile": lower},
        device_id_type=pl.DeviceIdType.MESH,
    )
    pl.semaphore_wait(barrier, peers - 1)
    halo.start()
    views = (cols(low_t, 1, 1), cols(low_t, 0, 1))
    parts = [Gather(view, place, middle, send, recv, i, True) for i, view in enumerate(views)]
    mid_gather = Gather(lambda t: mid_t.at[t], place, middle, send, recv, 2)
    fin_gather = Gather(lambda t: fin_all.at[t], place, middle, send, recv, 3)
    hid_gather = Gather(rows(hid_all), place, middle, send, recv, 4)
    d_gather = Gather(rows(d_all), place, middle, send, recv, 5, True)
    dh_gather = Gather(rows(dh_all), place, middle, send, recv, 6)

    loads[0].wait()
    loads[1].wait()
    dattended = mm(up[...], ow[...], NT).astype(jnp.bfloat16)
    d_all[mine, :] = dattended
    d_gather.own()

    line = lax.broadcasted_iota(jnp.int32, (2 * n, 2 * n), 0)
    cell = lax.broadcasted_iota(jnp.int32, (2 * n, 2 * n), 1)
    wanted = jnp.where(line < n, 2 * line, 2 * (line - n) + 1)
    order = jnp.where(cell == wanted, 1.0, 0.0).astype(jnp.bfloat16)

    def apart(row):
        sorted_row = mm(order, row).astype(jnp.bfloat16)
        return sorted_row[:n], sorted_row[n:]

    loads[2].wait()
    mid_even, mid_odd = apart(fine[0])
    low_even, low_odd = apart(fine[1])
    mid_t[me, :chans, :] = mid_even.T

    for load in loads[3:]:
        load.wait()
    mid_t[me, chans:, :] = mid_odd.T
    low_t[me + 1, :chans, :] = low_even.T
    low_t[me + 1, chans:, :] = low_odd.T
    mid_gather.own_x()
    for part in parts:
        part.own_x()
    low_t[0] = jnp.zeros_like(low_t[0])
    kv_w[:, :HD] = qk[1]
    kv_w[:, HD:] = vw[...]

    def conv_row(a, even, odd):
        return mm(even, conv[a, 1]) + mm(odd, conv[a, 2]), mm(odd, conv[a, 0])

    mid, mid_late = conv_row(1, mid_even, mid_odd)
    low, low_late = conv_row(2, low_even, low_odd)
    halo.wait_recv()
    top_even, top_odd = apart(jnp.where(me == 0, jnp.zeros_like(above[...]), above[...]))
    top, top_late = conv_row(0, top_even, top_odd)
    late = top_late + mid_late + low_late
    row_at = lax.broadcasted_iota(jnp.int32, (n, chans), 0)
    late = jnp.where(row_at == 0, 0.0, pltpu.roll(late, 1, 0))
    hidden = (top + mid + low + late).astype(jnp.bfloat16)
    hid_all[mine, :] = hidden
    hid_gather.own()

    def scaled_query(mat):
        full_query = mm(mat, qk[0]).astype(jnp.bfloat16)
        return (full_query.astype(jnp.float32) * HDIM**-0.5).astype(jnp.bfloat16)

    key_value = mm(hidden, kv_w[...]).astype(jnp.bfloat16)
    q2 = two_heads(scaled_query(hidden))
    d2 = two_heads(dattended)

    def project(k, flip_x):
        span = both(chip(k, flip_x))
        kv_all[span, :] = mm(hid_all[span, :], kv_w[...]).astype(jnp.bfloat16)

    def attend(flip_x, which):
        first = 4 * flip_x + which[0]
        lanes = slice(first * pair, (first + len(which)) * pair)
        for i, k in enumerate(which):
            keys = kv_all[both(chip(k, flip_x)), :HD]
            scores[:, i * pair : (i + 1) * pair] = mm(q2, keys, NT)
        block = scores[:, : len(which) * pair]
        high = jnp.max(block, axis=1, keepdims=True)
        expd = jnp.exp(block - high)
        exp_buf[:, lanes] = expd
        total = jnp.sum(expd, axis=1, keepdims=True)
        mixed = jnp.zeros((pair, HD), jnp.float32)
        for i, k in enumerate(which):
            weights = expd[:, i * pair : (i + 1) * pair].astype(jnp.bfloat16)
            mixed = mixed + mm(weights, kv_all[both(chip(k, flip_x)), HD:])
        groups.append((high, total, mixed, len(which)))

    groups = []
    k2 = two_heads(key_value[:, :HD])
    v2 = two_heads(key_value[:, HD:])

    def prepare_queries(flip_x):
        for k in range(4):
            j = 4 * flip_x + k
            span = both(chip(k, flip_x))
            queries = scaled_query(hid_all[span, :])
            q_all[span, :] = queries
            st_buf[:, j * pair : (j + 1) * pair] = mm(k2, queries, NT)

    def prepare_grads(flip_x):
        for k in range(4):
            j = 4 * flip_x + k
            dpt_buf[:, j * pair : (j + 1) * pair] = mm(v2, d_all[both(chip(k, flip_x)), :], NT)

    def prepare_probs(flip_x):
        for k in range(4):
            j = 4 * flip_x + k
            dp_buf[:, j * pair : (j + 1) * pair] = mm(d2, kv_all[both(chip(k, flip_x)), HD:], NT)

    d_gather.across()

    hid_gather.across()
    parts[0].own_z(2, 1)
    parts[1].own_z(2, 1)
    mid_gather.over(0)
    d_gather.over()
    hid_gather.over(0)
    hid_gather.finish_column()
    for k in range(4):
        project(k, 0)
    attend(0, (0, 1, 2, 3))
    parts[0].own_z(3)
    parts[1].own_z(3)
    hid_gather.over(1)

    prepare_queries(0)
    hid_gather.over(2)

    d_gather.finish_column()
    d_gather.finish_other()
    prepare_grads(0)
    prepare_probs(0)
    hid_gather.over(3)
    parts[0].across(2, 1)
    prepare_grads(1)
    hid_gather.finish_other()
    for k in range(4):
        project(k, 1)

    attend(1, (0, 1, 2, 3))
    high = functools.reduce(jnp.maximum, [g[0] for g in groups])
    shares = [jnp.exp(g[0] - high) for g in groups]
    total = sum(g[1] * share for g, share in zip(groups, shares))
    lse = high + jnp.log(total)
    inverse = 1.0 / total
    shares = [share * inverse for share in shares]
    attended = pick_heads(sum(g[2] * share for g, share in zip(groups, shares)))
    attended = attended.astype(jnp.bfloat16)
    factors = [share for g, share in zip(groups, shares) for _ in range(g[3])]
    product = dattended.astype(jnp.float32) * attended.astype(jnp.float32)
    delta = jnp.sum(two_heads(product), axis=1, keepdims=True)
    lane = lax.broadcasted_iota(jnp.int32, (2 * n, 128), 1)
    packed = jnp.where(lane == 0, lse, jnp.where(lane == 1, delta, 0.0)).T
    stats[me] = packed[:2]
    stat_copies = []
    for step in range(1, peers):
        made = pltpu.make_async_remote_copy(
            src_ref=stats.at[me],
            dst_ref=stats.at[me],
            send_sem=stat_send.at[step],
            recv_sem=stat_recv.at[step],
            device_id={"tile": lax.rem(me + step, peers)},
            device_id_type=pl.DeviceIdType.MESH,
        )
        made.start()
        stat_copies.append(made)
    parts[0].across(3)
    parts[1].across(2, 1)
    block_out[...] = (hidden.astype(jnp.float32) + mm(attended, ow[...])).astype(jnp.bfloat16)
    store(block_out, block_res)
    prepare_queries(1)
    prepare_probs(1)
    dquery = jnp.zeros((pair, HD), jnp.float32)
    for flip_x in (0, 1):
        for k in range(4):
            j = 4 * flip_x + k
            span = both(chip(k, flip_x))
            prob = exp_buf[:, j * pair : (j + 1) * pair] * factors[j]
            dprob = dp_buf[:, j * pair : (j + 1) * pair]
            dscore = (prob * (dprob - delta)).astype(jnp.bfloat16)
            dquery = dquery + mm(dscore, kv_all[span, :HD])
    dquery = (pick_heads(dquery) * HDIM**-0.5).astype(jnp.bfloat16)
    grad_h = up[...].astype(jnp.float32) + mm(dquery, qk[0], NT)


    for step in range(1, peers):
        block = lax.rem(me - step + peers, peers)
        pltpu.make_async_remote_copy(
            src_ref=stats.at[block],
            dst_ref=stats.at[block],
            send_sem=stat_send.at[step],
            recv_sem=stat_recv.at[step],
            device_id={"tile": lower},
            device_id_type=pl.DeviceIdType.MESH,
        ).wait_recv()
    dk = jnp.zeros((2 * n, HD), jnp.float32)
    dv = jnp.zeros((2 * n, HD), jnp.float32)
    for flip_x in (0, 1):
        for k in range(4):
            j = 4 * flip_x + k
            at = chip(k, flip_x)
            span = both(at)

            def stat_rows(kind):
                heads = []
                for h in range(HEADS):
                    lines = [stats[at + c, kind : kind + 1, h * n : (h + 1) * n] for c in (0, 1)]
                    heads.append(jnp.broadcast_to(jnp.concatenate(lines, axis=1), (n, pair)))
                return jnp.concatenate(heads, axis=0)

            lanes = slice(j * pair, (j + 1) * pair)
            prob_t = jnp.exp(st_buf[:, lanes] - stat_rows(0))
            dscore_t = (prob_t * (dpt_buf[:, lanes] - stat_rows(1))).astype(jnp.bfloat16)
            dv = dv + mm(prob_t.astype(jnp.bfloat16), d_all[span, :])
            dk = dk + mm(dscore_t, q_all[span, :])
    dkeys = pick_heads(dk).astype(jnp.bfloat16)
    dvalues = pick_heads(dv).astype(jnp.bfloat16)
    grad_h = grad_h + mm(dkeys, qk[1], NT) + mm(dvalues, vw[...], NT)
    dhidden = grad_h.astype(jnp.bfloat16)
    dh_all[mine, :] = dhidden
    dh_gather.own_x()
    dh_gather.own_z()


    def back_row(a, grads):
        even = mm(grads, conv[a, 1], NT)
        later = mm(grads, conv[a, 0], NT)
        later = jnp.where(row_at == n - 1, 0.0, pltpu.roll(later, n - 1, 0))
        return even, mm(grads, conv[a, 2], NT) + later

    even_mid, odd_mid = back_row(1, dhidden)
    grad_fine[0, :, :chans] = even_mid.astype(jnp.bfloat16)
    grad_fine[0, :, chans:] = odd_mid.astype(jnp.bfloat16)
    even_low, odd_low = back_row(2, dhidden)
    norm = 1.0 / math.sqrt(full)
    pair_at = lax.broadcasted_iota(jnp.int32, (pair, chans), 0)
    edge = jnp.logical_or(pair_at == n - 1, pair_at == pair - 1)

    def kernel_grads(flip_x, which, last, first):
        straight = []
        moved = []
        for k in which:
            block = dh_all[both(chip(k, flip_x)), :]
            rolled = pltpu.roll(block.astype(jnp.float32), pair - 1, 0)
            straight.append(block)
            moved.append(jnp.where(edge, 0.0, rolled).astype(jnp.bfloat16))
        straight = jnp.concatenate(straight, axis=0)
        moved = jnp.concatenate(moved, axis=0)

        def features(part, shift):
            picks = []
            for k in which:
                at = chip(k, flip_x) + shift
                picks.append(low_t[at, part * chans : (part + 1) * chans, :])
                picks.append(low_t[at + 1, part * chans : (part + 1) * chans, :])
            return jnp.concatenate(picks, axis=1)

        for a, shift in ((2, 1), (0, 0)):
            for b in (1, 2, 0):
                part = mm(features(0 if b == 1 else 1, shift), straight if b else moved)
                slot = 3 * (a // 2) + b
                if not first:
                    part = part + acc[slot]
                if last:
                    grad_conv[slot] = part * norm
                    store(grad_conv.at[slot], grad_conv_res.at[slot])
                else:
                    acc[slot] = part

    strip = chans // 4
    slim = strip // 4
    strip_at = pl.multiple_of((col * 2 + core) * strip, strip)
    strip_copies = []

    def strip_copy(k, target_level):
        return pltpu.make_async_remote_copy(
            src_ref=strip_out.at[target_level],
            dst_ref=strip_in.at[level],
            send_sem=stat_send.at[peers + k],
            recv_sem=stat_recv.at[peers + k],
            device_id={"tile": place(k, 0, 0)},
            device_id_type=pl.DeviceIdType.MESH,
        )

    def strips():
        at = level * 4
        block = dh_all[pl.ds(pl.multiple_of(at * n, 4 * n), 4 * n), :]
        block_row = lax.broadcasted_iota(jnp.int32, block.shape, 0)
        rolled = pltpu.roll(block.astype(jnp.float32), 4 * n - 1, 0)
        rolled = jnp.where(lax.rem(block_row, n) == n - 1, 0.0, rolled).astype(jnp.bfloat16)
        for b, part, grads in ((0, 1, rolled), (1, 0, block), (2, 1, block)):
            lines = pl.ds(pl.multiple_of(part * chans + strip_at, strip), strip)
            picks = jnp.concatenate([mid_t[at + i, lines, :] for i in range(4)], axis=1)
            sums = mm(picks, grads)
            for i in range(4):
                piece = sums[i * slim : (i + 1) * slim]
                strip_sum[i, b * slim : (b + 1) * slim, :] = piece
                strip_out[i, b * slim : (b + 1) * slim, :] = piece.astype(jnp.bfloat16)
        for k in (2, 3, 1):
            made = strip_copy(k, levels[k])
            made.start()
            strip_copies.append(made)

    def strips_sum():
        total = strip_sum[level]
        for k in (1, 2, 3):
            strip_copy(k, levels[k]).wait_recv()
        for k in (1, 2, 3):
            total = total + strip_in[levels[k]].astype(jnp.float32)
        fin_all[me] = (total * norm).astype(jnp.bfloat16)

    def strips_end():
        store(fin_all, strips_res)

    parts[1].across(3)
    dh_gather.across(1)
    dh_gather.over(0)

    dh_gather.finish_column(0)
    dh_gather.finish_other(0)
    mid_gather.finish_column(0)
    mid_gather.finish_other(0)
    strips()

    dh_gather.across(2, 3)

    for part in parts:
        part.over()
    dh_gather.over(1)
    dh_gather.finish_column(1, 2, 3)
    for part in parts:
        part.finish_column()
        part.finish_other()
    kernel_grads(0, (0, 1, 2, 3), False, True)
    dh_gather.over(2)
    strips_sum()
    fin_gather.own_diagonal()
    fin_gather.own()
    dh_gather.finish_other(1, 2)
    kernel_grads(1, (0, 1, 2), False, False)
    dh_gather.over(3)
    dh_gather.finish_other(3)
    kernel_grads(1, (3,), True, False)
    fin_gather.across(wide=False)

    below = dh_all[pl.ds(pl.multiple_of(lower * n, n), n), :]
    below = jnp.where(me == peers - 1, jnp.zeros_like(below), below)
    even_top, odd_top = back_row(0, below)
    grad_fine[1, :, :chans] = (even_low + even_top).astype(jnp.bfloat16)
    grad_fine[1, :, chans:] = (odd_low + odd_top).astype(jnp.bfloat16)
    store(grad_fine, grad_fine_res)

    fin_gather.over()
    fin_gather.finish_column()
    fin_gather.finish_other()
    strips_end()
    for made in strip_copies:
        made.wait_send()
    halo.wait_send()
    for gather in (*parts, mid_gather, fin_gather, hid_gather, d_gather, dh_gather):
        gather.drain()
    for made in stat_copies:
        made.wait_send()
    for made in stores:
        made.wait()


def emit_kernel(
    block_in, taps_in, fine_in, strips_in, block_out, taps_out, fine_out, gathered, middle_taps, sem
):
    moves = [pltpu.make_async_copy(strips_in, gathered, sem.at[12])]
    for i in range(6):
        moves.append(pltpu.make_async_copy(taps_in.at[i], taps_out.at[i + i // 3 * 3], sem.at[i]))
    moves.append(pltpu.make_async_copy(block_in, block_out, sem.at[6]))
    for i in range(2):
        moves.append(pltpu.make_async_copy(fine_in.at[i], fine_out.at[i], sem.at[7 + i]))
    for move in moves:
        move.start()
    moves[0].wait()
    slim = gathered.shape[1] // 3
    for b in range(3):
        for i in range(4):
            for r in range(4):
                at = (4 * r + i) * slim
                piece = gathered[i * 4 + r, b * slim : (b + 1) * slim, :]
                middle_taps[b, at : at + slim, :] = piece.astype(jnp.float32)
        move = pltpu.make_async_copy(middle_taps.at[b], taps_out.at[3 + b], sem.at[9 + b])
        move.start()
        moves.append(move)
    for move in moves[1:]:
        move.wait()


def emit(block_out, taps, fine, strips):
    where = pl.BlockSpec(memory_space=pl.ANY)
    chans = taps.shape[1]
    return pl.pallas_call(
        emit_kernel,
        out_shape=(
            jax.ShapeDtypeStruct(block_out.shape, block_out.dtype),
            jax.ShapeDtypeStruct((9, chans, chans), taps.dtype),
            jax.ShapeDtypeStruct(fine.shape, fine.dtype),
        ),
        in_specs=[where] * 4,
        out_specs=(where,) * 3,
        scratch_shapes=[
            pltpu.VMEM(strips.shape, strips.dtype),
            pltpu.VMEM((3, chans, chans), taps.dtype),
            pltpu.SemaphoreType.DMA((16,)),
        ],
        compiler_params=pltpu.CompilerParams(vmem_limit_bytes=4 * 2**20),
    )(block_out, taps, fine, strips)


def fused_body(fine, conv_weight, qk_weight, v_weight, o_weight, upstream):
    peers = lax.axis_size("tile")
    n, chans = upstream.shape
    full = n * peers
    hbm = pl.BlockSpec(memory_space=pltpu.HBM)
    free = pl.BlockSpec(memory_space=pl.ANY)
    dma = pltpu.SemaphoreType.DMA
    low = jnp.bfloat16
    sources = (fine, conv_weight, qk_weight, v_weight, o_weight, upstream)
    block_out, taps, grad_fine, strips = pl.pallas_call(
        functools.partial(fused_kernel, peers),
        out_shape=(
            jax.ShapeDtypeStruct((n, chans), low),
            jax.ShapeDtypeStruct((6, chans, chans), jnp.float32),
            jax.ShapeDtypeStruct((2, n, 2 * chans), low),
            jax.ShapeDtypeStruct((peers, 3 * chans // 16, chans), low),
        ),
        in_specs=[hbm] * 6,
        out_specs=(free,) * 4,
        scratch_shapes=[
            pltpu.VMEM(fine.shape, low),
            pltpu.VMEM(conv_weight.shape, low),
            pltpu.VMEM(qk_weight.shape, low),
            pltpu.VMEM(v_weight.shape, low),
            pltpu.VMEM(o_weight.shape, low),
            pltpu.VMEM(upstream.shape, low),
            pltpu.VMEM((n, chans), low),
            pltpu.VMEM((6, chans, chans), jnp.float32),
            pltpu.VMEM((2, n, 2 * chans), low),
            dma((6,)),
            dma((11,)),
            pltpu.VMEM((2 * n, chans), low),
            pltpu.VMEM((full, chans), low),
            pltpu.VMEM((full, 2 * HD), low),
            pltpu.VMEM((full, HD), low),
            pltpu.VMEM((full, HD), low),
            pltpu.VMEM((full, chans), low),
            pltpu.VMEM((peers, 2 * chans, n), low),
            pltpu.VMEM((peers + 1, 2 * chans, n), low),
            pltpu.VMEM((peers, 2, 2 * n), jnp.float32),
            pltpu.VMEM((2 * n, full), jnp.float32),
            pltpu.VMEM((2 * n, full), jnp.float32),
            pltpu.VMEM((2 * n, full), jnp.float32),
            pltpu.VMEM((chans, 2 * HD), low),
            pltpu.VMEM((6, chans, chans), jnp.float32),
            dma((7, 16)),
            dma((7, 16)),
            dma((peers + 4,)),
            dma((peers + 4,)),
            dma,
            dma,
            pltpu.VMEM((4, 3 * chans // 16, chans), jnp.float32),
            pltpu.VMEM((4, 3 * chans // 16, chans), low),
            pltpu.VMEM((4, 3 * chans // 16, chans), low),
            pltpu.VMEM((peers, 3 * chans // 16, chans), low),
            pltpu.VMEM((2 * n, full // 2), jnp.float32),
            pltpu.VMEM((2 * n, full), jnp.float32),
        ],
        compiler_params=pltpu.CompilerParams(
            collective_id=0, has_side_effects=True, vmem_limit_bytes=36 * 2**20
        ),
    )(*[pltpu.with_memory_space_constraint(v, pltpu.HBM) for v in sources])
    results = emit(block_out, taps, grad_fine.reshape(fine.shape), strips)
    block_out, grad_conv, grad_fine = results
    return block_out, grad_conv.reshape(3, 3, chans, chans), grad_fine


def solution(mesh):
    def whole(fine, *rest):
        devices = mesh.shape["groups"] * mesh.shape["tile"]
        one_row = fine.shape[0] == 2 * devices and fine.shape[1] == 256 and fine.shape[2] == 256
        fits = mesh.shape["tile"] == 16
        return jax.shard_map(
            fused_body if one_row and fits else body,
            mesh=mesh,
            in_specs=(
                P(("groups", "tile"), None, None),
                P(),
                P(),
                P(),
                P(),
                P(("groups", "tile"), None),
            ),
            out_specs=(
                P(("groups", "tile"), None),
                P("groups", None, None, None),
                P(("groups", "tile"), None, None),
            ),
            check_vma=False,
        )(fine, *rest)

    return whole
```
